32 devices in a mesh: trainer: 16 (over z, x, core), store: 2 (over y).
Axes of the slice: x: 2, y: 2, z: 4, core: 2. Of those that a mesh axis runs over, the one named last changes fastest.
Arguments:
- memory: float32 [256, 512], P('store'), may hold values from -240 to 240
- event_feats: bfloat16 [25600, 128], P('store'), may hold values from -6 to 6
- batch_rows: int32 [16, 64], P('trainer', 'store'), may hold values from 0 to 127, as said below
- target_time: int32 [16, 64], P('trainer', 'store'), may hold values from 1024 to 2047
- neighbor_owner: int32 [16, 64, 100, 1], P('trainer', 'store'), may hold values from 0 to 1; in each aligned block of 3200 rows (0 to 3199, 3200 to 6399, ..., all dimensions but the last counted through in order) at most 3200 rows name the same one
- neighbor_event: int32 [16, 64, 100], P('trainer', 'store'), may hold values from 0 to 12799
- neighbor_time: int32 [16, 64, 100], P('trainer', 'store'), may hold values from 0 to 1023, as said below
- time_freq: float32 [128], replicated, may hold values from 0.001 to 1
- time_phase: float32 [128], replicated, may hold values from -3.140625 to 3.140625
- w_query: bfloat16 [512, 512], replicated, may hold values from -0.25 to 0.25
- w_key: bfloat16 [256, 512], replicated, may hold values from -0.375 to 0.375
- w_value: bfloat16 [256, 512], replicated, may hold values from -0.375 to 0.375
- ln_gain: float32 [512], replicated, may hold values from 0.5 to 1.5
- gru_input: bfloat16 [256, 1536], replicated, may hold values from -0.375 to 0.375
- gru_hidden: bfloat16 [512, 1536], replicated, may hold values from -0.25 to 0.25
- emb_cotangent: bfloat16 [16, 64, 512], P('trainer', 'store'), may hold values from -6 to 6
Outputs:
- embedding: bfloat16 [16, 64, 512], P('trainer', 'store')
- memory_next: float32 [16, 256, 512], P('trainer', 'store')
- key_value_grad: float32 [262144], P(('trainer', 'store'))
The draws below stay inside these ranges and needn't reach their ends.
Inputs may be any that keep to these rules, and one draw needn't show every extreme that they name: `batch_rows`: the 32 entries that one device holds are distinct. `neighbor_owner`: among the 3200 neighbor rows of one device, no owner is named by more than 3200 rows. `neighbor_time`: along the 100 neighbors of a target, times never rise.
All inputs are finite; a program needn't handle non-finite values.
Results may differ from the reference program's by a relative error of at most 0.003.
The reference program's roundings to bfloat16 on the way (of `mem_low` and `key_inputs`) count: a program that leaves them out, or rounds other values in their place, can miss the bound.
Values may be sent and summed in bfloat16 or wider, within the bound.
No kernel may reach another device: no remote copies, remote signals or barrier semaphores. Data moves between devices by JAX's collectives and lax.ppermute only.
A program may use at most 64 MiB of HBM per device.

```python
import math
import jax
import jax.numpy as jnp
import numpy as np
from jax import lax

MEM = 512
EF = 128
TE = 128
HEADS = 2
K = 100
B_DEV = 32
NODE_DEV = 128
TRAINERS = 16
STORES = 2
REPLICAS = 32
TGT = 64
NODES = 256
CAP = 3200
EV_DEV = 12800
EVENTS = 25600
KIN = 256


def draw_memory(key, part):
    normal_values = jnp.clip(jax.random.normal(key, (NODES, MEM), jnp.float32), -4.0, 4.0)
    return normal_values


def draw_batch_rows(key, part):
    devices = TRAINERS * (TGT // B_DEV)
    device_keys = jax.random.split(jax.random.fold_in(key, 11), devices)

    def first_rows(device_key):
        return jax.random.permutation(device_key, NODE_DEV)[:B_DEV]
    chosen = jax.vmap(first_rows)(device_keys)
    return chosen.reshape(TRAINERS, TGT).astype(jnp.int32)


def draw_neighbor_time(key, part):
    raw_times = jax.random.randint(jax.random.fold_in(key, 23), (TRAINERS, TGT, K), 0, 1024, jnp.int32)
    raw_times = raw_times.at[0, 0, 0].set(1023)
    raw_times = raw_times.at[TRAINERS - 1, TGT - 1, K - 1].set(0)
    ascending = jnp.sort(raw_times, axis=-1)
    return jnp.flip(ascending, axis=-1).astype(jnp.int32)


def touch_ends(drawn, key, least, top_value):
    longest = drawn.shape.index(max(drawn.shape))
    spots = []
    for shift in (0, 1):
        where = [jax.random.randint(jax.random.fold_in(key, axis), (), 0, length) for axis, length in enumerate(drawn.shape)]
        where[longest] = (where[longest] + shift) % drawn.shape[longest]
        spots.append(tuple(where))
    return drawn.at[spots[0]].set(least).at[spots[1]].set(top_value)


def level_of(stream_key, extent, cuts, least, high):
    factor_of, own = 1.0, jax.random.fold_in(stream_key, 6)
    for position, parts in cuts:
        heights = jnp.exp(jax.random.uniform(jax.random.fold_in(own, position), (parts,), jnp.float32, least / len(cuts), high / len(cuts)))
        factor_of = factor_of * jnp.repeat(heights, extent[position] // parts).reshape([-1 if axis == position else 1 for axis in range(len(extent))])
    return factor_of


def deal_out(key, own, number, rows, number_of, top, most, lean):
    sequence = jax.random.permutation(key, number_of)
    packed, usual = load_shares(number_of, rows * top, most, lean, True), load_shares(number_of, rows * top, most, lean, False)
    places = jnp.arange(number_of)

    def named(tallies, offset_by):
        used = int((tallies > 0).sum())
        fixed = max(1, used // 4)
        moved = fixed + (places - fixed + offset_by * (used - fixed)) % max(1, number_of - fixed)
        return jnp.zeros((number_of,), jnp.int32).at[sequence[jnp.where(places < fixed, places, moved)]].set(jnp.asarray(tallies, jnp.int32))

    tallies = jnp.where(number % 4 == 0, named(packed, number // 4), named(usual, number - number // 4 - 1))
    mixed = jax.random.permutation(jax.random.fold_in(own, 3), number_of)
    source_of, sink = mixed[0:number_of // 2 * 2:2], mixed[1:number_of // 2 * 2:2]
    room = jnp.minimum(tallies[source_of] - 1, most - tallies[sink]) // 2
    room = jnp.where((source_of == sequence[0]) | (sink == sequence[0]) | (tallies[sink] == 0), 0, jnp.maximum(room, 0))
    moved = jax.random.randint(jax.random.fold_in(own, 4), (number_of // 2,), 0, 1 << 20) % (room + 1)
    tallies = tallies.at[source_of].add(-moved).at[sink].add(moved)
    members = jnp.searchsorted(jnp.cumsum(tallies), jnp.arange(rows * top), side="right").astype(jnp.int32)
    grid = members.reshape(top, rows).T
    grid = grid[jax.random.permutation(jax.random.fold_in(own, 1), rows)]
    offset_by = jax.random.randint(jax.random.fold_in(own, 2), (rows, 1), 0, top)
    return jnp.take_along_axis(grid, (jnp.arange(top)[None, :] + offset_by) % top, axis=1)


def load_shares(amount, total, bound, skew, full):
    loads = [(1 << 20) // math.isqrt(rank ** skew) + 1 for rank in range(1, amount + 1)]
    largest = bound if full else min(bound, max(-(-total // amount), total * loads[0] // sum(loads)))
    least = 1 if total - largest >= amount - 1 else 0
    given, spare = [largest] + [least] * (amount - 1), total - largest - least * (amount - 1)
    while spare > 0:
        candidates = [i for i in range(1, amount) if given[i] < largest] or [i for i in range(1, amount) if given[i] < bound]
        mass, left = sum([loads[i] for i in candidates]), spare
        for i in candidates:
            more = min(bound - given[i], max(1, left * loads[i] // mass), spare)
            given[i] = given[i] + more
            spare = spare - more
    return np.array(given)


def gaussian(own_key, shape, width, reach, pieces=(), held_as=jnp.bfloat16):
    drawn = width * jax.random.normal(own_key, shape, jnp.float32)
    if pieces:
        drawn = drawn * level_of(own_key, shape, pieces, -0.22, 0.18)
    return jnp.clip(drawn, -reach, reach).astype(held_as)


def setup_inputs(seed: int = 0) -> dict:
    splits = jax.random.split(jax.random.key(seed), 17)
    memory = draw_memory(jax.random.fold_in(splits[16], 71), 0)
    event_feats = gaussian(splits[1], (EVENTS, EF), 1.0, 6.0, ((0, 2),))
    batch_rows = draw_batch_rows(jax.random.fold_in(splits[16], 71), 0)
    target_time = touch_ends(jax.random.randint(splits[3], (TRAINERS, TGT), 1024, 2048), jax.random.fold_in(splits[3], 1), 1024, 2047).astype(jnp.int32)
    neighbor_owner_keys = jax.random.split(jax.random.fold_in(splits[4], 1), TRAINERS * TGT * K // (B_DEV * K))
    neighbor_owner_turns = jax.random.permutation(jax.random.fold_in(splits[4], 3), TRAINERS * TGT * K // (B_DEV * K))
    neighbor_owner = jax.vmap(lambda own, number: deal_out(jax.random.fold_in(splits[4], 2), own, number, B_DEV * K, STORES, 1, CAP, 2))(neighbor_owner_keys, neighbor_owner_turns).reshape((TRAINERS, TGT, K, 1))
    neighbor_event = touch_ends(jax.random.randint(splits[5], (TRAINERS, TGT, K), 0, EV_DEV), jax.random.fold_in(splits[5], 1), 0, EV_DEV - 1).astype(jnp.int32)
    neighbor_time = draw_neighbor_time(jax.random.fold_in(splits[16], 71), 0)
    time_freq = jnp.clip(jnp.exp(jax.random.uniform(splits[7], (TE,), jnp.float32, math.log(0.001), math.log(1.0))), 0.001, 1.0)
    time_phase = jnp.clip(jax.random.uniform(splits[8], (TE,), jnp.float32, -3.140625, 3.140625), -3.140625, 3.140625)
    w_query = gaussian(splits[9], (MEM, MEM), MEM ** -0.5, 0.25)
    w_key = gaussian(splits[10], (KIN, MEM), KIN ** -0.5, 0.375)
    w_value = gaussian(splits[11], (KIN, MEM), KIN ** -0.5, 0.375)
    ln_gain = jnp.clip(1.0 + 0.1 * jax.random.normal(splits[12], (MEM,), jnp.float32), 0.5, 1.5)
    gru_input = gaussian(splits[13], (KIN, 3 * MEM), KIN ** -0.5, 0.375)
    gru_hidden = gaussian(splits[14], (MEM, 3 * MEM), MEM ** -0.5, 0.25)
    emb_cotangent = gaussian(splits[15], (TRAINERS, TGT, MEM), 1.0, 6.0, ((0, 16), (1, 2)))
    return {"memory": memory, "event_feats": event_feats, "batch_rows": batch_rows, "target_time": target_time, "neighbor_owner": neighbor_owner, "neighbor_event": neighbor_event, "neighbor_time": neighbor_time, "time_freq": time_freq, "time_phase": time_phase, "w_query": w_query, "w_key": w_key, "w_value": w_value, "ln_gain": ln_gain, "gru_input": gru_input, "gru_hidden": gru_hidden, "emb_cotangent": emb_cotangent}


highest = lax.Precision.HIGHEST

def key_inputs_of(feature_rows, target_times, neighbor_times, time_freq, time_phase):
    elapsed = (target_times[:, None] - neighbor_times).astype(jnp.float32)
    encoded = jnp.cos(elapsed[:, :, None] * time_freq + time_phase)
    return jnp.concatenate([feature_rows, encoded.astype(jnp.bfloat16)], axis=-1)

def memory_step(mem_rows, mem_low, latest_inputs, gru_input, gru_hidden):
    mem_width = mem_rows.shape[1]
    from_input = jnp.dot(latest_inputs, gru_input, preferred_element_type=jnp.float32)
    from_state = jnp.dot(mem_low, gru_hidden, preferred_element_type=jnp.float32)
    update_gate = jax.nn.sigmoid(from_input[:, :mem_width] + from_state[:, :mem_width])
    reset_gate = jax.nn.sigmoid(from_input[:, mem_width:2 * mem_width] + from_state[:, mem_width:2 * mem_width])
    candidate = jnp.tanh(from_input[:, 2 * mem_width:] + reset_gate * from_state[:, 2 * mem_width:])
    return (1.0 - update_gate) * candidate + update_gate * mem_rows

def attend_block(mem_rows, query, key_inputs, cotangent, w_key, w_value, ln_gain):
    block_size, neighbors, in_width = key_inputs.shape
    mem_width = w_key.shape[1]
    head_dim = mem_width // HEADS
    flat_inputs = key_inputs.reshape(block_size * neighbors, in_width)
    key_rows = jnp.dot(flat_inputs, w_key, preferred_element_type=jnp.float32).reshape(block_size, neighbors, HEADS, head_dim)
    value_rows = jnp.dot(flat_inputs, w_value, preferred_element_type=jnp.float32).reshape(block_size, neighbors, HEADS, head_dim)
    query_heads = query.reshape(block_size, HEADS, head_dim)
    score_scale = 1.0 / math.sqrt(head_dim)
    scores = jnp.einsum('bhd,bkhd->bhk', query_heads, key_rows, precision=highest) * score_scale
    row_max = lax.optimization_barrier(jnp.max(scores, axis=-1, keepdims=True))
    exponent = jnp.exp(scores - row_max)
    attention = exponent / lax.optimization_barrier(jnp.sum(exponent, axis=-1, keepdims=True))
    aggregate = jnp.einsum('bhk,bkhd->bhd', attention, value_rows, precision=highest).reshape(block_size, mem_width)
    summed = aggregate + mem_rows
    centered = summed - lax.optimization_barrier(jnp.mean(summed, axis=-1, keepdims=True))
    inv_std = lax.rsqrt(lax.optimization_barrier(jnp.mean(centered * centered, axis=-1, keepdims=True)) + 1e-05)
    normed = centered * inv_std
    embedded = normed * ln_gain
    grad_normed = cotangent * ln_gain
    grad_summed = (grad_normed - lax.optimization_barrier(jnp.mean(grad_normed, axis=-1, keepdims=True)) - normed * lax.optimization_barrier(jnp.mean(grad_normed * normed, axis=-1, keepdims=True))) * inv_std
    grad_heads = grad_summed.reshape(block_size, HEADS, head_dim)
    grad_values = jnp.einsum('bhk,bhd->bkhd', attention, grad_heads, precision=highest)
    grad_attention = jnp.einsum('bhd,bkhd->bhk', grad_heads, value_rows, precision=highest)
    grad_scores = attention * (grad_attention - lax.optimization_barrier(jnp.sum(attention * grad_attention, axis=-1, keepdims=True)))
    grad_keys = jnp.einsum('bhk,bhd->bkhd', grad_scores, query_heads, precision=highest) * score_scale
    contract = (((0,), (0,)), ((), ()))
    grad_key = lax.dot_general(flat_inputs, grad_keys.reshape(block_size * neighbors, mem_width).astype(jnp.bfloat16), contract, preferred_element_type=jnp.float32)
    grad_value = lax.dot_general(flat_inputs, grad_values.reshape(block_size * neighbors, mem_width).astype(jnp.bfloat16), contract, preferred_element_type=jnp.float32)
    return (embedded, jnp.stack([grad_key, grad_value]))

def reference(memory, event_feats, batch_rows, target_time, neighbor_owner, neighbor_event, neighbor_time, time_freq, time_phase, w_query, w_key, w_value, ln_gain, gru_input, gru_hidden, emb_cotangent):
    mem_width = memory.shape[1]
    owner_base = jnp.arange(TGT, dtype=jnp.int32) // B_DEV * NODE_DEV
    node_ids = (batch_rows + owner_base[None, :]).astype(jnp.int32)
    event_ids = (neighbor_owner[..., 0] * EV_DEV + neighbor_event).astype(jnp.int32)
    block_size = math.gcd(B_DEV, 8)
    blocks = TRAINERS * TGT // block_size
    grad_scale = 1.0 / math.sqrt(REPLICAS)

    def one_block(carried, inputs):
        nodes_here, events_here, target_here, times_here, cot_here = inputs
        mem_rows = memory[nodes_here]
        mem_low = mem_rows.astype(jnp.bfloat16)
        query = jnp.dot(mem_low, w_query, preferred_element_type=jnp.float32)
        key_inputs = key_inputs_of(event_feats[events_here], target_here, times_here, time_freq, time_phase)
        new_rows = memory_step(mem_rows, mem_low, key_inputs[:, 0, :], gru_input, gru_hidden)
        embedded, grads = attend_block(mem_rows, query, key_inputs, cot_here.astype(jnp.float32) * grad_scale, w_key, w_value, ln_gain)
        return (carried + grads, (embedded.astype(jnp.bfloat16), new_rows))
    scanned = (node_ids.reshape(blocks, block_size), event_ids.reshape(blocks, block_size, K), target_time.reshape(blocks, block_size), neighbor_time.reshape(blocks, block_size, K), emb_cotangent.reshape(blocks, block_size, mem_width))
    zero_grads = jnp.zeros((2, w_key.shape[0], mem_width), jnp.float32)
    grads, (embedded, new_rows) = lax.scan(one_block, zero_grads, scanned)
    embedding = embedded.reshape(TRAINERS, TGT, mem_width)
    new_rows = new_rows.reshape(TRAINERS, TGT, mem_width)

    def place_rows(node_list, row_values):
        return memory.at[node_list].set(row_values)
    memory_next = jax.vmap(place_rows)(jnp.roll(node_ids, 1, axis=0), jnp.roll(new_rows, 1, axis=0))
    return (embedding, memory_next, grads.reshape(-1))
```

```python
import functools
import math

import jax
import jax.numpy as jnp
from jax import lax
from jax.experimental import pallas as pl
from jax.experimental.pallas import tpu as pltpu
from jax.sharding import PartitionSpec as P

HEADS = 2
LANES = 128
AXES = ("trainer", "store")

f32 = jnp.float32
bf16 = jnp.bfloat16
NT = (((1,), (1,)), ((), ()))
NN = (((1,), (0,)), ((), ()))
TN = (((0,), (0,)), ((), ()))
VM = pl.BlockSpec(memory_space=pltpu.VMEM)
SM = pl.BlockSpec(memory_space=pltpu.SMEM)
ANY = pl.BlockSpec(memory_space=pl.ANY)
PARAMS = pltpu.CompilerParams(vmem_limit_bytes=56 * 1024 * 1024)


def dot(a, b, dims):
    return lax.dot_general(a, b, dims, preferred_element_type=f32)


def split(x, parts):
    terms = []
    for _ in range(parts):
        term = x.astype(bf16)
        terms.append(term)
        x = x - term.astype(f32)
    return terms


def cosine(x):
    turns = jnp.floor(x * (1.0 / math.pi) + 0.5)
    r = x - turns * 3.140625
    r = r - turns * 9.67502593994140625e-4
    r = r - turns * 1.50995788317e-7
    u = r * r
    c = f32(1.0 / 479001600.0)
    for k in (-1.0 / 3628800.0, 1.0 / 40320.0, -1.0 / 720.0, 1.0 / 24.0, -0.5, 1.0):
        c = c * u + f32(k)
    odd = (turns.astype(jnp.int32) & 1) == 1
    return jnp.where(odd, -c, c)


def pack_kernel(
    rows_ref, memory_ref, own_ref, event_ref, ntime_ref, ttime_ref, cot_ref, out_ref, *, held
):
    targets, neighbors = event_ref.shape
    width = memory_ref.shape[1]
    ids = own_ref[...] * held + event_ref[...]
    out_ref[:, width : width + 2 * LANES] = jnp.full((targets, 2 * LANES), -1.0, f32)
    out_ref[:, width : width + neighbors] = ids.astype(f32)
    elapsed = ttime_ref[...] - ntime_ref[...]
    out_ref[:, width + LANES : width + LANES + neighbors] = elapsed.astype(f32)
    out_ref[:, width + 2 * LANES :] = cot_ref[...].astype(f32)
    for b in range(targets):
        out_ref[pl.ds(b, 1), :width] = memory_ref[pl.ds(rows_ref[0, b], 1), :]


def attend_kernel(
    place_ref,
    pack_ref,
    table_ref,
    freq_ref,
    phase_ref,
    wq_ref,
    wk_ref,
    state_ref,
    p_ref,
    q_ref,
    x_ref,
    tbf_ref,
    tab_ref,
    ids_ref,
    sids_ref,
    rows_ref,
    qk_ref,
    s_ref,
    when_ref,
    latest_ref,
    tsem,
    isem,
    *,
    neighbors,
):
    targets = pack_ref.shape[0]
    held, feat = table_ref.shape
    width = wq_ref.shape[0]
    kin = wk_ref.shape[0]
    head = width // HEADS
    hb = HEADS * targets
    chunks = tsem.shape[0]
    step = held // chunks
    copies = [
        pltpu.make_async_copy(
            table_ref.at[pl.ds(c * step, step)], tbf_ref.at[pl.ds(c * step, step)], tsem.at[c]
        )
        for c in range(chunks)
    ]
    for copy in copies:
        copy.start()
    ids = pack_ref[:, width : width + LANES].astype(jnp.int32) - place_ref[0] * held
    valid = (ids >= 0) & (ids < held)
    lane = lax.broadcasted_iota(jnp.int32, ids.shape, 1)
    valid = valid & (lane < neighbors)
    ids_ref[...] = jnp.where(valid, ids, 0)
    id_copy = pltpu.make_async_copy(ids_ref, sids_ref, isem)
    id_copy.start()
    mem_low = pack_ref[:, :width].astype(bf16)
    query = dot(mem_low, wq_ref[...], NN)
    q_ref[...] = query
    scale = 1.0 / math.sqrt(head)
    for h in range(HEADS):
        cols = slice(h * head, (h + 1) * head)
        stacked = jnp.concatenate(split(query[:, cols], 3), axis=0)
        full = dot(stacked, wk_ref[:, cols], NT)
        qk = (full[:targets] + full[targets : 2 * targets] + full[2 * targets :]) * scale
        for i, term in enumerate(split(qk, 3)):
            qk_ref[i * hb + h * targets : i * hb + (h + 1) * targets, :] = term
    rows_ref[...] = jnp.zeros(rows_ref.shape, f32)
    when_ref[...] = pack_ref[:, width + LANES : width + 2 * LANES]
    id_copy.wait()
    block = math.gcd(step, 320)
    for c in range(chunks):
        copies[c].wait()

        def widen(i, _, c=c):
            at = pl.multiple_of(c * step + i * block, block)
            tab_ref[pl.ds(at, block), :] = tbf_ref[pl.ds(at, block), :].astype(f32)
            return 0

        lax.fori_loop(0, step // block, widen, 0)
    row_of = lax.broadcasted_iota(jnp.int32, (hb, LANES), 0) % targets

    def scores_of(pair):
        at = pl.multiple_of(jnp.maximum(pair, 0) * 2 * LANES, 2 * LANES)
        full = dot(qk_ref[...], x_ref[pl.ds(at, 2 * LANES), :], NT)
        return full[:hb] + full[hb : 2 * hb] + full[2 * hb :]

    def keep_scores(pair, part):
        old = s_ref[...]
        new = jnp.where(row_of == 2 * pair, part[:, :LANES], old)
        s_ref[...] = jnp.where(row_of == 2 * pair + 1, part[:, LANES:], new)

    def one_pair(pair, _):
        part = scores_of(pair - 1)
        for t in range(2):
            for n in range(neighbors):
                rows_ref[pl.ds(t * LANES + n, 1), :] = tab_ref[
                    pl.ds(sids_ref[2 * pair + t, n], 1), :
                ]
        for t in range(2):
            b = 2 * pair + t
            at = pl.multiple_of(b * LANES, LANES)
            elapsed = when_ref[pl.ds(b, 1), :]
            column = jnp.broadcast_to(elapsed, (LANES, LANES)).T
            encoded = cosine(column * freq_ref[...] + phase_ref[...])
            x_ref[pl.ds(at, LANES), feat:] = encoded.astype(bf16)
            x_ref[pl.ds(at, LANES), :feat] = rows_ref[t * LANES : (t + 1) * LANES, :].astype(bf16)
            latest_ref[pl.ds(b, 1), :] = rows_ref[t * LANES : t * LANES + 1, :]
        keep_scores(pair - 1, part)
        return 0

    pairs = targets // 2
    s_ref[...] = jnp.zeros(s_ref.shape, f32)
    lax.fori_loop(0, pairs, one_pair, 0)
    keep_scores(pairs - 1, scores_of(pairs - 1))
    valid2 = jnp.concatenate([valid] * HEADS, axis=0)
    s = s_ref[...]
    top = jnp.max(jnp.where(valid2, s, -1e30), axis=1, keepdims=True)
    p = jnp.where(valid2, jnp.exp(s - top), 0.0)
    p_ref[...] = p
    total = jnp.sum(p, axis=1, keepdims=True)
    acc = weighted(p, x_ref, row_of)
    state_ref[:hb, :] = acc
    lane = lax.broadcasted_iota(jnp.int32, (targets, LANES), 1)
    stat = total[targets:]
    for value, end in ((top[targets:], 96), (total[:targets], 64), (top[:targets], 32)):
        stat = jnp.where(lane < end, value, stat)
    state_ref[hb:, :LANES] = stat
    first = jnp.where(valid, 1.0, 0.0)[:, :1]
    state_ref[hb:, LANES:] = latest_ref[...] * first


def weighted(p, x_ref, row_of):
    hb = p.shape[0]
    targets = hb // HEADS
    terms = jnp.concatenate(split(p, 2), axis=0)
    rows = jnp.concatenate([row_of, row_of], axis=0)
    acc = jnp.zeros((2 * hb, x_ref.shape[1]), f32)
    zero = jnp.zeros_like(terms)
    for pair in range(targets // 2):
        left = jnp.where(rows == 2 * pair, terms, zero)
        right = jnp.where(rows == 2 * pair + 1, terms, zero)
        lhs = jnp.concatenate([left, right], axis=1)
        acc = acc + dot(lhs, x_ref[2 * pair * LANES : 2 * (pair + 1) * LANES, :], NN)
    return acc[:hb] + acc[hb:]


def grad_kernel(*refs, stores, targets, replicas, grid):
    at = 0

    def take(n):
        nonlocal at
        at += n
        return refs[at - n : at]

    (place_ref, gain_ref, wv_ref) = take(3)
    packs = take(stores)
    queries = take(stores)
    weights = take(stores)
    inputs = take(stores)
    states = [take(stores) for _ in range(stores)]
    emb_ref, keep_ref, send_ref = take(3)
    (grad_ref,) = take(1)
    his, los = grid
    width = gain_ref.shape[1]
    head = width // HEADS
    kin = wv_ref.shape[0]
    hb = HEADS * targets
    gain = gain_ref[...]
    row_of = lax.broadcasted_iota(jnp.int32, (hb, LANES), 0) % targets
    scale = 1.0 / math.sqrt(head)
    lefts = [[] for _ in range(HEADS)]
    rights = [[] for _ in range(HEADS)]

    def stats(state):
        tops = jnp.concatenate([state[hb:, 0:1], state[hb:, 64:65]], axis=0)
        totals = jnp.concatenate([state[hb:, 32:33], state[hb:, 96:97]], axis=0)
        return tops, totals

    def matmul3(a, b, dims):
        n = a.shape[0]
        full = dot(jnp.concatenate(split(a, 3), axis=0), b, dims)
        return full[:n] + full[n : 2 * n] + full[2 * n :]

    for d in range(stores):
        parts = [stats(state) for state in states[d]]
        top = functools.reduce(jnp.maximum, [m for m, _ in parts])
        fac = [jnp.exp(m - top) for m, _ in parts]
        total = sum(f * l for f, (_, l) in zip(fac, parts))
        inv = 1.0 / total
        attended = sum(f * state[:hb, :] for f, state in zip(fac, states[d])) * inv
        share = fac[0] * inv
        agg = jnp.concatenate(
            [
                matmul3(
                    attended[h * targets : (h + 1) * targets],
                    wv_ref[:, h * head : (h + 1) * head],
                    NN,
                )
                for h in range(HEADS)
            ],
            axis=1,
        )
        summed = agg + packs[d][:, :width]
        centered = summed - jnp.mean(summed, axis=1, keepdims=True)
        inv_std = lax.rsqrt(jnp.mean(centered * centered, axis=1, keepdims=True) + 1e-05)
        normed = centered * inv_std
        if d == 0:
            emb_ref[...] = (normed * gain).astype(bf16)
        cot = packs[d][:, width + 2 * LANES :] * (1.0 / math.sqrt(replicas))
        gn = cot * gain
        gsum = (
            gn
            - jnp.mean(gn, axis=1, keepdims=True)
            - normed * jnp.mean(gn * normed, axis=1, keepdims=True)
        ) * inv_std
        gv = jnp.concatenate(
            [
                matmul3(
                    gsum[:, h * head : (h + 1) * head], wv_ref[:, h * head : (h + 1) * head], NT
                )
                for h in range(HEADS)
            ],
            axis=0,
        )
        rowdot = jnp.sum(gv * attended, axis=1, keepdims=True)
        terms = jnp.concatenate(split(gv, 2), axis=0)
        ga = jnp.zeros((hb, LANES), f32)
        x_ref = inputs[d]
        for pair in range(targets // 2):
            full = dot(terms, x_ref[2 * pair * LANES : 2 * (pair + 1) * LANES, :], NT)
            full = full[:hb] + full[hb:]
            ga = jnp.where(row_of == 2 * pair, full[:, :LANES], ga)
            ga = jnp.where(row_of == 2 * pair + 1, full[:, LANES:], ga)
        gs = weights[d][...] * share * (ga - rowdot)
        ks = weighted(gs, x_ref, row_of) * scale
        for h in range(HEADS):
            k1, k2 = split(ks[h * targets : (h + 1) * targets], 2)
            q1, q2 = split(queries[d][:, h * head : (h + 1) * head], 2)
            lefts[h] += [k1, k1, k2]
            rights[h] += [q1, q2, q1]
            if d == 0:
                a1, a2 = split(attended[h * targets : (h + 1) * targets], 2)
                g1, g2 = split(gsum[:, h * head : (h + 1) * head], 2)
                grad_ref[kin:, h * head : (h + 1) * head] = dot(
                    jnp.concatenate([a1, a1, a2], axis=0),
                    jnp.concatenate([g1, g2, g1], axis=0),
                    TN,
                )
    for h in range(HEADS):
        grad_ref[:kin, h * head : (h + 1) * head] = dot(
            jnp.concatenate(lefts[h], axis=0), jnp.concatenate(rights[h], axis=0), TN
        )
    rows = 2 * kin // replicas
    hi, lo, core, store = (place_ref[i] for i in range(4))
    for lr in range(los):
        for sr in range(stores):
            for hr in range(his):
                to = ((lr * stores + sr) * his + hr) * rows
                base = ((hi ^ hr) * los + (lo ^ lr)) * 2
                for ref, c in ((keep_ref, core), (send_ref, 1 - core)):
                    src = ((base + c) * stores + (store ^ sr)) * rows
                    src = pl.multiple_of(src, rows)
                    ref[to : to + rows, :] = grad_ref[pl.ds(src, rows), :]


def gru_kernel(*refs, stores, targets):
    pack_ref, rows_ref, freq_ref, phase_ref, gi_ref, gh_ref = refs[:6]
    states, out_ref = refs[6 : 6 + stores], refs[6 + stores]
    width = gh_ref.shape[0]
    hb = HEADS * targets
    latest = sum(state[hb:, LANES:] for state in states)
    elapsed = pack_ref[:, width + LANES : width + LANES + 1]
    encoded = cosine(elapsed * freq_ref[...] + phase_ref[...])
    inputs = jnp.concatenate([latest.astype(bf16), encoded.astype(bf16)], axis=1)
    mem_rows = pack_ref[:, :width]
    gi = dot(inputs, gi_ref[...], NN)
    gh = dot(mem_rows.astype(bf16), gh_ref[...], NN)
    update = jax.nn.sigmoid(gi[:, :width] + gh[:, :width])
    reset = jax.nn.sigmoid(gi[:, width : 2 * width] + gh[:, width : 2 * width])
    candidate = jnp.tanh(gi[:, 2 * width :] + reset * gh[:, 2 * width :])
    out_ref[:targets, :] = (1.0 - update) * candidate + update * mem_rows
    out_ref[targets:, :] = jnp.zeros((8, width), f32)
    out_ref[targets : targets + 1, :targets] = rows_ref[...].astype(f32)


def place_kernel(memory_ref, new_ref, out_ref, ids_ref, sids_ref, sem):
    targets = new_ref.shape[0] - 8
    ids_ref[...] = new_ref[targets:, :LANES].astype(jnp.int32)
    copy = pltpu.make_async_copy(ids_ref, sids_ref, sem)
    copy.start()
    out_ref[...] = memory_ref[...]
    copy.wait()
    for b in range(targets):
        out_ref[pl.ds(sids_ref[0, b], 1), :] = new_ref[b : b + 1, :]


def sum_split_kernel(*refs, count, outs):
    total = refs[0][...]
    for ref in refs[1:count]:
        total = total + ref[...].astype(f32)
    size = total.shape[0] // outs
    for i, ref in enumerate(refs[count:]):
        ref[...] = total[i * size : (i + 1) * size].astype(ref.dtype)


def last_sum_kernel(*refs):
    total = refs[0][...]
    for ref in refs[1:-1]:
        total = total + ref[...].astype(f32)
    out_ref = refs[-1]
    rows, width = total.shape
    per = width // LANES
    for j in range(per):
        out_ref[pl.ds(j, rows, stride=per), :] = total[:, j * LANES : (j + 1) * LANES]


def call(kernel, ins, outs, scratch=(), specs=None, name=None):
    return pl.pallas_call(
        kernel,
        in_specs=specs or [VM] * len(ins),
        out_specs=[VM] * len(outs),
        out_shape=outs,
        scratch_shapes=list(scratch),
        compiler_params=PARAMS,
        name=name,
    )(*ins)


def shape(*dims, dtype=f32):
    return jax.ShapeDtypeStruct(dims, dtype)


def on_device(
    memory,
    event_feats,
    batch_rows,
    target_time,
    neighbor_owner,
    neighbor_event,
    neighbor_time,
    time_freq,
    time_phase,
    w_query,
    w_key,
    w_value,
    ln_gain,
    gru_input,
    gru_hidden,
    emb_cotangent,
):
    trainers, stores = lax.axis_size("trainer"), lax.axis_size("store")
    replicas = trainers * stores
    targets, neighbors = neighbor_event.shape[1:]
    held, feat = event_feats.shape
    width = memory.shape[1]
    kin = w_key.shape[0]
    hb = HEADS * targets
    trainer, store = lax.axis_index("trainer"), lax.axis_index("store")
    los = 2
    his = trainers // (2 * los)
    place = jnp.stack([trainer // (2 * los), (trainer // 2) % los, trainer % 2, store])
    place = place.astype(jnp.int32)
    freq, phase = time_freq[None], time_phase[None]

    (pack,) = call(
        functools.partial(pack_kernel, held=held),
        [
            batch_rows,
            memory,
            neighbor_owner[0, :, :, 0],
            neighbor_event[0],
            neighbor_time[0],
            target_time.reshape(targets, 1),
            emb_cotangent[0],
        ],
        [shape(targets, 2 * width + 2 * LANES)],
        specs=[SM] + [VM] * 6,
        name="pack",
    )

    def from_store(value, d):
        return lax.ppermute(value, "store", [((i + d) % stores, i) for i in range(stores)])

    packs = [pack] + [from_store(pack, d) for d in range(1, stores)]
    chunks = 4
    local, weights, queries, inputs = [], [], [], []
    for d in range(stores):
        state, p, q, x = call(
            functools.partial(attend_kernel, neighbors=neighbors),
            [store[None].astype(jnp.int32), packs[d], event_feats, freq, phase, w_query, w_key],
            [
                shape(hb + targets, kin),
                shape(hb, LANES),
                shape(targets, width),
                shape(targets * LANES, kin, dtype=bf16),
            ],
            scratch=[
                pltpu.VMEM((held, feat), bf16),
                pltpu.VMEM((held, feat), f32),
                pltpu.VMEM((targets, LANES), jnp.int32),
                pltpu.SMEM((targets, LANES), jnp.int32),
                pltpu.VMEM((2 * LANES, feat), f32),
                pltpu.VMEM((3 * hb, kin), bf16),
                pltpu.VMEM((hb, LANES), f32),
                pltpu.VMEM((targets, LANES), f32),
                pltpu.VMEM((targets, LANES), f32),
                pltpu.SemaphoreType.DMA((chunks,)),
                pltpu.SemaphoreType.DMA,
            ],
            specs=[SM, VM, ANY] + [VM] * 4,
            name="attend",
        )
        local.append(state)
        weights.append(p)
        queries.append(q)
        inputs.append(x)
    gathered = [local] + [[from_store(state, e) for state in local] for e in range(1, stores)]
    states = [[gathered[e][(d - e) % stores] for e in range(stores)] for d in range(stores)]

    flat_states = [state for group in states for state in group]
    ins = [place, ln_gain[None], w_value, *packs, *queries, *weights, *inputs, *flat_states]
    emb, keep, send = call(
        functools.partial(
            grad_kernel, stores=stores, targets=targets, replicas=replicas, grid=(his, los)
        ),
        ins,
        [shape(targets, width, dtype=bf16), shape(kin, width), shape(kin, width)],
        scratch=[pltpu.VMEM((2 * kin, width), f32)],
        specs=[SM] + [VM] * (len(ins) - 1),
        name="grads",
    )

    (news,) = call(
        functools.partial(gru_kernel, stores=stores, targets=targets),
        [pack, batch_rows, freq, phase, gru_input, gru_hidden, *states[0]],
        [shape(targets + 8, width)],
        name="gru",
    )

    def exchange(value, hr, lr, cr, sr):
        def other(i):
            t, s = i // stores, i % stores
            t = ((t // (2 * los)) ^ hr) * 2 * los + (((t // 2) % los) ^ lr) * 2 + ((t % 2) ^ cr)
            return t * stores + (s ^ sr)

        return lax.ppermute(value, AXES, [(i, other(i)) for i in range(replicas)])

    swapped = exchange(send, 0, 0, 1, 0)
    members = los * stores
    out = call(
        functools.partial(sum_split_kernel, count=2, outs=members),
        [keep, swapped],
        [shape(kin // members, width)] * members,
        name="core_sum",
    )
    got = [exchange(out[j], 0, j // stores, 0, j % stores) for j in range(1, members)]
    out = call(
        functools.partial(sum_split_kernel, count=members, outs=his),
        [out[0], *got],
        [shape(kin // members // his, width)] * his,
        name="plane_sum",
    )
    got = [exchange(out[j], j, 0, 0, 0) for j in range(1, his)]
    (share,) = call(
        last_sum_kernel,
        [out[0], *got],
        [shape(2 * kin * width // replicas // LANES, LANES)],
        name="last_sum",
    )
    moved = lax.ppermute(news, "trainer", [(i, (i + 1) % trainers) for i in range(trainers)])
    (memory_next,) = call(
        place_kernel,
        [memory, moved],
        [shape(*memory.shape)],
        scratch=[
            pltpu.VMEM((8, LANES), jnp.int32),
            pltpu.SMEM((8, LANES), jnp.int32),
            pltpu.SemaphoreType.DMA,
        ],
        name="place",
    )
    return (emb[None], memory_next[None], share.reshape(-1))


def solution(mesh):
    placed = (
        P("store", None),
        P("store", None),
        P("trainer", "store"),
        P("trainer", "store"),
        P("trainer", "store", None, None),
        P("trainer", "store", None),
        P("trainer", "store", None),
        P(),
        P(),
        P(),
        P(),
        P(),
        P(),
        P(),
        P(),
        P("trainer", "store", None),
    )
    return jax.shard_map(
        on_device,
        mesh=mesh,
        in_specs=placed,
        out_specs=(
            P("trainer", "store", None),
            P("trainer", "store", None),
            P(("trainer", "store")),
        ),
        check_vma=False,
    )
```

```python
import functools
import math

import jax
import jax.numpy as jnp
from jax import lax
from jax.experimental import pallas as pl
from jax.experimental.pallas import tpu as pltpu
from jax.sharding import PartitionSpec as P

HEADS = 2
LANES = 128
TURN = 0.5 / math.pi
AXES = ("trainer", "store")

f32 = jnp.float32
bf16 = jnp.bfloat16
NT = (((1,), (1,)), ((), ()))
NN = (((1,), (0,)), ((), ()))
TN = (((0,), (0,)), ((), ()))
VM = pl.BlockSpec(memory_space=pltpu.VMEM)
SM = pl.BlockSpec(memory_space=pltpu.SMEM)
FAR = pl.BlockSpec(memory_space=pltpu.HBM)
PARAMS = pltpu.CompilerParams(vmem_limit_bytes=20 * 1024 * 1024)


def dot(a, b, dims):
    return lax.dot_general(a, b, dims, preferred_element_type=f32)


def split(x, parts):
    terms = []
    for _ in range(parts):
        term = x.astype(bf16)
        terms.append(term)
        x = x - term.astype(f32)
    return terms


def cosine(turns):
    part = turns - jnp.floor(turns)
    g = 0.25 - jnp.abs(part - 0.5)
    u = g * g
    c = f32(-((2 * math.pi) ** 11) / math.factorial(11))
    for k in (9, 7, 5, 3, 1):
        c = c * u + f32((1 if k % 4 == 1 else -1) * (2 * math.pi) ** k / math.factorial(k))
    return -(c * g)


def pack_kernel(
    rows_ref, memory_ref, own_ref, event_ref, ntime_ref, ttime_ref, cot_ref, out_ref, *, held
):
    targets, neighbors = event_ref.shape
    width = memory_ref.shape[1]
    ids = own_ref[...] * held + event_ref[...]
    out_ref[:, width : width + 2 * LANES] = jnp.full((targets, 2 * LANES), -1.0, f32)
    out_ref[:, width : width + neighbors] = ids.astype(f32)
    row = lax.broadcasted_iota(jnp.int32, (targets, targets), 0)
    lane = lax.broadcasted_iota(jnp.int32, (targets, targets), 1)
    times = jnp.sum(jnp.where(row == lane, ttime_ref[...].astype(f32), 0.0), axis=1, keepdims=True)
    elapsed = times - ntime_ref[...].astype(f32)
    out_ref[:, width + LANES : width + LANES + neighbors] = elapsed.astype(f32)
    out_ref[:, width + 2 * LANES :] = cot_ref[...].astype(f32)
    for b in range(targets):
        out_ref[pl.ds(b, 1), :width] = memory_ref[pl.ds(rows_ref[0, b], 1), :]


def attend_kernel(*refs, neighbors):
    place_ref, pack_ref, table_ref, freq_ref, phase_ref, wq_ref, wk_ref = refs[:7]
    state_ref, p_ref, q_ref, x_ref = refs[7:11]
    tbf_ref, tab_ref, ids_ref, sids_ref, rows_ref, qk_ref, s_ref, when_ref, latest_ref = refs[11:20]
    tsem, isem = refs[20:]
    targets = pack_ref.shape[0]
    width = wq_ref.shape[0]
    kin = wk_ref.shape[0]
    feat = tab_ref.shape[1]
    head = width // HEADS
    hb = HEADS * targets
    held = tab_ref.shape[0]
    chunks = tsem.shape[0]
    step = held // chunks
    copies = [
        pltpu.make_async_copy(
            table_ref.at[pl.ds(c * step, step)], tbf_ref.at[pl.ds(c * step, step)], tsem.at[c]
        )
        for c in range(chunks)
    ]
    for copy in copies:
        copy.start()
    ids = pack_ref[:, width : width + LANES].astype(jnp.int32) - place_ref[0] * held
    valid = (ids >= 0) & (ids < held)
    lane = lax.broadcasted_iota(jnp.int32, ids.shape, 1)
    valid = valid & (lane < neighbors)
    ids_ref[...] = jnp.where(valid, ids, 0)
    id_copy = pltpu.make_async_copy(ids_ref, sids_ref, isem)
    id_copy.start()
    mem_low = pack_ref[:, :width].astype(bf16)
    query = dot(mem_low, wq_ref[...], NN)
    q_ref[...] = query
    scale = 1.0 / math.sqrt(head)
    for h in range(HEADS):
        cols = slice(h * head, (h + 1) * head)
        stacked = jnp.concatenate(split(query[:, cols], 3), axis=0)
        full = dot(stacked, wk_ref[:, cols], NT)
        qk = (full[:targets] + full[targets : 2 * targets] + full[2 * targets :]) * scale
        for i, term in enumerate(split(qk, 3)):
            qk_ref[i * hb + h * targets : i * hb + (h + 1) * targets, :] = term
    when_ref[...] = pack_ref[:, width + LANES : width + 2 * LANES]
    id_copy.wait()
    block = math.gcd(step, 320)
    for c in range(chunks):
        copies[c].wait()

        def widen(i, _, c=c):
            at = pl.multiple_of(c * step + i * block, block)
            tab_ref[pl.ds(at, block), :] = tbf_ref[pl.ds(at, block), :].astype(f32)
            return 0

        lax.fori_loop(0, step // block, widen, 0)
    row_of = lax.broadcasted_iota(jnp.int32, (hb, LANES), 0) % targets

    freq, phase = freq_ref[...] * TURN, phase_ref[...] * TURN
    pairs = targets // 2
    both = 2 * LANES

    def start_of(pair):
        return pl.multiple_of(pair * both, both)

    def scores_of(pair):
        full = dot(qk_ref[...], x_ref[pl.ds(start_of(pair), both), :], NT)
        return full[:hb] + full[hb : 2 * hb] + full[2 * hb :]

    def keep_scores(pair, part):
        new = jnp.where(row_of == 2 * pair, part[:, :LANES], s_ref[...])
        s_ref[...] = jnp.where(row_of == 2 * pair + 1, part[:, LANES:], new)

    def one_pair(pair, _):
        part = scores_of(jnp.maximum(pair - 1, 0))
        at = start_of(pair)
        for t in range(2):
            elapsed = when_ref[pl.ds(2 * pair + t, 1), :]
            column = jnp.broadcast_to(elapsed, (LANES, LANES)).T
            encoded = cosine(column * freq + phase)
            x_ref[pl.ds(at + t * LANES, LANES), feat:] = encoded.astype(bf16)
        for t in range(2):
            row_ids = sids_ref.at[2 * pair + t]
            for n in range(neighbors):
                rows_ref[t * LANES + n : t * LANES + n + 1, :] = tab_ref[pl.ds(row_ids[n], 1), :]
        x_ref[pl.ds(at, both), :feat] = rows_ref[...].astype(bf16)
        for t in range(2):
            latest_ref[pl.ds(2 * pair + t, 1), :] = rows_ref[t * LANES : t * LANES + 1, :]
        keep_scores(pair - 1, part)
        return 0

    s_ref[...] = jnp.zeros(s_ref.shape, f32)
    rows_ref[...] = jnp.zeros(rows_ref.shape, f32)
    lax.fori_loop(0, pairs, one_pair, 0)
    keep_scores(pairs - 1, scores_of(pairs - 1))
    valid2 = jnp.concatenate([valid] * HEADS, axis=0)
    s = s_ref[...]
    top = jnp.max(jnp.where(valid2, s, -1e30), axis=1, keepdims=True)
    p = jnp.where(valid2, jnp.exp(s - top), 0.0)
    p_ref[...] = p
    total = jnp.sum(p, axis=1, keepdims=True)
    acc = weighted(p, x_ref, row_of)
    state_ref[:hb, :] = acc
    lane = lax.broadcasted_iota(jnp.int32, (targets, LANES), 1)
    stat = total[targets:]
    for value, end in ((top[targets:], 96), (total[:targets], 64), (top[:targets], 32)):
        stat = jnp.where(lane < end, value, stat)
    state_ref[hb:, :LANES] = stat
    first = jnp.where(valid, 1.0, 0.0)[:, :1]
    state_ref[hb:, LANES:] = latest_ref[...] * first


def weighted(p, x_ref, row_of):
    hb = p.shape[0]
    targets = hb // HEADS
    terms = jnp.concatenate(split(p, 2), axis=0)
    rows = jnp.concatenate([row_of, row_of], axis=0)
    acc = jnp.zeros((2 * hb, x_ref.shape[1]), f32)
    zero = jnp.zeros_like(terms)
    for pair in range(targets // 2):
        left = jnp.where(rows == 2 * pair, terms, zero)
        right = jnp.where(rows == 2 * pair + 1, terms, zero)
        lhs = jnp.concatenate([left, right], axis=1)
        acc = acc + dot(lhs, x_ref[2 * pair * LANES : 2 * (pair + 1) * LANES, :], NN)
    return acc[:hb] + acc[hb:]


def grad_kernel(*refs, stores, targets, replicas, grid):
    at = 0

    def take(n):
        nonlocal at
        at += n
        return refs[at - n : at]

    (place_ref, gain_ref, wv_ref) = take(3)
    packs = take(stores)
    queries = take(stores)
    weights = take(stores)
    inputs = take(stores)
    states = [take(stores) for _ in range(stores)]
    emb_ref, keep_ref, send_ref = take(3)
    (grad_ref,) = take(1)
    his, los = grid
    width = gain_ref.shape[1]
    head = width // HEADS
    kin = wv_ref.shape[0]
    hb = HEADS * targets
    gain = gain_ref[...]
    row_of = lax.broadcasted_iota(jnp.int32, (hb, LANES), 0) % targets
    scale = 1.0 / math.sqrt(head)
    lefts = [[] for _ in range(HEADS)]
    rights = [[] for _ in range(HEADS)]

    def stats(state):
        tops = jnp.concatenate([state[hb:, 0:1], state[hb:, 64:65]], axis=0)
        totals = jnp.concatenate([state[hb:, 32:33], state[hb:, 96:97]], axis=0)
        return tops, totals

    def matmul3(a, b, dims):
        n = a.shape[0]
        full = dot(jnp.concatenate(split(a, 3), axis=0), b, dims)
        return full[:n] + full[n : 2 * n] + full[2 * n :]

    for d in range(stores):
        parts = [stats(state) for state in states[d]]
        top = functools.reduce(jnp.maximum, [m for m, _ in parts])
        fac = [jnp.exp(m - top) for m, _ in parts]
        total = sum(f * l for f, (_, l) in zip(fac, parts))
        inv = 1.0 / total
        attended = sum(f * state[:hb, :] for f, state in zip(fac, states[d])) * inv
        share = fac[0] * inv
        agg = jnp.concatenate(
            [
                matmul3(
                    attended[h * targets : (h + 1) * targets],
                    wv_ref[:, h * head : (h + 1) * head],
                    NN,
                )
                for h in range(HEADS)
            ],
            axis=1,
        )
        summed = agg + packs[d][:, :width]
        centered = summed - jnp.mean(summed, axis=1, keepdims=True)
        inv_std = lax.rsqrt(jnp.mean(centered * centered, axis=1, keepdims=True) + 1e-05)
        normed = centered * inv_std
        if d == 0:
            emb_ref[...] = (normed * gain).astype(bf16)
        cot = packs[d][:, width + 2 * LANES :] * (1.0 / math.sqrt(replicas))
        gn = cot * gain
        gsum = (
            gn
            - jnp.mean(gn, axis=1, keepdims=True)
            - normed * jnp.mean(gn * normed, axis=1, keepdims=True)
        ) * inv_std
        gv = jnp.concatenate(
            [
                matmul3(
                    gsum[:, h * head : (h + 1) * head], wv_ref[:, h * head : (h + 1) * head], NT
                )
                for h in range(HEADS)
            ],
            axis=0,
        )
        rowdot = jnp.sum(gv * attended, axis=1, keepdims=True)
        terms = jnp.concatenate(split(gv, 2), axis=0)
        ga = jnp.zeros((hb, LANES), f32)
        x_ref = inputs[d]
        for pair in range(targets // 2):
            full = dot(terms, x_ref[2 * pair * LANES : 2 * (pair + 1) * LANES, :], NT)
            full = full[:hb] + full[hb:]
            ga = jnp.where(row_of == 2 * pair, full[:, :LANES], ga)
            ga = jnp.where(row_of == 2 * pair + 1, full[:, LANES:], ga)
        gs = weights[d][...] * share * (ga - rowdot)
        ks = weighted(gs, x_ref, row_of) * scale
        for h in range(HEADS):
            k1, k2 = split(ks[h * targets : (h + 1) * targets], 2)
            q1, q2 = split(queries[d][:, h * head : (h + 1) * head], 2)
            lefts[h] += [k1, k1, k2]
            rights[h] += [q1, q2, q1]
            if d == 0:
                a1, a2 = split(attended[h * targets : (h + 1) * targets], 2)
                g1, g2 = split(gsum[:, h * head : (h + 1) * head], 2)
                grad_ref[kin:, h * head : (h + 1) * head] = dot(
                    jnp.concatenate([a1, a1, a2], axis=0),
                    jnp.concatenate([g1, g2, g1], axis=0),
                    TN,
                )
    for h in range(HEADS):
        grad_ref[:kin, h * head : (h + 1) * head] = dot(
            jnp.concatenate(lefts[h], axis=0), jnp.concatenate(rights[h], axis=0), TN
        )
    rows = 2 * kin // replicas
    hi, lo, core, store = (place_ref[i] for i in range(4))
    for lr in range(los):
        for sr in range(stores):
            for hr in range(his):
                to = ((lr * stores + sr) * his + hr) * rows
                base = ((hi ^ hr) * los + (lo ^ lr)) * 2
                for ref, c in ((keep_ref, core), (send_ref, 1 - core)):
                    src = ((base + c) * stores + (store ^ sr)) * rows
                    src = pl.multiple_of(src, rows)
                    ref[to : to + rows, :] = grad_ref[pl.ds(src, rows), :]


def gru_kernel(*refs, stores, targets):
    pack_ref, rows_ref, freq_ref, phase_ref, gi_ref, gh_ref = refs[:6]
    states, out_ref = refs[6 : 6 + stores], refs[6 + stores]
    width = gh_ref.shape[0]
    hb = HEADS * targets
    latest = sum(state[hb:, LANES:] for state in states)
    elapsed = pack_ref[:, width + LANES : width + LANES + 1]
    encoded = cosine(elapsed * (freq_ref[...] * TURN) + phase_ref[...] * TURN)
    inputs = jnp.concatenate([latest.astype(bf16), encoded.astype(bf16)], axis=1)
    mem_rows = pack_ref[:, :width]
    gi = dot(inputs, gi_ref[...], NN)
    gh = dot(mem_rows.astype(bf16), gh_ref[...], NN)
    update = jax.nn.sigmoid(gi[:, :width] + gh[:, :width])
    reset = jax.nn.sigmoid(gi[:, width : 2 * width] + gh[:, width : 2 * width])
    candidate = jnp.tanh(gi[:, 2 * width :] + reset * gh[:, 2 * width :])
    out_ref[:targets, :] = (1.0 - update) * candidate + update * mem_rows
    out_ref[targets:, :] = jnp.zeros((8, width), f32)
    out_ref[targets : targets + 1, :targets] = rows_ref[...].astype(f32)


def place_kernel(memory_ref, new_ref, out_ref, ids_ref, sids_ref, sem):
    targets = new_ref.shape[0] - 8
    ids_ref[...] = new_ref[targets:, :LANES].astype(jnp.int32)
    copy = pltpu.make_async_copy(ids_ref, sids_ref, sem)
    copy.start()
    out_ref[...] = memory_ref[...]
    copy.wait()
    for b in range(targets):
        out_ref[pl.ds(sids_ref[0, b], 1), :] = new_ref[b : b + 1, :]


def sum_split_kernel(*refs, count, outs):
    total = refs[0][...]
    for ref in refs[1:count]:
        total = total + ref[...].astype(f32)
    size = total.shape[0] // outs
    for i, ref in enumerate(refs[count:]):
        ref[...] = total[i * size : (i + 1) * size].astype(ref.dtype)


def last_sum_kernel(*refs):
    total = refs[0][...]
    for ref in refs[1:-1]:
        total = total + ref[...].astype(f32)
    out_ref = refs[-1]
    rows, width = total.shape
    per = width // LANES
    for j in range(per):
        out_ref[pl.ds(j, rows, stride=per), :] = total[:, j * LANES : (j + 1) * LANES]


def call(kernel, ins, outs, scratch=(), specs=None, name=None):
    return pl.pallas_call(
        kernel,
        in_specs=specs or [VM] * len(ins),
        out_specs=[VM] * len(outs),
        out_shape=outs,
        scratch_shapes=list(scratch),
        compiler_params=PARAMS,
        name=name,
    )(*ins)


def near(x):
    return pltpu.with_memory_space_constraint(x, pltpu.VMEM)


def shape(*dims, dtype=f32):
    return pltpu.VMEM(dims, dtype)


def far(*dims, dtype=f32):
    return jax.ShapeDtypeStruct(dims, dtype)


def on_device(
    memory,
    event_feats,
    batch_rows,
    target_time,
    neighbor_owner,
    neighbor_event,
    neighbor_time,
    time_freq,
    time_phase,
    w_query,
    w_key,
    w_value,
    ln_gain,
    gru_input,
    gru_hidden,
    emb_cotangent,
):
    trainers, stores = lax.axis_size("trainer"), lax.axis_size("store")
    replicas = trainers * stores
    targets, neighbors = neighbor_event.shape[1:]
    held, feat = event_feats.shape
    width = memory.shape[1]
    kin = w_key.shape[0]
    hb = HEADS * targets
    trainer, store = lax.axis_index("trainer"), lax.axis_index("store")
    los = 2
    his = trainers // (2 * los)
    place = jnp.stack([trainer // (2 * los), (trainer // 2) % los, trainer % 2, store])
    place = place.astype(jnp.int32)
    freq, phase = time_freq[None], time_phase[None]

    (pack,) = call(
        functools.partial(pack_kernel, held=held),
        [
            batch_rows,
            memory,
            neighbor_owner[0, :, :, 0],
            neighbor_event[0],
            neighbor_time[0],
            target_time,
            emb_cotangent[0],
        ],
        [shape(targets, 2 * width + 2 * LANES)],
        specs=[SM] + [VM] * 6,
        name="pack",
    )

    def from_store(value, d):
        return lax.ppermute(value, "store", [((i + d) % stores, i) for i in range(stores)])

    packs = [pack] + [from_store(pack, d) for d in range(1, stores)]
    table = pltpu.with_memory_space_constraint(event_feats, pltpu.HBM)
    chunks = 4
    local, weights, queries, inputs = [], [], [], []
    for d in range(stores):
        state, p, q, x = call(
            functools.partial(attend_kernel, neighbors=neighbors),
            [
                store[None].astype(jnp.int32),
                near(packs[d]),
                table,
                freq,
                phase,
                w_query,
                w_key,
            ],
            [
                shape(hb + targets, kin),
                shape(hb, LANES),
                shape(targets, width),
                shape(targets * LANES, kin, dtype=bf16),
            ],
            scratch=[
                pltpu.VMEM((held, feat), bf16),
                pltpu.VMEM((held, feat), f32),
                pltpu.VMEM((targets, LANES), jnp.int32),
                pltpu.SMEM((targets, LANES), jnp.int32),
                pltpu.VMEM((2 * LANES, feat), f32),
                pltpu.VMEM((3 * hb, kin), bf16),
                pltpu.VMEM((hb, LANES), f32),
                pltpu.VMEM((targets, LANES), f32),
                pltpu.VMEM((targets, LANES), f32),
                pltpu.SemaphoreType.DMA((chunks,)),
                pltpu.SemaphoreType.DMA,
            ],
            specs=[SM, VM, FAR] + [VM] * 4,
            name="attend",
        )
        local.append(state)
        weights.append(p)
        queries.append(q)
        inputs.append(x)
    gathered = [local] + [[from_store(state, e) for state in local] for e in range(1, stores)]
    states = [[gathered[e][(d - e) % stores] for e in range(stores)] for d in range(stores)]

    flat_states = [state for group in states for state in group]
    near_ins = [near(x) for x in (*packs, *queries, *weights, *inputs, *flat_states)]
    ins = [place, ln_gain[None], w_value, *near_ins]
    emb, keep, send = call(
        functools.partial(
            grad_kernel, stores=stores, targets=targets, replicas=replicas, grid=(his, los)
        ),
        ins,
        [far(targets, width, dtype=bf16), shape(kin, width), shape(kin, width)],
        scratch=[pltpu.VMEM((2 * kin, width), f32)],
        specs=[SM] + [VM] * (len(ins) - 1),
        name="grads",
    )

    (news,) = call(
        functools.partial(gru_kernel, stores=stores, targets=targets),
        [near(pack), batch_rows, freq, phase, gru_input, gru_hidden, *map(near, states[0])],
        [shape(targets + 8, width)],
        name="gru",
    )

    def exchange(value, hr, lr, cr, sr):
        def other(i):
            t, s = i // stores, i % stores
            t = ((t // (2 * los)) ^ hr) * 2 * los + (((t // 2) % los) ^ lr) * 2 + ((t % 2) ^ cr)
            return t * stores + (s ^ sr)

        return lax.ppermute(value, AXES, [(i, other(i)) for i in range(replicas)])

    swapped = exchange(send, 0, 0, 1, 0)
    members = los * stores
    out = call(
        functools.partial(sum_split_kernel, count=2, outs=members),
        [near(keep), near(swapped)],
        [shape(kin // members, width)] * members,
        name="core_sum",
    )
    got = [exchange(out[j], 0, j // stores, 0, j % stores) for j in range(1, members)]
    out = call(
        functools.partial(sum_split_kernel, count=members, outs=his),
        [*map(near, [out[0], *got])],
        [shape(kin // members // his, width)] * his,
        name="plane_sum",
    )
    got = [exchange(out[j], j, 0, 0, 0) for j in range(1, his)]
    (share,) = call(
        last_sum_kernel,
        [*map(near, [out[0], *got])],
        [far(2 * kin * width // replicas // LANES, LANES)],
        name="last_sum",
    )
    moved = lax.ppermute(news, "trainer", [(i, (i + 1) % trainers) for i in range(trainers)])
    (memory_next,) = call(
        place_kernel,
        [memory, near(moved)],
        [far(*memory.shape)],
        scratch=[
            pltpu.VMEM((8, LANES), jnp.int32),
            pltpu.SMEM((8, LANES), jnp.int32),
            pltpu.SemaphoreType.DMA,
        ],
        name="place",
    )
    return (emb[None], memory_next[None], share.reshape(-1))


def solution(mesh):
    placed = (
        P("store", None),
        P("store", None),
        P("trainer", "store"),
        P("trainer", "store"),
        P("trainer", "store", None, None),
        P("trainer", "store", None),
        P("trainer", "store", None),
        P(),
        P(),
        P(),
        P(),
        P(),
        P(),
        P(),
        P(),
        P("trainer", "store", None),
    )
    return jax.shard_map(
        on_device,
        mesh=mesh,
        in_specs=placed,
        out_specs=(
            P("trainer", "store", None),
            P("trainer", "store", None),
            P(("trainer", "store")),
        ),
        check_vma=False,
    )
```

```python
import functools
import math

import jax
import jax.numpy as jnp
from jax import lax
from jax.experimental import pallas as pl
from jax.experimental.pallas import tpu as pltpu
from jax.sharding import PartitionSpec as P

HEADS = 2
LANES = 128
TURN = 0.5 / math.pi
AXES = ("trainer", "store")

f32 = jnp.float32
bf16 = jnp.bfloat16
NT = (((1,), (1,)), ((), ()))
NN = (((1,), (0,)), ((), ()))
TN = (((0,), (0,)), ((), ()))
VM = pl.BlockSpec(memory_space=pltpu.VMEM)
SM = pl.BlockSpec(memory_space=pltpu.SMEM)
FAR = pl.BlockSpec(memory_space=pltpu.HBM)
PARAMS = pltpu.CompilerParams(vmem_limit_bytes=20 * 1024 * 1024)


def dot(a, b, dims):
    return lax.dot_general(a, b, dims, preferred_element_type=f32)


def split(x, parts):
    terms = []
    for _ in range(parts):
        term = x.astype(bf16)
        terms.append(term)
        x = x - term.astype(f32)
    return terms


SERIES = (-39.53670604797494, 76.5497822911237, -81.60100407314816, 41.341655031414376, -6.283185160089465)


def cosine(turns):
    part = turns - jnp.floor(turns)
    g = 0.25 - jnp.abs(part - 0.5)
    u = g * g
    c = f32(SERIES[0])
    for k in SERIES[1:]:
        c = c * u + f32(k)
    return c * g


def pack_kernel(*refs, held):
    sources, rest = refs[:11], refs[11:]
    out_ref, turns_ref, wq_out, wk_out = rest[:4]
    kept, sems = rest[4:13], rest[13]
    rows_ref, memory_ref, own_ref, event_ref, ntime_ref, ttime_ref, cot_ref, freq_ref, phase_ref = kept
    copies = [
        pltpu.make_async_copy(src, dst, sems.at[i])
        for i, (src, dst) in enumerate(zip(sources, (*kept, wq_out, wk_out)))
    ]
    for copy in copies:
        copy.start()
    for copy in copies[:-2]:
        copy.wait()
    turns_ref[0:1, :] = freq_ref[...] * TURN
    turns_ref[1:2, :] = phase_ref[...] * TURN
    turns_ref[2:, :] = jnp.zeros((turns_ref.shape[0] - 2, LANES), f32)
    targets, neighbors = event_ref.shape
    width = memory_ref.shape[1]
    ids = own_ref[...] * held + event_ref[...]
    out_ref[:, width : width + 2 * LANES] = jnp.full((targets, 2 * LANES), -1.0, f32)
    out_ref[:, width : width + neighbors] = ids.astype(f32)
    row = lax.broadcasted_iota(jnp.int32, (targets, targets), 0)
    lane = lax.broadcasted_iota(jnp.int32, (targets, targets), 1)
    times = jnp.sum(jnp.where(row == lane, ttime_ref[...].astype(f32), 0.0), axis=1, keepdims=True)
    elapsed = times - ntime_ref[...].astype(f32)
    out_ref[:, width + LANES : width + LANES + neighbors] = elapsed.astype(f32)
    out_ref[:, width + 2 * LANES :] = cot_ref[...].astype(f32)
    for b in range(targets):
        out_ref[pl.ds(b, 1), :width] = memory_ref[pl.ds(rows_ref[0, b], 1), :]
    for copy in copies[-2:]:
        copy.wait()


def attend_kernel(*refs, neighbors):
    place_ref, pack_ref, table_ref, turns_ref, wq_ref, wk_ref = refs[:6]
    state_ref, p_ref, q_ref, x_ref = refs[6:10]
    tbf_ref, tab_ref, ids_ref, sids_ref, rows_ref, qk_ref, s_ref, when_ref, latest_ref = refs[10:19]
    tsem, isem = refs[19:]
    targets = pack_ref.shape[0]
    width = wq_ref.shape[0]
    kin = wk_ref.shape[0]
    feat = tab_ref.shape[1]
    head = width // HEADS
    hb = HEADS * targets
    held = tab_ref.shape[0]
    chunks = tsem.shape[0]
    step = held // chunks
    copies = [
        pltpu.make_async_copy(
            table_ref.at[pl.ds(c * step, step)], tbf_ref.at[pl.ds(c * step, step)], tsem.at[c]
        )
        for c in range(chunks)
    ]
    for copy in copies:
        copy.start()
    ids = pack_ref[:, width : width + LANES].astype(jnp.int32) - place_ref[0] * held
    valid = (ids >= 0) & (ids < held)
    lane = lax.broadcasted_iota(jnp.int32, ids.shape, 1)
    valid = valid & (lane < neighbors)
    ids_ref[...] = jnp.where(valid, ids, 0)
    id_copy = pltpu.make_async_copy(ids_ref, sids_ref, isem)
    id_copy.start()
    mem_low = pack_ref[:, :width].astype(bf16)
    query = dot(mem_low, wq_ref[...], NN)
    q_ref[...] = query
    scale = 1.0 / math.sqrt(head)
    for h in range(HEADS):
        cols = slice(h * head, (h + 1) * head)
        stacked = jnp.concatenate(split(query[:, cols], 3), axis=0)
        full = dot(stacked, wk_ref[:, cols], NT)
        qk = (full[:targets] + full[targets : 2 * targets] + full[2 * targets :]) * scale
        for i, term in enumerate(split(qk, 3)):
            qk_ref[i * hb + h * targets : i * hb + (h + 1) * targets, :] = term
    when_ref[...] = pack_ref[:, width + LANES : width + 2 * LANES]
    id_copy.wait()
    block = math.gcd(step, 320)
    for c in range(chunks):
        copies[c].wait()

        def widen(i, _, c=c):
            at = pl.multiple_of(c * step + i * block, block)
            tab_ref[pl.ds(at, block), :] = tbf_ref[pl.ds(at, block), :].astype(f32)
            return 0

        lax.fori_loop(0, step // block, widen, 0)
    row_of = lax.broadcasted_iota(jnp.int32, (hb, LANES), 0) % targets

    freq, phase = turns_ref[0:1, :], turns_ref[1:2, :]
    pairs = targets // 2
    both = 2 * LANES

    def start_of(pair):
        return pl.multiple_of(pair * both, both)

    def scores_of(pair):
        full = dot(qk_ref[...], x_ref[pl.ds(start_of(pair), both), :], NT)
        return full[:hb] + full[hb : 2 * hb] + full[2 * hb :]

    def keep_scores(pair, part):
        new = jnp.where(row_of == 2 * pair, part[:, :LANES], s_ref[...])
        s_ref[...] = jnp.where(row_of == 2 * pair + 1, part[:, LANES:], new)

    def one_pair(pair, _):
        part = scores_of(jnp.maximum(pair - 1, 0))
        at = start_of(pair)
        for t in range(2):
            elapsed = when_ref[pl.ds(2 * pair + t, 1), :]
            column = jnp.broadcast_to(elapsed, (LANES, LANES)).T
            encoded = cosine(column * freq + phase)
            x_ref[pl.ds(at + t * LANES, LANES), feat:] = encoded.astype(bf16)
        row_ids = [sids_ref.at[2 * pair + t] for t in range(2)]
        for n in range(neighbors):
            for t in range(2):
                rows_ref[t * LANES + n : t * LANES + n + 1, :] = tab_ref[pl.ds(row_ids[t][n], 1), :]
        x_ref[pl.ds(at, both), :feat] = rows_ref[...].astype(bf16)
        for t in range(2):
            latest_ref[pl.ds(2 * pair + t, 1), :] = rows_ref[t * LANES : t * LANES + 1, :]
        keep_scores(pair - 1, part)
        return 0

    s_ref[...] = jnp.zeros(s_ref.shape, f32)
    rows_ref[...] = jnp.zeros(rows_ref.shape, f32)
    lax.fori_loop(0, pairs, one_pair, 0)
    keep_scores(pairs - 1, scores_of(pairs - 1))
    valid2 = jnp.concatenate([valid] * HEADS, axis=0)
    s = s_ref[...]
    top = jnp.max(jnp.where(valid2, s, -1e30), axis=1, keepdims=True)
    p = jnp.where(valid2, jnp.exp(s - top), 0.0)
    p_ref[...] = p
    total = jnp.sum(p, axis=1, keepdims=True)
    acc = weighted(p, x_ref, row_of)
    state_ref[:hb, :] = acc
    lane = lax.broadcasted_iota(jnp.int32, (targets, LANES), 1)
    stat = total[targets:]
    for value, end in ((top[targets:], 96), (total[:targets], 64), (top[:targets], 32)):
        stat = jnp.where(lane < end, value, stat)
    state_ref[hb:, :LANES] = stat
    first = jnp.where(valid, 1.0, 0.0)[:, :1]
    state_ref[hb:, LANES:] = latest_ref[...] * first


def weighted(p, x_ref, row_of):
    hb = p.shape[0]
    targets = hb // HEADS
    terms = jnp.concatenate(split(p, 2), axis=0)
    rows = jnp.concatenate([row_of, row_of], axis=0)
    acc = jnp.zeros((2 * hb, x_ref.shape[1]), f32)
    zero = jnp.zeros_like(terms)
    for pair in range(targets // 2):
        left = jnp.where(rows == 2 * pair, terms, zero)
        right = jnp.where(rows == 2 * pair + 1, terms, zero)
        lhs = jnp.concatenate([left, right], axis=1)
        acc = acc + dot(lhs, x_ref[2 * pair * LANES : 2 * (pair + 1) * LANES, :], NN)
    return acc[:hb] + acc[hb:]


def grad_kernel(*refs, stores, targets, replicas, grid):
    at = 0

    def take(n):
        nonlocal at
        at += n
        return refs[at - n : at]

    (place_ref, gain_ref, wv_ref) = take(3)
    packs = take(stores)
    queries = take(stores)
    weights = take(stores)
    inputs = take(stores)
    states = [take(stores) for _ in range(stores)]
    emb_ref, keep_ref, send_ref = take(3)
    (grad_ref,) = take(1)
    his, los = grid
    width = gain_ref.shape[1]
    head = width // HEADS
    kin = wv_ref.shape[0]
    hb = HEADS * targets
    gain = gain_ref[...]
    row_of = lax.broadcasted_iota(jnp.int32, (hb, LANES), 0) % targets
    scale = 1.0 / math.sqrt(head)
    lefts = [[] for _ in range(HEADS)]
    rights = [[] for _ in range(HEADS)]

    def stats(state):
        tops = jnp.concatenate([state[hb:, 0:1], state[hb:, 64:65]], axis=0)
        totals = jnp.concatenate([state[hb:, 32:33], state[hb:, 96:97]], axis=0)
        return tops, totals

    def matmul3(a, b, dims):
        n = a.shape[0]
        full = dot(jnp.concatenate(split(a, 3), axis=0), b, dims)
        return full[:n] + full[n : 2 * n] + full[2 * n :]

    for d in range(stores):
        parts = [stats(state) for state in states[d]]
        top = functools.reduce(jnp.maximum, [m for m, _ in parts])
        fac = [jnp.exp(m - top) for m, _ in parts]
        total = sum(f * l for f, (_, l) in zip(fac, parts))
        inv = 1.0 / total
        attended = sum(f * state[:hb, :] for f, state in zip(fac, states[d])) * inv
        share = fac[0] * inv
        agg = jnp.concatenate(
            [
                matmul3(
                    attended[h * targets : (h + 1) * targets],
                    wv_ref[:, h * head : (h + 1) * head],
                    NN,
                )
                for h in range(HEADS)
            ],
            axis=1,
        )
        summed = agg + packs[d][:, :width]
        centered = summed - jnp.mean(summed, axis=1, keepdims=True)
        inv_std = lax.rsqrt(jnp.mean(centered * centered, axis=1, keepdims=True) + 1e-05)
        normed = centered * inv_std
        if d == 0:
            emb_ref[...] = (normed * gain).astype(bf16)
        cot = packs[d][:, width + 2 * LANES :] * (1.0 / math.sqrt(replicas))
        gn = cot * gain
        gsum = (
            gn
            - jnp.mean(gn, axis=1, keepdims=True)
            - normed * jnp.mean(gn * normed, axis=1, keepdims=True)
        ) * inv_std
        gv = jnp.concatenate(
            [
                matmul3(
                    gsum[:, h * head : (h + 1) * head], wv_ref[:, h * head : (h + 1) * head], NT
                )
                for h in range(HEADS)
            ],
            axis=0,
        )
        rowdot = jnp.sum(gv * attended, axis=1, keepdims=True)
        terms = jnp.concatenate(split(gv, 2), axis=0)
        ga = jnp.zeros((hb, LANES), f32)
        x_ref = inputs[d]
        for pair in range(targets // 2):
            full = dot(terms, x_ref[2 * pair * LANES : 2 * (pair + 1) * LANES, :], NT)
            full = full[:hb] + full[hb:]
            ga = jnp.where(row_of == 2 * pair, full[:, :LANES], ga)
            ga = jnp.where(row_of == 2 * pair + 1, full[:, LANES:], ga)
        gs = weights[d][...] * share * (ga - rowdot)
        ks = weighted(gs, x_ref, row_of) * scale
        for h in range(HEADS):
            k1, k2 = split(ks[h * targets : (h + 1) * targets], 2)
            q1, q2 = split(queries[d][:, h * head : (h + 1) * head], 2)
            lefts[h] += [k1, k1, k2]
            rights[h] += [q1, q2, q1]
            if d == 0:
                a1, a2 = split(attended[h * targets : (h + 1) * targets], 2)
                g1, g2 = split(gsum[:, h * head : (h + 1) * head], 2)
                grad_ref[kin:, h * head : (h + 1) * head] = dot(
                    jnp.concatenate([a1, a1, a2], axis=0),
                    jnp.concatenate([g1, g2, g1], axis=0),
                    TN,
                )
    for h in range(HEADS):
        grad_ref[:kin, h * head : (h + 1) * head] = dot(
            jnp.concatenate(lefts[h], axis=0), jnp.concatenate(rights[h], axis=0), TN
        )
    rows = 2 * kin // replicas
    hi, lo, core, store = (place_ref[i] for i in range(4))
    for lr in range(los):
        for sr in range(stores):
            for hr in range(his):
                to = ((lr * stores + sr) * his + hr) * rows
                base = ((hi ^ hr) * los + (lo ^ lr)) * 2
                for ref, c in ((keep_ref, core), (send_ref, 1 - core)):
                    src = ((base + c) * stores + (store ^ sr)) * rows
                    src = pl.multiple_of(src, rows)
                    ref[to : to + rows, :] = grad_ref[pl.ds(src, rows), :]


def gru_kernel(*refs, stores, targets):
    pack_ref, rows_ref, turns_ref, gi_ref, gh_ref = refs[:5]
    states, out_ref = refs[5 : 5 + stores], refs[5 + stores]
    width = gh_ref.shape[0]
    hb = HEADS * targets
    latest = sum(state[hb:, LANES:] for state in states)
    elapsed = pack_ref[:, width + LANES : width + LANES + 1]
    encoded = cosine(elapsed * turns_ref[0:1, :] + turns_ref[1:2, :])
    inputs = jnp.concatenate([latest.astype(bf16), encoded.astype(bf16)], axis=1)
    mem_rows = pack_ref[:, :width]
    gi = dot(inputs, gi_ref[...], NN)
    gh = dot(mem_rows.astype(bf16), gh_ref[...], NN)
    update = jax.nn.sigmoid(gi[:, :width] + gh[:, :width])
    reset = jax.nn.sigmoid(gi[:, width : 2 * width] + gh[:, width : 2 * width])
    candidate = jnp.tanh(gi[:, 2 * width :] + reset * gh[:, 2 * width :])
    out_ref[:targets, :] = (1.0 - update) * candidate + update * mem_rows
    out_ref[targets:, :] = jnp.zeros((8, width), f32)
    out_ref[targets : targets + 1, :targets] = rows_ref[...].astype(f32)


def place_kernel(memory_ref, new_ref, out_ref, ids_ref, sids_ref, sem):
    targets = new_ref.shape[0] - 8
    ids_ref[...] = new_ref[targets:, :LANES].astype(jnp.int32)
    copy = pltpu.make_async_copy(ids_ref, sids_ref, sem)
    copy.start()
    out_ref[...] = memory_ref[...]
    copy.wait()
    for b in range(targets):
        out_ref[pl.ds(sids_ref[0, b], 1), :] = new_ref[b : b + 1, :]


def sum_split_kernel(*refs, count, outs):
    total = refs[0][...]
    for ref in refs[1:count]:
        total = total + ref[...].astype(f32)
    size = total.shape[0] // outs
    for i, ref in enumerate(refs[count:]):
        ref[...] = total[i * size : (i + 1) * size].astype(ref.dtype)


def last_sum_kernel(*refs):
    total = refs[0][...]
    for ref in refs[1:-1]:
        total = total + ref[...].astype(f32)
    out_ref = refs[-1]
    rows, width = total.shape
    per = width // LANES
    for j in range(per):
        out_ref[pl.ds(j, rows, stride=per), :] = total[:, j * LANES : (j + 1) * LANES]


def call(kernel, ins, outs, scratch=(), specs=None, name=None):
    return pl.pallas_call(
        kernel,
        in_specs=specs or [VM] * len(ins),
        out_specs=[VM] * len(outs),
        out_shape=outs,
        scratch_shapes=list(scratch),
        compiler_params=PARAMS,
        name=name,
    )(*ins)


def near(x):
    return pltpu.with_memory_space_constraint(x, pltpu.VMEM)


def far(x):
    return pltpu.with_memory_space_constraint(x, pltpu.HBM)


def shape(*dims, dtype=f32):
    return pltpu.VMEM(dims, dtype)


def out_shape(*dims, dtype=f32):
    return jax.ShapeDtypeStruct(dims, dtype)


def on_device(
    memory,
    event_feats,
    batch_rows,
    target_time,
    neighbor_owner,
    neighbor_event,
    neighbor_time,
    time_freq,
    time_phase,
    w_query,
    w_key,
    w_value,
    ln_gain,
    gru_input,
    gru_hidden,
    emb_cotangent,
):
    trainers, stores = lax.axis_size("trainer"), lax.axis_size("store")
    replicas = trainers * stores
    targets, neighbors = neighbor_event.shape[1:]
    held, feat = event_feats.shape
    width = memory.shape[1]
    kin = w_key.shape[0]
    hb = HEADS * targets
    trainer, store = lax.axis_index("trainer"), lax.axis_index("store")
    los = 2
    his = trainers // (2 * los)
    place = jnp.stack([trainer // (2 * los), (trainer // 2) % los, trainer % 2, store])
    place = place.astype(jnp.int32)

    sources = [
        batch_rows,
        memory,
        neighbor_owner[0, :, :, 0],
        neighbor_event[0],
        neighbor_time[0],
        target_time,
        emb_cotangent[0],
        time_freq[None],
        time_phase[None],
        w_query,
        w_key,
    ]
    pack, turns, wq_near, wk_near = call(
        functools.partial(pack_kernel, held=held),
        [far(x) for x in sources],
        [
            shape(targets, 2 * width + 2 * LANES),
            shape(8, LANES),
            shape(*w_query.shape, dtype=bf16),
            shape(*w_key.shape, dtype=bf16),
        ],
        scratch=[pltpu.SMEM(batch_rows.shape, jnp.int32)]
        + [pltpu.VMEM(x.shape, x.dtype) for x in sources[1:9]]
        + [pltpu.SemaphoreType.DMA((len(sources),))],
        specs=[FAR] * len(sources),
        name="pack",
    )

    def from_store(value, d):
        return lax.ppermute(value, "store", [((i + d) % stores, i) for i in range(stores)])

    packs = [pack] + [from_store(pack, d) for d in range(1, stores)]
    table = far(event_feats)
    chunks = 4
    local, weights, queries, inputs = [], [], [], []
    for d in range(stores):
        state, p, q, x = call(
            functools.partial(attend_kernel, neighbors=neighbors),
            [
                store[None].astype(jnp.int32),
                near(packs[d]),
                table,
                near(turns),
                near(wq_near),
                near(wk_near),
            ],
            [
                shape(hb + targets, kin),
                shape(hb, LANES),
                shape(targets, width),
                shape(targets * LANES, kin, dtype=bf16),
            ],
            scratch=[
                pltpu.VMEM((held, feat), bf16),
                pltpu.VMEM((held, feat), f32),
                pltpu.VMEM((targets, LANES), jnp.int32),
                pltpu.SMEM((targets, LANES), jnp.int32),
                pltpu.VMEM((2 * LANES, feat), f32),
                pltpu.VMEM((3 * hb, kin), bf16),
                pltpu.VMEM((hb, LANES), f32),
                pltpu.VMEM((targets, LANES), f32),
                pltpu.VMEM((targets, LANES), f32),
                pltpu.SemaphoreType.DMA((chunks,)),
                pltpu.SemaphoreType.DMA,
            ],
            specs=[SM, VM, FAR] + [VM] * 3,
            name="attend",
        )
        local.append(state)
        weights.append(p)
        queries.append(q)
        inputs.append(x)
    gathered = [local] + [[from_store(state, e) for state in local] for e in range(1, stores)]
    states = [[gathered[e][(d - e) % stores] for e in range(stores)] for d in range(stores)]

    flat_states = [state for group in states for state in group]
    near_ins = [near(x) for x in (*packs, *queries, *weights, *inputs, *flat_states)]
    ins = [place, ln_gain[None], w_value, *near_ins]
    emb, keep, send = call(
        functools.partial(
            grad_kernel, stores=stores, targets=targets, replicas=replicas, grid=(his, los)
        ),
        ins,
        [out_shape(targets, width, dtype=bf16), shape(kin, width), shape(kin, width)],
        scratch=[pltpu.VMEM((2 * kin, width), f32)],
        specs=[SM] + [VM] * (len(ins) - 1),
        name="grads",
    )

    (news,) = call(
        functools.partial(gru_kernel, stores=stores, targets=targets),
        [near(pack), batch_rows, near(turns), gru_input, gru_hidden, *map(near, states[0])],
        [shape(targets + 8, width)],
        name="gru",
    )

    def exchange(value, hr, lr, cr, sr):
        def other(i):
            t, s = i // stores, i % stores
            t = ((t // (2 * los)) ^ hr) * 2 * los + (((t // 2) % los) ^ lr) * 2 + ((t % 2) ^ cr)
            return t * stores + (s ^ sr)

        return lax.ppermute(value, AXES, [(i, other(i)) for i in range(replicas)])

    swapped = exchange(send, 0, 0, 1, 0)
    members = los * stores
    out = call(
        functools.partial(sum_split_kernel, count=2, outs=members),
        [near(keep), near(swapped)],
        [shape(kin // members, width)] * members,
        name="core_sum",
    )
    got = [exchange(out[j], 0, j // stores, 0, j % stores) for j in range(1, members)]
    out = call(
        functools.partial(sum_split_kernel, count=members, outs=his),
        [*map(near, [out[0], *got])],
        [shape(kin // members // his, width)] * his,
        name="plane_sum",
    )
    got = [exchange(out[j], j, 0, 0, 0) for j in range(1, his)]
    (share,) = call(
        last_sum_kernel,
        [*map(near, [out[0], *got])],
        [out_shape(2 * kin * width // replicas // LANES, LANES)],
        name="last_sum",
    )
    moved = lax.ppermute(news, "trainer", [(i, (i + 1) % trainers) for i in range(trainers)])
    (memory_next,) = call(
        place_kernel,
        [memory, near(moved)],
        [out_shape(*memory.shape)],
        scratch=[
            pltpu.VMEM((8, LANES), jnp.int32),
            pltpu.SMEM((8, LANES), jnp.int32),
            pltpu.SemaphoreType.DMA,
        ],
        name="place",
    )
    return (emb[None], memory_next[None], share.reshape(-1))


def solution(mesh):
    placed = (
        P("store", None),
        P("store", None),
        P("trainer", "store"),
        P("trainer", "store"),
        P("trainer", "store", None, None),
        P("trainer", "store", None),
        P("trainer", "store", None),
        P(),
        P(),
        P(),
        P(),
        P(),
        P(),
        P(),
        P(),
        P("trainer", "store", None),
    )
    return jax.shard_map(
        on_device,
        mesh=mesh,
        in_specs=placed,
        out_specs=(
            P("trainer", "store", None),
            P("trainer", "store", None),
            P(("trainer", "store")),
        ),
        check_vma=False,
    )
```

```python
import functools
import math

import jax
import jax.numpy as jnp
from jax import lax
from jax.experimental import pallas as pl
from jax.experimental.pallas import tpu as pltpu
from jax.sharding import PartitionSpec as P

HEADS = 2
LANES = 128
TURN = 0.5 / math.pi
AXES = ("trainer", "store")

f32 = jnp.float32
bf16 = jnp.bfloat16
NT = (((1,), (1,)), ((), ()))
NN = (((1,), (0,)), ((), ()))
TN = (((0,), (0,)), ((), ()))
VM = pl.BlockSpec(memory_space=pltpu.VMEM)
SM = pl.BlockSpec(memory_space=pltpu.SMEM)
FAR = pl.BlockSpec(memory_space=pltpu.HBM)
PARAMS = pltpu.CompilerParams(vmem_limit_bytes=20 * 1024 * 1024)


def dot(a, b, dims):
    return lax.dot_general(a, b, dims, preferred_element_type=f32)


def split(x, parts):
    terms = []
    for _ in range(parts):
        term = x.astype(bf16)
        terms.append(term)
        x = x - term.astype(f32)
    return terms


SERIES = (-39.53670604797494, 76.5497822911237, -81.60100407314816, 41.341655031414376, -6.283185160089465)


def cosine(turns):
    part = turns - jnp.floor(turns)
    g = 0.25 - jnp.abs(part - 0.5)
    u = g * g
    c = f32(SERIES[0])
    for k in SERIES[1:]:
        c = c * u + f32(k)
    return c * g


def pack_kernel(*refs, held):
    sources, rest = refs[:11], refs[11:]
    out_ref, turns_ref, wq_out, wk_out = rest[:4]
    kept, sems = rest[4:13], rest[13]
    rows_ref, memory_ref, own_ref, event_ref, ntime_ref, ttime_ref, cot_ref, freq_ref, phase_ref = kept
    copies = [
        pltpu.make_async_copy(src, dst, sems.at[i])
        for i, (src, dst) in enumerate(zip(sources, (*kept, wq_out, wk_out)))
    ]
    for copy in copies:
        copy.start()
    for copy in copies[:-2]:
        copy.wait()
    turns_ref[0:1, :] = freq_ref[...] * TURN
    turns_ref[1:2, :] = phase_ref[...] * TURN
    turns_ref[2:, :] = jnp.zeros((turns_ref.shape[0] - 2, LANES), f32)
    targets, neighbors = event_ref.shape
    width = memory_ref.shape[1]
    ids = own_ref[...] * held + event_ref[...]
    out_ref[:, width : width + 2 * LANES] = jnp.full((targets, 2 * LANES), -1.0, f32)
    out_ref[:, width : width + neighbors] = ids.astype(f32)
    row = lax.broadcasted_iota(jnp.int32, (targets, targets), 0)
    lane = lax.broadcasted_iota(jnp.int32, (targets, targets), 1)
    times = jnp.sum(jnp.where(row == lane, ttime_ref[...].astype(f32), 0.0), axis=1, keepdims=True)
    elapsed = times - ntime_ref[...].astype(f32)
    out_ref[:, width + LANES : width + LANES + neighbors] = elapsed.astype(f32)
    out_ref[:, width + 2 * LANES :] = cot_ref[...].astype(f32)
    for b in range(targets):
        out_ref[pl.ds(b, 1), :width] = memory_ref[pl.ds(rows_ref[0, b], 1), :]
    for copy in copies[-2:]:
        copy.wait()


def attend_kernel(*refs, neighbors):
    place_ref, pack_ref, table_ref, turns_ref, wq_ref, wk_ref = refs[:6]
    state_ref, p_ref, q_ref, x_ref = refs[6:10]
    tbf_ref, tab_ref, ids_ref, sids_ref, rows_ref, qk_ref, s_ref, when_ref, latest_ref = refs[10:19]
    tsem, isem = refs[19:]
    targets = pack_ref.shape[0]
    width = wq_ref.shape[0]
    kin = wk_ref.shape[0]
    feat = tab_ref.shape[1]
    head = width // HEADS
    hb = HEADS * targets
    held = tab_ref.shape[0]
    chunks = tsem.shape[0]
    step = held // chunks
    copies = [
        pltpu.make_async_copy(
            table_ref.at[pl.ds(c * step, step)], tbf_ref.at[pl.ds(c * step, step)], tsem.at[c]
        )
        for c in range(chunks)
    ]
    for copy in copies:
        copy.start()
    ids = pack_ref[:, width : width + LANES].astype(jnp.int32) - place_ref[0] * held
    valid = (ids >= 0) & (ids < held)
    lane = lax.broadcasted_iota(jnp.int32, ids.shape, 1)
    valid = valid & (lane < neighbors)
    ids_ref[...] = jnp.where(valid, ids, 0)
    id_copy = pltpu.make_async_copy(ids_ref, sids_ref, isem)
    id_copy.start()
    mem_low = pack_ref[:, :width].astype(bf16)
    query = dot(mem_low, wq_ref[...], NN)
    q_ref[...] = query
    scale = 1.0 / math.sqrt(head)
    for h in range(HEADS):
        cols = slice(h * head, (h + 1) * head)
        stacked = jnp.concatenate(split(query[:, cols], 3), axis=0)
        full = dot(stacked, wk_ref[:, cols], NT)
        qk = (full[:targets] + full[targets : 2 * targets] + full[2 * targets :]) * scale
        for i, term in enumerate(split(qk, 3)):
            qk_ref[i * hb + h * targets : i * hb + (h + 1) * targets, :] = term
    when_ref[...] = pack_ref[:, width + LANES : width + 2 * LANES]
    id_copy.wait()
    block = math.gcd(step, 320)
    for c in range(chunks):
        copies[c].wait()

        def widen(i, _, c=c):
            at = pl.multiple_of(c * step + i * block, block)
            tab_ref[pl.ds(at, block), :] = tbf_ref[pl.ds(at, block), :].astype(f32)
            return 0

        lax.fori_loop(0, step // block, widen, 0)
    row_of = lax.broadcasted_iota(jnp.int32, (hb, LANES), 0) % targets

    freq, phase = turns_ref[0:1, :], turns_ref[1:2, :]
    pairs = targets // 2
    both = 2 * LANES

    def start_of(pair):
        return pl.multiple_of(pair * both, both)

    def scores_of(pair):
        full = dot(qk_ref[...], x_ref[pl.ds(start_of(pair), both), :], NT)
        return full[:hb] + full[hb : 2 * hb] + full[2 * hb :]

    def keep_scores(pair, part):
        new = jnp.where(row_of == 2 * pair, part[:, :LANES], s_ref[...])
        s_ref[...] = jnp.where(row_of == 2 * pair + 1, part[:, LANES:], new)

    def one_pair(pair, _):
        part = scores_of(jnp.maximum(pair - 1, 0))
        at = start_of(pair)
        for t in range(2):
            elapsed = when_ref[pl.ds(2 * pair + t, 1), :]
            column = jnp.broadcast_to(elapsed, (LANES, LANES)).T
            encoded = cosine(column * freq + phase)
            x_ref[pl.ds(at + t * LANES, LANES), feat:] = encoded.astype(bf16)
        row_ids = [sids_ref.at[2 * pair + t] for t in range(2)]
        for n in range(neighbors):
            for t in range(2):
                rows_ref[t * LANES + n : t * LANES + n + 1, :] = tab_ref[pl.ds(row_ids[t][n], 1), :]
        x_ref[pl.ds(at, both), :feat] = rows_ref[...].astype(bf16)
        for t in range(2):
            latest_ref[pl.ds(2 * pair + t, 1), :] = rows_ref[t * LANES : t * LANES + 1, :]
        keep_scores(pair - 1, part)
        return 0

    s_ref[...] = jnp.zeros(s_ref.shape, f32)
    rows_ref[...] = jnp.zeros(rows_ref.shape, f32)
    lax.fori_loop(0, pairs, one_pair, 0)
    keep_scores(pairs - 1, scores_of(pairs - 1))
    valid2 = jnp.concatenate([valid] * HEADS, axis=0)
    s = s_ref[...]
    top = jnp.max(jnp.where(valid2, s, -1e30), axis=1, keepdims=True)
    p = jnp.where(valid2, jnp.exp(s - top), 0.0)
    p_ref[...] = p
    total = jnp.sum(p, axis=1, keepdims=True)
    acc = weighted(p, x_ref, row_of)
    state_ref[:hb, :] = acc
    lane = lax.broadcasted_iota(jnp.int32, (targets, LANES), 1)
    stat = total[targets:]
    for value, end in ((top[targets:], 96), (total[:targets], 64), (top[:targets], 32)):
        stat = jnp.where(lane < end, value, stat)
    state_ref[hb:, :LANES] = stat
    first = jnp.where(valid, 1.0, 0.0)[:, :1]
    state_ref[hb:, LANES:] = latest_ref[...] * first


def weighted(p, x_ref, row_of):
    hb = p.shape[0]
    targets = hb // HEADS
    terms = jnp.concatenate(split(p, 2), axis=0)
    rows = jnp.concatenate([row_of, row_of], axis=0)
    acc = jnp.zeros((2 * hb, x_ref.shape[1]), f32)
    zero = jnp.zeros_like(terms)
    for pair in range(targets // 2):
        left = jnp.where(rows == 2 * pair, terms, zero)
        right = jnp.where(rows == 2 * pair + 1, terms, zero)
        lhs = jnp.concatenate([left, right], axis=1)
        acc = acc + dot(lhs, x_ref[2 * pair * LANES : 2 * (pair + 1) * LANES, :], NN)
    return acc[:hb] + acc[hb:]


def matmul3(a, b, dims):
    n = a.shape[0]
    full = dot(jnp.concatenate(split(a, 3), axis=0), b, dims)
    return full[:n] + full[n : 2 * n] + full[2 * n :]


def by_head(rows, targets):
    return [rows[h * targets : (h + 1) * targets] for h in range(HEADS)]


def backward(gain_ref, wv_ref, pack_ref, q_ref, p_ref, x_ref, states, replicas):
    width = gain_ref.shape[1]
    head = width // HEADS
    targets = pack_ref.shape[0]
    hb = HEADS * targets
    gain = gain_ref[...]
    row_of = lax.broadcasted_iota(jnp.int32, (hb, LANES), 0) % targets

    def stats(state):
        tops = jnp.concatenate([state[hb:, 0:1], state[hb:, 64:65]], axis=0)
        totals = jnp.concatenate([state[hb:, 32:33], state[hb:, 96:97]], axis=0)
        return tops, totals

    columns = [slice(h * head, (h + 1) * head) for h in range(HEADS)]
    parts = [stats(state) for state in states]
    top = functools.reduce(jnp.maximum, [m for m, _ in parts])
    fac = [jnp.exp(m - top) for m, _ in parts]
    inv = 1.0 / sum(f * l for f, (_, l) in zip(fac, parts))
    attended = sum(f * state[:hb, :] for f, state in zip(fac, states)) * inv
    share = fac[0] * inv
    agg = jnp.concatenate(
        [matmul3(a, wv_ref[:, c], NN) for a, c in zip(by_head(attended, targets), columns)], axis=1
    )
    summed = agg + pack_ref[:, :width]
    centered = summed - jnp.mean(summed, axis=1, keepdims=True)
    inv_std = lax.rsqrt(jnp.mean(centered * centered, axis=1, keepdims=True) + 1e-05)
    normed = centered * inv_std
    gn = pack_ref[:, width + 2 * LANES :] * (1.0 / math.sqrt(replicas)) * gain
    gsum = (
        gn
        - jnp.mean(gn, axis=1, keepdims=True)
        - normed * jnp.mean(gn * normed, axis=1, keepdims=True)
    ) * inv_std
    gv = jnp.concatenate([matmul3(gsum[:, c], wv_ref[:, c], NT) for c in columns], axis=0)
    rowdot = jnp.sum(gv * attended, axis=1, keepdims=True)
    terms = jnp.concatenate(split(gv, 2), axis=0)
    ga = jnp.zeros((hb, LANES), f32)
    for pair in range(targets // 2):
        full = dot(terms, x_ref[2 * pair * LANES : 2 * (pair + 1) * LANES, :], NT)
        full = full[:hb] + full[hb:]
        ga = jnp.where(row_of == 2 * pair, full[:, :LANES], ga)
        ga = jnp.where(row_of == 2 * pair + 1, full[:, LANES:], ga)
    gs = p_ref[...] * share * (ga - rowdot)
    ks = weighted(gs, x_ref, row_of) * (1.0 / math.sqrt(head))
    lefts, rights = [], []
    for k, c in zip(by_head(ks, targets), columns):
        k1, k2 = split(k, 2)
        q1, q2 = split(q_ref[:, c], 2)
        lefts.append(jnp.concatenate([k1, k1, k2], axis=0))
        rights.append(jnp.concatenate([q1, q2, q1], axis=0))
    return normed * gain, attended, gsum, lefts, rights


def other_grad_kernel(*refs, stores, replicas):
    gain_ref, wv_ref, pack_ref, q_ref, p_ref, x_ref = refs[:6]
    states, left_ref, right_ref = refs[6 : 6 + stores], refs[6 + stores], refs[7 + stores]
    *_, lefts, rights = backward(
        gain_ref, wv_ref, pack_ref, q_ref, p_ref, x_ref, states, replicas
    )
    left_ref[...] = jnp.concatenate(lefts, axis=1)
    right_ref[...] = jnp.concatenate(rights, axis=1)


def own_grad_kernel(*refs, stores, replicas, grid):
    place_ref, gain_ref, wv_ref, pack_ref, q_ref, p_ref, x_ref = refs[:7]
    states, refs = refs[7 : 7 + stores], refs[7 + stores :]
    others, refs = refs[: 2 * (stores - 1)], refs[2 * (stores - 1) :]
    emb_ref, keep_ref, send_ref, grad_ref = refs
    his, los = grid
    width = gain_ref.shape[1]
    head = width // HEADS
    kin = wv_ref.shape[0]
    targets = pack_ref.shape[0]
    embedded, attended, gsum, lefts, rights = backward(
        gain_ref, wv_ref, pack_ref, q_ref, p_ref, x_ref, states, replicas
    )
    emb_ref[...] = embedded.astype(bf16)
    for h in range(HEADS):
        cols = slice(h * head, (h + 1) * head)
        a1, a2 = split(by_head(attended, targets)[h], 2)
        g1, g2 = split(gsum[:, cols], 2)
        grad_ref[kin:, cols] = dot(
            jnp.concatenate([a1, a1, a2], axis=0), jnp.concatenate([g1, g2, g1], axis=0), TN
        )
        left = [lefts[h]] + [ref[:, h * kin : (h + 1) * kin] for ref in others[0::2]]
        right = [rights[h]] + [ref[:, cols] for ref in others[1::2]]
        grad_ref[:kin, cols] = dot(
            jnp.concatenate(left, axis=0), jnp.concatenate(right, axis=0), TN
        )
    rows = 2 * kin // replicas
    hi, lo, core, store = (place_ref[i] for i in range(4))
    for lr in range(los):
        for sr in range(stores):
            for hr in range(his):
                to = ((lr * stores + sr) * his + hr) * rows
                base = ((hi ^ hr) * los + (lo ^ lr)) * 2
                for ref, c in ((keep_ref, core), (send_ref, 1 - core)):
                    src = ((base + c) * stores + (store ^ sr)) * rows
                    src = pl.multiple_of(src, rows)
                    ref[to : to + rows, :] = grad_ref[pl.ds(src, rows), :]


def gru_kernel(*refs, stores, targets):
    pack_ref, rows_ref, turns_ref, gi_ref, gh_ref = refs[:5]
    states, out_ref = refs[5 : 5 + stores], refs[5 + stores]
    width = gh_ref.shape[0]
    hb = HEADS * targets
    latest = sum(state[hb:, LANES:] for state in states)
    elapsed = pack_ref[:, width + LANES : width + LANES + 1]
    encoded = cosine(elapsed * turns_ref[0:1, :] + turns_ref[1:2, :])
    inputs = jnp.concatenate([latest.astype(bf16), encoded.astype(bf16)], axis=1)
    mem_rows = pack_ref[:, :width]
    gi = dot(inputs, gi_ref[...], NN)
    gh = dot(mem_rows.astype(bf16), gh_ref[...], NN)
    update = jax.nn.sigmoid(gi[:, :width] + gh[:, :width])
    reset = jax.nn.sigmoid(gi[:, width : 2 * width] + gh[:, width : 2 * width])
    candidate = jnp.tanh(gi[:, 2 * width :] + reset * gh[:, 2 * width :])
    out_ref[:targets, :] = (1.0 - update) * candidate + update * mem_rows
    out_ref[targets:, :] = jnp.zeros((8, width), f32)
    out_ref[targets : targets + 1, :targets] = rows_ref[...].astype(f32)


def place_kernel(memory_ref, new_ref, out_ref, ids_ref, sids_ref, sem):
    targets = new_ref.shape[0] - 8
    ids_ref[...] = new_ref[targets:, :LANES].astype(jnp.int32)
    copy = pltpu.make_async_copy(ids_ref, sids_ref, sem)
    copy.start()
    out_ref[...] = memory_ref[...]
    copy.wait()
    for b in range(targets):
        out_ref[pl.ds(sids_ref[0, b], 1), :] = new_ref[b : b + 1, :]


def sum_split_kernel(*refs, count, outs):
    total = refs[0][...]
    for ref in refs[1:count]:
        total = total + ref[...].astype(f32)
    size = total.shape[0] // outs
    for i, ref in enumerate(refs[count:]):
        ref[...] = total[i * size : (i + 1) * size].astype(ref.dtype)


def last_sum_kernel(*refs):
    total = refs[0][...]
    for ref in refs[1:-1]:
        total = total + ref[...].astype(f32)
    out_ref = refs[-1]
    rows, width = total.shape
    per = width // LANES
    for j in range(per):
        out_ref[pl.ds(j, rows, stride=per), :] = total[:, j * LANES : (j + 1) * LANES]


def call(kernel, ins, outs, scratch=(), specs=None, name=None):
    return pl.pallas_call(
        kernel,
        in_specs=specs or [VM] * len(ins),
        out_specs=[VM] * len(outs),
        out_shape=outs,
        scratch_shapes=list(scratch),
        compiler_params=PARAMS,
        name=name,
    )(*ins)


def near(x):
    return pltpu.with_memory_space_constraint(x, pltpu.VMEM)


def far(x):
    return pltpu.with_memory_space_constraint(x, pltpu.HBM)


def shape(*dims, dtype=f32):
    return pltpu.VMEM(dims, dtype)


def out_shape(*dims, dtype=f32):
    return jax.ShapeDtypeStruct(dims, dtype)


def on_device(
    memory,
    event_feats,
    batch_rows,
    target_time,
    neighbor_owner,
    neighbor_event,
    neighbor_time,
    time_freq,
    time_phase,
    w_query,
    w_key,
    w_value,
    ln_gain,
    gru_input,
    gru_hidden,
    emb_cotangent,
):
    trainers, stores = lax.axis_size("trainer"), lax.axis_size("store")
    replicas = trainers * stores
    targets, neighbors = neighbor_event.shape[1:]
    held, feat = event_feats.shape
    width = memory.shape[1]
    kin = w_key.shape[0]
    hb = HEADS * targets
    trainer, store = lax.axis_index("trainer"), lax.axis_index("store")
    los = 2
    his = trainers // (2 * los)
    place = jnp.stack([trainer // (2 * los), (trainer // 2) % los, trainer % 2, store])
    place = place.astype(jnp.int32)

    sources = [
        batch_rows,
        memory,
        neighbor_owner[0, :, :, 0],
        neighbor_event[0],
        neighbor_time[0],
        target_time,
        emb_cotangent[0],
        time_freq[None],
        time_phase[None],
        w_query,
        w_key,
    ]
    pack, turns, wq_near, wk_near = call(
        functools.partial(pack_kernel, held=held),
        [far(x) for x in sources],
        [
            shape(targets, 2 * width + 2 * LANES),
            shape(8, LANES),
            shape(*w_query.shape, dtype=bf16),
            shape(*w_key.shape, dtype=bf16),
        ],
        scratch=[pltpu.SMEM(batch_rows.shape, jnp.int32)]
        + [pltpu.VMEM(x.shape, x.dtype) for x in sources[1:9]]
        + [pltpu.SemaphoreType.DMA((len(sources),))],
        specs=[FAR] * len(sources),
        name="pack",
    )

    def from_store(value, d):
        return lax.ppermute(value, "store", [((i + d) % stores, i) for i in range(stores)])

    packs = [pack] + [from_store(pack, d) for d in range(1, stores)]
    table = far(event_feats)
    chunks = 4
    local, weights, queries, inputs = [], [], [], []
    for d in range(stores):
        state, p, q, x = call(
            functools.partial(attend_kernel, neighbors=neighbors),
            [
                store[None].astype(jnp.int32),
                near(packs[d]),
                table,
                near(turns),
                near(wq_near),
                near(wk_near),
            ],
            [
                shape(hb + targets, kin),
                shape(hb, LANES),
                shape(targets, width),
                shape(targets * LANES, kin, dtype=bf16),
            ],
            scratch=[
                pltpu.VMEM((held, feat), bf16),
                pltpu.VMEM((held, feat), f32),
                pltpu.VMEM((targets, LANES), jnp.int32),
                pltpu.SMEM((targets, LANES), jnp.int32),
                pltpu.VMEM((2 * LANES, feat), f32),
                pltpu.VMEM((3 * hb, kin), bf16),
                pltpu.VMEM((hb, LANES), f32),
                pltpu.VMEM((targets, LANES), f32),
                pltpu.VMEM((targets, LANES), f32),
                pltpu.SemaphoreType.DMA((chunks,)),
                pltpu.SemaphoreType.DMA,
            ],
            specs=[SM, VM, FAR] + [VM] * 3,
            name="attend",
        )
        local.append(state)
        weights.append(p)
        queries.append(q)
        inputs.append(x)
    gathered = [local] + [[from_store(state, e) for state in local] for e in range(1, stores)]
    states = [[gathered[e][(d - e) % stores] for e in range(stores)] for d in range(stores)]

    def set_of(d):
        return [near(x) for x in (packs[d], queries[d], weights[d], inputs[d], *states[d])]

    gain = ln_gain[None]
    others = []
    for d in range(1, stores):
        ins = [gain, w_value, *set_of(d)]
        others += call(
            functools.partial(other_grad_kernel, stores=stores, replicas=replicas),
            ins,
            [
                shape(3 * targets, HEADS * kin, dtype=bf16),
                shape(3 * targets, width, dtype=bf16),
            ],
            name="other_grads",
        )
    ins = [place, gain, w_value, *set_of(0), *map(near, others)]
    emb, keep, send = call(
        functools.partial(own_grad_kernel, stores=stores, replicas=replicas, grid=(his, los)),
        ins,
        [out_shape(targets, width, dtype=bf16), shape(kin, width), shape(kin, width)],
        scratch=[pltpu.VMEM((2 * kin, width), f32)],
        specs=[SM] + [VM] * (len(ins) - 1),
        name="own_grads",
    )

    (news,) = call(
        functools.partial(gru_kernel, stores=stores, targets=targets),
        [near(pack), batch_rows, near(turns), gru_input, gru_hidden, *map(near, states[0])],
        [shape(targets + 8, width)],
        name="gru",
    )

    def exchange(value, hr, lr, cr, sr):
        def other(i):
            t, s = i // stores, i % stores
            t = ((t // (2 * los)) ^ hr) * 2 * los + (((t // 2) % los) ^ lr) * 2 + ((t % 2) ^ cr)
            return t * stores + (s ^ sr)

        return lax.ppermute(value, AXES, [(i, other(i)) for i in range(replicas)])

    swapped = exchange(send, 0, 0, 1, 0)
    members = los * stores
    out = call(
        functools.partial(sum_split_kernel, count=2, outs=members),
        [near(keep), near(swapped)],
        [shape(kin // members, width)]
        + [shape(kin // members, width, dtype=bf16)] * (members - 1),
        name="core_sum",
    )
    got = [exchange(out[j], 0, j // stores, 0, j % stores) for j in reversed(range(1, members))]
    out = call(
        functools.partial(sum_split_kernel, count=members, outs=his),
        [*map(near, [out[0], *got])],
        [shape(kin // members // his, width)] * his,
        name="plane_sum",
    )
    got = [exchange(out[j], j, 0, 0, 0) for j in reversed(range(1, his))]
    (share,) = call(
        last_sum_kernel,
        [*map(near, [out[0], *got])],
        [out_shape(2 * kin * width // replicas // LANES, LANES)],
        name="last_sum",
    )
    moved = lax.ppermute(news, "trainer", [(i, (i + 1) % trainers) for i in range(trainers)])
    (memory_next,) = call(
        place_kernel,
        [memory, near(moved)],
        [out_shape(*memory.shape)],
        scratch=[
            pltpu.VMEM((8, LANES), jnp.int32),
            pltpu.SMEM((8, LANES), jnp.int32),
            pltpu.SemaphoreType.DMA,
        ],
        name="place",
    )
    return (emb[None], memory_next[None], share.reshape(-1))


def solution(mesh):
    placed = (
        P("store", None),
        P("store", None),
        P("trainer", "store"),
        P("trainer", "store"),
        P("trainer", "store", None, None),
        P("trainer", "store", None),
        P("trainer", "store", None),
        P(),
        P(),
        P(),
        P(),
        P(),
        P(),
        P(),
        P(),
        P("trainer", "store", None),
    )
    return jax.shard_map(
        on_device,
        mesh=mesh,
        in_specs=placed,
        out_specs=(
            P("trainer", "store", None),
            P("trainer", "store", None),
            P(("trainer", "store")),
        ),
        check_vma=False,
    )
```

```python
import functools
import math

import jax
import jax.numpy as jnp
from jax import lax
from jax.experimental import pallas as pl
from jax.experimental.pallas import tpu as pltpu
from jax.sharding import PartitionSpec as P

HEADS = 2
LANES = 128
STRIP = 16
GROUP = 16
TURN = 0.5 / math.pi
AXES = ("trainer", "store")

f32 = jnp.float32
bf16 = jnp.bfloat16
NT = (((1,), (1,)), ((), ()))
NN = (((1,), (0,)), ((), ()))
TN = (((0,), (0,)), ((), ()))
VM = pl.BlockSpec(memory_space=pltpu.VMEM)
SM = pl.BlockSpec(memory_space=pltpu.SMEM)
FAR = pl.BlockSpec(memory_space=pltpu.HBM)
PARAMS = pltpu.CompilerParams(vmem_limit_bytes=20 * 1024 * 1024)


def dot(a, b, dims):
    return lax.dot_general(a, b, dims, preferred_element_type=f32)


def split(x, parts):
    terms = []
    for _ in range(parts):
        term = x.astype(bf16)
        terms.append(term)
        x = x - term.astype(f32)
    return terms


SERIES = (-39.53670604797494, 76.5497822911237, -81.60100407314816, 41.341655031414376, -6.283185160089465)


def cosine(turns):
    part = turns - jnp.floor(turns)
    g = 0.25 - jnp.abs(part - 0.5)
    u = g * g
    c = f32(SERIES[0])
    for k in SERIES[1:]:
        c = c * u + f32(k)
    return c * g


def pack_kernel(*refs, held):
    sources, rest = refs[:11], refs[11:]
    out_ref, turns_ref, wq_out, wk_out = rest[:4]
    kept, sems = rest[4:13], rest[13]
    rows_ref, memory_ref, own_ref, event_ref, ntime_ref, ttime_ref, cot_ref, freq_ref, phase_ref = kept
    copies = [
        pltpu.make_async_copy(src, dst, sems.at[i])
        for i, (src, dst) in enumerate(zip(sources, (*kept, wq_out, wk_out)))
    ]
    for copy in copies:
        copy.start()
    for copy in copies[:-2]:
        copy.wait()
    turns_ref[0:1, :] = freq_ref[...] * TURN
    turns_ref[1:2, :] = phase_ref[...] * TURN
    turns_ref[2:, :] = jnp.zeros((turns_ref.shape[0] - 2, LANES), f32)
    targets, neighbors = event_ref.shape
    width = memory_ref.shape[1]
    ids = own_ref[...] * held + event_ref[...]
    out_ref[:, width : width + 2 * LANES] = jnp.full((targets, 2 * LANES), -1.0, f32)
    out_ref[:, width : width + neighbors] = ids.astype(f32)
    row = lax.broadcasted_iota(jnp.int32, (targets, targets), 0)
    lane = lax.broadcasted_iota(jnp.int32, (targets, targets), 1)
    times = jnp.sum(jnp.where(row == lane, ttime_ref[...].astype(f32), 0.0), axis=1, keepdims=True)
    elapsed = times - ntime_ref[...].astype(f32)
    out_ref[:, width + LANES : width + LANES + neighbors] = elapsed.astype(f32)
    out_ref[:, width + 2 * LANES :] = cot_ref[...].astype(f32)
    for b in range(targets):
        out_ref[pl.ds(b, 1), :width] = memory_ref[pl.ds(rows_ref[0, b], 1), :]
    for copy in copies[-2:]:
        copy.wait()


def attend_kernel(*refs, neighbors):
    place_ref, pack_ref, table_ref, turns_ref, wq_ref, wk_ref = refs[:6]
    state_ref, p_ref, q_ref, x_ref = refs[6:10]
    tbf_ref, tab_ref, ids_ref, sids_ref, rows_ref, qk_ref, s_ref, when_ref, latest_ref = refs[10:19]
    column_ref, lo_ref, hi_ref, src_ref, acc_ref, tsem, isem = refs[19:]
    targets = pack_ref.shape[0]
    width = wq_ref.shape[0]
    kin = wk_ref.shape[0]
    feat = tab_ref.shape[1]
    head = width // HEADS
    hb = HEADS * targets
    held = tab_ref.shape[0]
    chunks = tsem.shape[0]
    step = held // chunks
    copies = [
        pltpu.make_async_copy(
            table_ref.at[pl.ds(c * step, step)], tbf_ref.at[pl.ds(c * step, step)], tsem.at[c]
        )
        for c in range(chunks)
    ]
    for copy in copies:
        copy.start()
    ids = pack_ref[:, width : width + LANES].astype(jnp.int32) - place_ref[0] * held
    valid = (ids >= 0) & (ids < held)
    lane = lax.broadcasted_iota(jnp.int32, ids.shape, 1)
    valid = valid & (lane < neighbors)
    ids_ref[...] = jnp.where(valid, ids, 0)
    id_copy = pltpu.make_async_copy(ids_ref, sids_ref, isem)
    id_copy.start()
    mem_low = pack_ref[:, :width].astype(bf16)
    query = dot(mem_low, wq_ref[...], NN)
    q_ref[...] = query
    scale = 1.0 / math.sqrt(head)
    qk = []
    for h in range(HEADS):
        cols = slice(h * head, (h + 1) * head)
        qk.append(matmul3(query[:, cols], wk_ref[:, cols], NT) * scale)
    qk = split(jnp.concatenate(qk, axis=0), 3)
    qk_ref[...] = by_pair(qk, False, lo_ref, hi_ref, src_ref, targets)
    when_ref[...] = pack_ref[:, width + LANES : width + 2 * LANES]

    def stand_up(b, _):
        elapsed = when_ref[pl.ds(b, 1), :]
        at = pl.multiple_of(b * LANES, LANES)
        column_ref[pl.ds(at, LANES), :] = jnp.broadcast_to(elapsed, (LANES, LANES)).T
        return 0

    lax.fori_loop(0, targets, stand_up, 0, unroll=8)
    id_copy.wait()
    block = math.gcd(step, 320)
    for c in range(chunks):
        copies[c].wait()

        def widen(i, _, c=c):
            at = pl.multiple_of(c * step + i * block, block)
            tab_ref[pl.ds(at, block), :] = tbf_ref[pl.ds(at, block), :].astype(f32)
            return 0

        lax.fori_loop(0, step // block, widen, 0)

    freq, phase = turns_ref[0:1, :], turns_ref[1:2, :]
    pairs = targets // 2
    both = 2 * LANES

    def start_of(pair):
        return pl.multiple_of(pair * both, both)

    freq, phase = turns_ref[0:1, :], turns_ref[1:2, :]
    pairs = targets // 2
    both = 2 * LANES

    def one_pair(pair, _):
        at = pl.multiple_of(pair * both, both)
        row_ids = [sids_ref.at[2 * pair + t] for t in range(2)]
        todo = [(n, t) for n in range(neighbors) for t in range(2)]
        strips = both // STRIP
        for i in range(strips):
            here = pl.ds(at + i * STRIP, STRIP)
            x_ref[here, feat:] = cosine(column_ref[here, :] * freq + phase).astype(bf16)
            for n, t in todo[i * len(todo) // strips : (i + 1) * len(todo) // strips]:
                rows_ref[t * LANES + n : t * LANES + n + 1, :] = tab_ref[pl.ds(row_ids[t][n], 1), :]
        x_ref[pl.ds(at, both), :feat] = rows_ref[...].astype(bf16)
        for t in range(2):
            latest_ref[pl.ds(2 * pair + t, 1), :] = rows_ref[t * LANES : t * LANES + 1, :]
        return 0

    rows_ref[...] = jnp.zeros(rows_ref.shape, f32)
    lax.fori_loop(0, pairs, one_pair, 0)
    for pair in range(pairs):
        rows = qk_ref[pair * GROUP : (pair + 1) * GROUP, :]
        part = add_terms(dot(rows, x_ref[pair * both : (pair + 1) * both, :], NT), 3)
        for h in range(HEADS):
            for t in range(2):
                to = h * targets + 2 * pair + t
                row = part[2 * h + t : 2 * h + t + 1, t * LANES : (t + 1) * LANES]
                s_ref[to : to + 1, :] = row
    valid2 = jnp.concatenate([valid] * HEADS, axis=0)
    s = s_ref[...]
    top = jnp.max(jnp.where(valid2, s, -1e30), axis=1, keepdims=True)
    p = jnp.where(valid2, jnp.exp(s - top), 0.0)
    p_ref[...] = p
    total = jnp.sum(p, axis=1, keepdims=True)
    state_ref[:hb, :] = weighted(p, x_ref, lo_ref, hi_ref, src_ref, acc_ref)
    lane = lax.broadcasted_iota(jnp.int32, (targets, LANES), 1)
    stat = total[targets:]
    for value, end in ((top[targets:], 96), (total[:targets], 64), (top[:targets], 32)):
        stat = jnp.where(lane < end, value, stat)
    state_ref[hb:, :LANES] = stat
    first = jnp.where(valid, 1.0, 0.0)[:, :1]
    state_ref[hb:, LANES:] = latest_ref[...] * first


def by_pair(terms, lanes, lo_ref, hi_ref, src_ref, targets):
    hb = HEADS * targets
    pairs = targets // 2
    lo_ref[...] = jnp.zeros(lo_ref.shape, f32)
    hi_ref[...] = jnp.zeros(hi_ref.shape, f32)
    for i, term in enumerate(terms):
        for j in range(term.shape[1] // LANES):
            base = (2 * i + j) * hb
            src_ref[base : base + hb, :] = term[:, j * LANES : (j + 1) * LANES].astype(f32)
            for h in range(HEADS):
                for t in range(2):
                    ref = (lo_ref, hi_ref)[t if lanes else j]
                    rows = pl.ds(2 * HEADS * i + 2 * h + t, pairs, stride=GROUP)
                    ref[rows, :] = src_ref[pl.ds(base + h * targets + t, pairs, stride=2), :]
    return jnp.concatenate([lo_ref[...], hi_ref[...]], axis=1).astype(bf16)


def add_terms(full, count):
    step = 2 * HEADS
    return sum(full[i * step : (i + 1) * step] for i in range(1, count)) + full[:step]


def weighted(p, x_ref, lo_ref, hi_ref, src_ref, out_ref):
    hb = p.shape[0]
    targets = hb // HEADS
    rows = by_pair(split(p, 2), True, lo_ref, hi_ref, src_ref, targets)
    for pair in range(targets // 2):
        here = rows[pair * GROUP : (pair + 1) * GROUP]
        full = dot(here, x_ref[2 * pair * LANES : 2 * (pair + 1) * LANES, :], NN)
        part = add_terms(full, 2)
        for h in range(HEADS):
            to = h * targets + 2 * pair
            out_ref[to : to + 2, :] = part[2 * h : 2 * h + 2]
    return out_ref[...]


def matmul3(a, b, dims):
    n = a.shape[0]
    full = dot(jnp.concatenate(split(a, 3), axis=0), b, dims)
    return full[:n] + full[n : 2 * n] + full[2 * n :]


def by_head(rows, targets):
    return [rows[h * targets : (h + 1) * targets] for h in range(HEADS)]


def backward(gain_ref, wv_ref, pack_ref, q_ref, p_ref, x_ref, states, replicas, scratch):
    width = gain_ref.shape[1]
    head = width // HEADS
    targets = pack_ref.shape[0]
    hb = HEADS * targets
    gain = gain_ref[...]

    def stats(state):
        tops = jnp.concatenate([state[hb:, 0:1], state[hb:, 64:65]], axis=0)
        totals = jnp.concatenate([state[hb:, 32:33], state[hb:, 96:97]], axis=0)
        return tops, totals

    columns = [slice(h * head, (h + 1) * head) for h in range(HEADS)]
    parts = [stats(state) for state in states]
    top = functools.reduce(jnp.maximum, [m for m, _ in parts])
    fac = [jnp.exp(m - top) for m, _ in parts]
    inv = 1.0 / sum(f * l for f, (_, l) in zip(fac, parts))
    attended = sum(f * state[:hb, :] for f, state in zip(fac, states)) * inv
    share = fac[0] * inv
    agg = jnp.concatenate(
        [matmul3(a, wv_ref[:, c], NN) for a, c in zip(by_head(attended, targets), columns)], axis=1
    )
    summed = agg + pack_ref[:, :width]
    centered = summed - jnp.mean(summed, axis=1, keepdims=True)
    inv_std = lax.rsqrt(jnp.mean(centered * centered, axis=1, keepdims=True) + 1e-05)
    normed = centered * inv_std
    gn = pack_ref[:, width + 2 * LANES :] * (1.0 / math.sqrt(replicas)) * gain
    gsum = (
        gn
        - jnp.mean(gn, axis=1, keepdims=True)
        - normed * jnp.mean(gn * normed, axis=1, keepdims=True)
    ) * inv_std
    gv = jnp.concatenate([matmul3(gsum[:, c], wv_ref[:, c], NT) for c in columns], axis=0)
    rowdot = jnp.sum(gv * attended, axis=1, keepdims=True)
    *pair_refs, acc_ref, ga_ref = scratch
    rows = by_pair(split(gv, 3), False, *pair_refs, targets)
    for pair in range(targets // 2):
        here = rows[pair * GROUP : (pair + 1) * GROUP]
        part = add_terms(dot(here, x_ref[2 * pair * LANES : 2 * (pair + 1) * LANES, :], NT), 3)
        for h in range(HEADS):
            for t in range(2):
                to = h * targets + 2 * pair + t
                row = part[2 * h + t : 2 * h + t + 1, t * LANES : (t + 1) * LANES]
                ga_ref[to : to + 1, :] = row
    gs = p_ref[...] * share * (ga_ref[...] - rowdot)
    ks = weighted(gs, x_ref, *pair_refs, acc_ref) * (1.0 / math.sqrt(head))
    lefts, rights = [], []
    for k, c in zip(by_head(ks, targets), columns):
        k1, k2 = split(k, 2)
        q1, q2 = split(q_ref[:, c], 2)
        lefts.append(jnp.concatenate([k1, k1, k2], axis=0))
        rights.append(jnp.concatenate([q1, q2, q1], axis=0))
    return normed * gain, attended, gsum, lefts, rights


def other_grad_kernel(*refs, stores, replicas):
    gain_ref, wv_ref, pack_ref, q_ref, p_ref, x_ref = refs[:6]
    states, refs = refs[6 : 6 + stores], refs[6 + stores :]
    left_ref, right_ref, *scratch = refs
    *_, lefts, rights = backward(
        gain_ref, wv_ref, pack_ref, q_ref, p_ref, x_ref, states, replicas, scratch
    )
    left_ref[...] = jnp.concatenate(lefts, axis=1)
    right_ref[...] = jnp.concatenate(rights, axis=1)


def own_grad_kernel(*refs, stores, replicas, grid):
    place_ref, gain_ref, wv_ref, pack_ref, q_ref, p_ref, x_ref = refs[:7]
    states, refs = refs[7 : 7 + stores], refs[7 + stores :]
    others, refs = refs[: 2 * (stores - 1)], refs[2 * (stores - 1) :]
    emb_ref, keep_ref, send_ref, grad_ref, *scratch = refs
    his, los = grid
    width = gain_ref.shape[1]
    head = width // HEADS
    kin = wv_ref.shape[0]
    targets = pack_ref.shape[0]
    embedded, attended, gsum, lefts, rights = backward(
        gain_ref, wv_ref, pack_ref, q_ref, p_ref, x_ref, states, replicas, scratch
    )
    emb_ref[...] = embedded.astype(bf16)
    for h in range(HEADS):
        cols = slice(h * head, (h + 1) * head)
        a1, a2 = split(by_head(attended, targets)[h], 2)
        g1, g2 = split(gsum[:, cols], 2)
        grad_ref[kin:, cols] = dot(
            jnp.concatenate([a1, a1, a2], axis=0), jnp.concatenate([g1, g2, g1], axis=0), TN
        )
        left = [lefts[h]] + [ref[:, h * kin : (h + 1) * kin] for ref in others[0::2]]
        right = [rights[h]] + [ref[:, cols] for ref in others[1::2]]
        grad_ref[:kin, cols] = dot(
            jnp.concatenate(left, axis=0), jnp.concatenate(right, axis=0), TN
        )
    rows = 2 * kin // replicas
    hi, lo, core, store = (place_ref[i] for i in range(4))
    for lr in range(los):
        for sr in range(stores):
            for hr in range(his):
                to = ((lr * stores + sr) * his + hr) * rows
                base = ((hi ^ hr) * los + (lo ^ lr)) * 2
                for ref, c in ((keep_ref, core), (send_ref, 1 - core)):
                    src = ((base + c) * stores + (store ^ sr)) * rows
                    src = pl.multiple_of(src, rows)
                    ref[to : to + rows, :] = grad_ref[pl.ds(src, rows), :]


def gru_kernel(*refs, stores, targets):
    pack_ref, rows_ref, turns_ref, gi_ref, gh_ref = refs[:5]
    states, out_ref = refs[5 : 5 + stores], refs[5 + stores]
    width = gh_ref.shape[0]
    hb = HEADS * targets
    latest = sum(state[hb:, LANES:] for state in states)
    elapsed = pack_ref[:, width + LANES : width + LANES + 1]
    encoded = cosine(elapsed * turns_ref[0:1, :] + turns_ref[1:2, :])
    inputs = jnp.concatenate([latest.astype(bf16), encoded.astype(bf16)], axis=1)
    mem_rows = pack_ref[:, :width]
    gi = dot(inputs, gi_ref[...], NN)
    gh = dot(mem_rows.astype(bf16), gh_ref[...], NN)
    update = jax.nn.sigmoid(gi[:, :width] + gh[:, :width])
    reset = jax.nn.sigmoid(gi[:, width : 2 * width] + gh[:, width : 2 * width])
    candidate = jnp.tanh(gi[:, 2 * width :] + reset * gh[:, 2 * width :])
    out_ref[:targets, :] = (1.0 - update) * candidate + update * mem_rows
    out_ref[targets:, :] = jnp.zeros((8, width), f32)
    out_ref[targets : targets + 1, :targets] = rows_ref[...].astype(f32)


def place_kernel(memory_ref, new_ref, out_ref, ids_ref, sids_ref, sem):
    targets = new_ref.shape[0] - 8
    ids_ref[...] = new_ref[targets:, :LANES].astype(jnp.int32)
    copy = pltpu.make_async_copy(ids_ref, sids_ref, sem)
    copy.start()
    out_ref[...] = memory_ref[...]
    copy.wait()
    for b in range(targets):
        out_ref[pl.ds(sids_ref[0, b], 1), :] = new_ref[b : b + 1, :]


def sum_split_kernel(*refs, count, outs):
    total = refs[0][...]
    for ref in refs[1:count]:
        total = total + ref[...].astype(f32)
    size = total.shape[0] // outs
    for i, ref in enumerate(refs[count:]):
        ref[...] = total[i * size : (i + 1) * size].astype(ref.dtype)


def last_sum_kernel(*refs):
    total = refs[0][...]
    for ref in refs[1:-1]:
        total = total + ref[...].astype(f32)
    out_ref = refs[-1]
    rows, width = total.shape
    per = width // LANES
    for j in range(per):
        out_ref[pl.ds(j, rows, stride=per), :] = total[:, j * LANES : (j + 1) * LANES]


def call(kernel, ins, outs, scratch=(), specs=None, name=None):
    return pl.pallas_call(
        kernel,
        in_specs=specs or [VM] * len(ins),
        out_specs=[VM] * len(outs),
        out_shape=outs,
        scratch_shapes=list(scratch),
        compiler_params=PARAMS,
        name=name,
    )(*ins)


def near(x):
    return pltpu.with_memory_space_constraint(x, pltpu.VMEM)


def far(x):
    return pltpu.with_memory_space_constraint(x, pltpu.HBM)


def shape(*dims, dtype=f32):
    return pltpu.VMEM(dims, dtype)


def out_shape(*dims, dtype=f32):
    return jax.ShapeDtypeStruct(dims, dtype)


def on_device(
    memory,
    event_feats,
    batch_rows,
    target_time,
    neighbor_owner,
    neighbor_event,
    neighbor_time,
    time_freq,
    time_phase,
    w_query,
    w_key,
    w_value,
    ln_gain,
    gru_input,
    gru_hidden,
    emb_cotangent,
):
    trainers, stores = lax.axis_size("trainer"), lax.axis_size("store")
    replicas = trainers * stores
    targets, neighbors = neighbor_event.shape[1:]
    held, feat = event_feats.shape
    width = memory.shape[1]
    kin = w_key.shape[0]
    hb = HEADS * targets
    trainer, store = lax.axis_index("trainer"), lax.axis_index("store")
    los = 2
    his = trainers // (2 * los)
    place = jnp.stack([trainer // (2 * los), (trainer // 2) % los, trainer % 2, store])
    place = place.astype(jnp.int32)

    sources = [
        batch_rows,
        memory,
        neighbor_owner[0, :, :, 0],
        neighbor_event[0],
        neighbor_time[0],
        target_time,
        emb_cotangent[0],
        time_freq[None],
        time_phase[None],
        w_query,
        w_key,
    ]
    pack, turns, wq_near, wk_near = call(
        functools.partial(pack_kernel, held=held),
        [far(x) for x in sources],
        [
            shape(targets, 2 * width + 2 * LANES),
            shape(8, LANES),
            shape(*w_query.shape, dtype=bf16),
            shape(*w_key.shape, dtype=bf16),
        ],
        scratch=[pltpu.SMEM(batch_rows.shape, jnp.int32)]
        + [pltpu.VMEM(x.shape, x.dtype) for x in sources[1:9]]
        + [pltpu.SemaphoreType.DMA((len(sources),))],
        specs=[FAR] * len(sources),
        name="pack",
    )

    def from_store(value, d):
        return lax.ppermute(value, "store", [((i + d) % stores, i) for i in range(stores)])

    packs = [pack] + [from_store(pack, d) for d in range(1, stores)]
    table = far(event_feats)
    chunks = 4
    pair_scratch = [
        pltpu.VMEM((GROUP * targets // 2, LANES), f32),
        pltpu.VMEM((GROUP * targets // 2, LANES), f32),
        pltpu.VMEM((6 * hb, LANES), f32),
        pltpu.VMEM((hb, kin), f32),
    ]
    local, weights, queries, inputs = [], [], [], []
    for d in range(stores):
        state, p, q, x = call(
            functools.partial(attend_kernel, neighbors=neighbors),
            [
                store[None].astype(jnp.int32),
                near(packs[d]),
                table,
                near(turns),
                near(wq_near),
                near(wk_near),
            ],
            [
                shape(hb + targets, kin),
                shape(hb, LANES),
                shape(targets, width),
                shape(targets * LANES, kin, dtype=bf16),
            ],
            scratch=[
                pltpu.VMEM((held, feat), bf16),
                pltpu.VMEM((held, feat), f32),
                pltpu.VMEM((targets, LANES), jnp.int32),
                pltpu.SMEM((targets, LANES), jnp.int32),
                pltpu.VMEM((2 * LANES, feat), f32),
                pltpu.VMEM((GROUP * targets // 2, kin), bf16),
                pltpu.VMEM((hb, LANES), f32),
                pltpu.VMEM((targets, LANES), f32),
                pltpu.VMEM((targets, LANES), f32),
                pltpu.VMEM((targets * LANES, LANES), f32),
                *pair_scratch,
                pltpu.SemaphoreType.DMA((chunks,)),
                pltpu.SemaphoreType.DMA,
            ],
            specs=[SM, VM, FAR] + [VM] * 3,
            name="attend",
        )
        local.append(state)
        weights.append(p)
        queries.append(q)
        inputs.append(x)
    gathered = [local] + [[from_store(state, e) for state in local] for e in range(1, stores)]
    states = [[gathered[e][(d - e) % stores] for e in range(stores)] for d in range(stores)]

    def set_of(d):
        return [near(x) for x in (packs[d], queries[d], weights[d], inputs[d], *states[d])]

    gain = ln_gain[None]
    others = []
    for d in range(1, stores):
        ins = [gain, w_value, *set_of(d)]
        others += call(
            functools.partial(other_grad_kernel, stores=stores, replicas=replicas),
            ins,
            [
                shape(3 * targets, HEADS * kin, dtype=bf16),
                shape(3 * targets, width, dtype=bf16),
            ],
            scratch=[*pair_scratch, pltpu.VMEM((hb, LANES), f32)],
            name="other_grads",
        )
    ins = [place, gain, w_value, *set_of(0), *map(near, others)]
    emb, keep, send = call(
        functools.partial(own_grad_kernel, stores=stores, replicas=replicas, grid=(his, los)),
        ins,
        [out_shape(targets, width, dtype=bf16), shape(kin, width), shape(kin, width)],
        scratch=[pltpu.VMEM((2 * kin, width), f32), *pair_scratch, pltpu.VMEM((hb, LANES), f32)],
        specs=[SM] + [VM] * (len(ins) - 1),
        name="own_grads",
    )

    (news,) = call(
        functools.partial(gru_kernel, stores=stores, targets=targets),
        [near(pack), batch_rows, near(turns), gru_input, gru_hidden, *map(near, states[0])],
        [shape(targets + 8, width)],
        name="gru",
    )

    def exchange(value, hr, lr, cr, sr):
        def other(i):
            t, s = i // stores, i % stores
            t = ((t // (2 * los)) ^ hr) * 2 * los + (((t // 2) % los) ^ lr) * 2 + ((t % 2) ^ cr)
            return t * stores + (s ^ sr)

        return lax.ppermute(value, AXES, [(i, other(i)) for i in range(replicas)])

    swapped = exchange(send, 0, 0, 1, 0)
    members = los * stores
    out = call(
        functools.partial(sum_split_kernel, count=2, outs=members),
        [near(keep), near(swapped)],
        [shape(kin // members, width)]
        + [shape(kin // members, width, dtype=bf16)] * (members - 1),
        name="core_sum",
    )
    got = [exchange(out[j], 0, j // stores, 0, j % stores) for j in reversed(range(1, members))]
    out = call(
        functools.partial(sum_split_kernel, count=members, outs=his),
        [*map(near, [out[0], *got])],
        [shape(kin // members // his, width)] * his,
        name="plane_sum",
    )
    got = [exchange(out[j], j, 0, 0, 0) for j in reversed(range(1, his))]
    (share,) = call(
        last_sum_kernel,
        [*map(near, [out[0], *got])],
        [out_shape(2 * kin * width // replicas // LANES, LANES)],
        name="last_sum",
    )
    moved = lax.ppermute(news, "trainer", [(i, (i + 1) % trainers) for i in range(trainers)])
    (memory_next,) = call(
        place_kernel,
        [memory, near(moved)],
        [out_shape(*memory.shape)],
        scratch=[
            pltpu.VMEM((8, LANES), jnp.int32),
            pltpu.SMEM((8, LANES), jnp.int32),
            pltpu.SemaphoreType.DMA,
        ],
        name="place",
    )
    return (emb[None], memory_next[None], share.reshape(-1))


def solution(mesh):
    placed = (
        P("store", None),
        P("store", None),
        P("trainer", "store"),
        P("trainer", "store"),
        P("trainer", "store", None, None),
        P("trainer", "store", None),
        P("trainer", "store", None),
        P(),
        P(),
        P(),
        P(),
        P(),
        P(),
        P(),
        P(),
        P("trainer", "store", None),
    )
    return jax.shard_map(
        on_device,
        mesh=mesh,
        in_specs=placed,
        out_specs=(
            P("trainer", "store", None),
            P("trainer", "store", None),
            P(("trainer", "store")),
        ),
        check_vma=False,
    )
```

```python
import functools
import math

import jax
import jax.numpy as jnp
from jax import lax
from jax.experimental import pallas as pl
from jax.experimental.pallas import tpu as pltpu
from jax.sharding import PartitionSpec as P

HEADS = 2
LANES = 128
STRIP = 16
GROUP = 16
TURN = 0.5 / math.pi
AXES = ("trainer", "store")

f32 = jnp.float32
bf16 = jnp.bfloat16
NT = (((1,), (1,)), ((), ()))
NN = (((1,), (0,)), ((), ()))
TN = (((0,), (0,)), ((), ()))
VM = pl.BlockSpec(memory_space=pltpu.VMEM)
FAR = pl.BlockSpec(memory_space=pltpu.HBM)
PARAMS = pltpu.CompilerParams(vmem_limit_bytes=20 * 1024 * 1024)


def dot(a, b, dims):
    return lax.dot_general(a, b, dims, preferred_element_type=f32)


def split(x, parts):
    terms = []
    for _ in range(parts):
        term = x.astype(bf16)
        terms.append(term)
        x = x - term.astype(f32)
    return terms


SERIES = (-39.53670604797494, 76.5497822911237, -81.60100407314816, 41.341655031414376, -6.283185160089465)


def cosine(turns):
    part = turns - jnp.floor(turns)
    g = 0.25 - jnp.abs(part - 0.5)
    u = g * g
    c = f32(SERIES[0])
    for k in SERIES[1:]:
        c = c * u + f32(k)
    return c * g


def pack_kernel(*refs, held):
    sources, rest = refs[:11], refs[11:]
    out_ref, turns_ref, wq_out, wk_out = rest[:4]
    kept, sems = rest[4:13], rest[13]
    rows_ref, memory_ref, own_ref, event_ref, ntime_ref, ttime_ref, cot_ref, freq_ref, phase_ref = kept
    copies = [
        pltpu.make_async_copy(src, dst, sems.at[i])
        for i, (src, dst) in enumerate(zip(sources, (*kept, wq_out, wk_out)))
    ]
    for copy in copies:
        copy.start()
    for copy in copies[:-2]:
        copy.wait()
    turns_ref[0:1, :] = freq_ref[...] * TURN
    turns_ref[1:2, :] = phase_ref[...] * TURN
    turns_ref[2:, :] = jnp.zeros((turns_ref.shape[0] - 2, LANES), f32)
    targets, neighbors = event_ref.shape
    width = memory_ref.shape[1]
    ids = own_ref[...] * held + event_ref[...]
    out_ref[:, width : width + 2 * LANES] = jnp.full((targets, 2 * LANES), -1.0, f32)
    out_ref[:, width : width + neighbors] = ids.astype(f32)
    row = lax.broadcasted_iota(jnp.int32, (targets, targets), 0)
    lane = lax.broadcasted_iota(jnp.int32, (targets, targets), 1)
    times = jnp.sum(jnp.where(row == lane, ttime_ref[...].astype(f32), 0.0), axis=1, keepdims=True)
    elapsed = times - ntime_ref[...].astype(f32)
    out_ref[:, width + LANES : width + LANES + neighbors] = elapsed.astype(f32)
    out_ref[:, width + 2 * LANES :] = cot_ref[...].astype(f32)
    for b in range(targets):
        out_ref[pl.ds(b, 1), :width] = memory_ref[pl.ds(rows_ref[0, b], 1), :]
    for copy in copies[-2:]:
        copy.wait()


def attend_kernel(*refs, neighbors):
    pack_ref, table_ref, turns_ref, wq_ref, wk_ref = refs[:5]
    state_ref, p_ref, q_ref, x_ref = refs[5:9]
    tbf_ref, tab_ref, ids_ref, sids_ref, rows_ref, qk_ref, s_ref, when_ref, latest_ref = refs[9:18]
    column_ref, lo_ref, hi_ref, src_ref, acc_ref, tsem, isem = refs[18:]
    targets = pack_ref.shape[0]
    width = wq_ref.shape[0]
    kin = wk_ref.shape[0]
    feat = tab_ref.shape[1]
    head = width // HEADS
    hb = HEADS * targets
    held = tab_ref.shape[0]
    chunks = tsem.shape[0]
    step = held // chunks
    copies = [
        pltpu.make_async_copy(
            table_ref.at[pl.ds(c * step, step)], tbf_ref.at[pl.ds(c * step, step)], tsem.at[c]
        )
        for c in range(chunks)
    ]
    for copy in copies:
        copy.start()
    ids = pack_ref[:, width : width + LANES].astype(jnp.int32) - lax.axis_index("store") * held
    valid = (ids >= 0) & (ids < held)
    lane = lax.broadcasted_iota(jnp.int32, ids.shape, 1)
    valid = valid & (lane < neighbors)
    ids_ref[...] = jnp.where(valid, ids, 0)
    id_copy = pltpu.make_async_copy(ids_ref, sids_ref, isem)
    id_copy.start()
    mem_low = pack_ref[:, :width].astype(bf16)
    query = dot(mem_low, wq_ref[...], NN)
    q_ref[...] = query
    scale = 1.0 / math.sqrt(head)
    qk = []
    for h in range(HEADS):
        cols = slice(h * head, (h + 1) * head)
        qk.append(matmul3(query[:, cols], wk_ref[:, cols], NT) * scale)
    qk = split(jnp.concatenate(qk, axis=0), 3)
    qk_ref[...] = by_pair(qk, False, lo_ref, hi_ref, src_ref, targets)
    when_ref[...] = pack_ref[:, width + LANES : width + 2 * LANES]

    def stand_up(b, _):
        elapsed = when_ref[pl.ds(b, 1), :]
        at = pl.multiple_of(b * LANES, LANES)
        column_ref[pl.ds(at, LANES), :] = jnp.broadcast_to(elapsed, (LANES, LANES)).T
        return 0

    lax.fori_loop(0, targets, stand_up, 0, unroll=8)
    id_copy.wait()
    block = math.gcd(step, 320)
    for c in range(chunks):
        copies[c].wait()

        def widen(i, _, c=c):
            at = pl.multiple_of(c * step + i * block, block)
            tab_ref[pl.ds(at, block), :] = tbf_ref[pl.ds(at, block), :].astype(f32)
            return 0

        lax.fori_loop(0, step // block, widen, 0)

    freq, phase = turns_ref[0:1, :], turns_ref[1:2, :]
    pairs = targets // 2
    both = 2 * LANES

    def start_of(pair):
        return pl.multiple_of(pair * both, both)

    freq, phase = turns_ref[0:1, :], turns_ref[1:2, :]
    pairs = targets // 2
    both = 2 * LANES

    def one_pair(pair, _):
        at = pl.multiple_of(pair * both, both)
        row_ids = [sids_ref.at[2 * pair + t] for t in range(2)]
        todo = [(n, t) for n in range(neighbors) for t in range(2)]
        strips = both // STRIP
        for i in range(strips):
            here = pl.ds(at + i * STRIP, STRIP)
            x_ref[here, feat:] = cosine(column_ref[here, :] * freq + phase).astype(bf16)
            for n, t in todo[i * len(todo) // strips : (i + 1) * len(todo) // strips]:
                rows_ref[t * LANES + n : t * LANES + n + 1, :] = tab_ref[pl.ds(row_ids[t][n], 1), :]
        x_ref[pl.ds(at, both), :feat] = rows_ref[...].astype(bf16)
        for t in range(2):
            latest_ref[pl.ds(2 * pair + t, 1), :] = rows_ref[t * LANES : t * LANES + 1, :]
        return 0

    rows_ref[...] = jnp.zeros(rows_ref.shape, f32)
    lax.fori_loop(0, pairs, one_pair, 0)
    for pair in range(pairs):
        rows = qk_ref[pair * GROUP : (pair + 1) * GROUP, :]
        part = add_terms(dot(rows, x_ref[pair * both : (pair + 1) * both, :], NT), 3)
        for h in range(HEADS):
            for t in range(2):
                to = h * targets + 2 * pair + t
                row = part[2 * h + t : 2 * h + t + 1, t * LANES : (t + 1) * LANES]
                s_ref[to : to + 1, :] = row
    valid2 = jnp.concatenate([valid] * HEADS, axis=0)
    s = s_ref[...]
    top = jnp.max(jnp.where(valid2, s, -1e30), axis=1, keepdims=True)
    p = jnp.where(valid2, jnp.exp(s - top), 0.0)
    p_ref[...] = p
    total = jnp.sum(p, axis=1, keepdims=True)
    state_ref[:hb, :] = weighted(p, x_ref, lo_ref, hi_ref, src_ref, acc_ref)
    lane = lax.broadcasted_iota(jnp.int32, (targets, LANES), 1)
    stat = total[targets:]
    for value, end in ((top[targets:], 96), (total[:targets], 64), (top[:targets], 32)):
        stat = jnp.where(lane < end, value, stat)
    state_ref[hb:, :LANES] = stat
    first = jnp.where(valid, 1.0, 0.0)[:, :1]
    state_ref[hb:, LANES:] = latest_ref[...] * first


def by_pair(terms, lanes, lo_ref, hi_ref, src_ref, targets):
    hb = HEADS * targets
    pairs = targets // 2
    lo_ref[...] = jnp.zeros(lo_ref.shape, f32)
    hi_ref[...] = jnp.zeros(hi_ref.shape, f32)
    for i, term in enumerate(terms):
        for j in range(term.shape[1] // LANES):
            base = (2 * i + j) * hb
            src_ref[base : base + hb, :] = term[:, j * LANES : (j + 1) * LANES].astype(f32)
            for h in range(HEADS):
                for t in range(2):
                    ref = (lo_ref, hi_ref)[t if lanes else j]
                    rows = pl.ds(2 * HEADS * i + 2 * h + t, pairs, stride=GROUP)
                    ref[rows, :] = src_ref[pl.ds(base + h * targets + t, pairs, stride=2), :]
    return jnp.concatenate([lo_ref[...], hi_ref[...]], axis=1).astype(bf16)


def add_terms(full, count):
    step = 2 * HEADS
    return sum(full[i * step : (i + 1) * step] for i in range(1, count)) + full[:step]


def weighted(p, x_ref, lo_ref, hi_ref, src_ref, out_ref):
    hb = p.shape[0]
    targets = hb // HEADS
    rows = by_pair(split(p, 2), True, lo_ref, hi_ref, src_ref, targets)
    for pair in range(targets // 2):
        here = rows[pair * GROUP : (pair + 1) * GROUP]
        full = dot(here, x_ref[2 * pair * LANES : 2 * (pair + 1) * LANES, :], NN)
        part = add_terms(full, 2)
        for h in range(HEADS):
            to = h * targets + 2 * pair
            out_ref[to : to + 2, :] = part[2 * h : 2 * h + 2]
    return out_ref[...]


def matmul3(a, b, dims):
    n = a.shape[0]
    full = dot(jnp.concatenate(split(a, 3), axis=0), b, dims)
    return full[:n] + full[n : 2 * n] + full[2 * n :]


def by_head(rows, targets):
    return [rows[h * targets : (h + 1) * targets] for h in range(HEADS)]


def backward(gain_ref, wv_ref, pack_ref, q_ref, p_ref, x_ref, states, replicas, scratch):
    width = gain_ref.shape[1]
    head = width // HEADS
    targets = pack_ref.shape[0]
    hb = HEADS * targets
    gain = gain_ref[...]

    def stats(state):
        tops = jnp.concatenate([state[hb:, 0:1], state[hb:, 64:65]], axis=0)
        totals = jnp.concatenate([state[hb:, 32:33], state[hb:, 96:97]], axis=0)
        return tops, totals

    columns = [slice(h * head, (h + 1) * head) for h in range(HEADS)]
    parts = [stats(state) for state in states]
    top = functools.reduce(jnp.maximum, [m for m, _ in parts])
    fac = [jnp.exp(m - top) for m, _ in parts]
    inv = 1.0 / sum(f * l for f, (_, l) in zip(fac, parts))
    attended = sum(f * state[:hb, :] for f, state in zip(fac, states)) * inv
    share = fac[0] * inv
    agg = jnp.concatenate(
        [matmul3(a, wv_ref[:, c], NN) for a, c in zip(by_head(attended, targets), columns)], axis=1
    )
    summed = agg + pack_ref[:, :width]
    centered = summed - jnp.mean(summed, axis=1, keepdims=True)
    inv_std = lax.rsqrt(jnp.mean(centered * centered, axis=1, keepdims=True) + 1e-05)
    normed = centered * inv_std
    gn = pack_ref[:, width + 2 * LANES :] * (1.0 / math.sqrt(replicas)) * gain
    gsum = (
        gn
        - jnp.mean(gn, axis=1, keepdims=True)
        - normed * jnp.mean(gn * normed, axis=1, keepdims=True)
    ) * inv_std
    gv = jnp.concatenate([matmul3(gsum[:, c], wv_ref[:, c], NT) for c in columns], axis=0)
    rowdot = jnp.sum(gv * attended, axis=1, keepdims=True)
    *pair_refs, acc_ref, ga_ref = scratch
    rows = by_pair(split(gv, 3), False, *pair_refs, targets)
    for pair in range(targets // 2):
        here = rows[pair * GROUP : (pair + 1) * GROUP]
        part = add_terms(dot(here, x_ref[2 * pair * LANES : 2 * (pair + 1) * LANES, :], NT), 3)
        for h in range(HEADS):
            for t in range(2):
                to = h * targets + 2 * pair + t
                row = part[2 * h + t : 2 * h + t + 1, t * LANES : (t + 1) * LANES]
                ga_ref[to : to + 1, :] = row
    gs = p_ref[...] * share * (ga_ref[...] - rowdot)
    ks = weighted(gs, x_ref, *pair_refs, acc_ref) * (1.0 / math.sqrt(head))
    lefts, rights = [], []
    for k, c in zip(by_head(ks, targets), columns):
        k1, k2 = split(k, 2)
        q1, q2 = split(q_ref[:, c], 2)
        lefts.append(jnp.concatenate([k1, k1, k2], axis=0))
        rights.append(jnp.concatenate([q1, q2, q1], axis=0))
    return normed * gain, attended, gsum, lefts, rights


def other_grad_kernel(*refs, stores, replicas):
    gain_ref, wv_ref, pack_ref, q_ref, p_ref, x_ref = refs[:6]
    states, refs = refs[6 : 6 + stores], refs[6 + stores :]
    left_ref, right_ref, *scratch = refs
    *_, lefts, rights = backward(
        gain_ref, wv_ref, pack_ref, q_ref, p_ref, x_ref, states, replicas, scratch
    )
    left_ref[...] = jnp.concatenate(lefts, axis=1)
    right_ref[...] = jnp.concatenate(rights, axis=1)


def own_grad_kernel(*refs, stores, replicas, grid):
    gain_ref, wv_ref, pack_ref, q_ref, p_ref, x_ref = refs[:6]
    states, refs = refs[6 : 6 + stores], refs[6 + stores :]
    others, refs = refs[: 2 * (stores - 1)], refs[2 * (stores - 1) :]
    emb_ref, keep_ref, send_ref, grad_ref, *scratch = refs
    his, los = grid
    width = gain_ref.shape[1]
    head = width // HEADS
    kin = wv_ref.shape[0]
    targets = pack_ref.shape[0]
    embedded, attended, gsum, lefts, rights = backward(
        gain_ref, wv_ref, pack_ref, q_ref, p_ref, x_ref, states, replicas, scratch
    )
    emb_ref[...] = embedded.astype(bf16)
    for h in range(HEADS):
        cols = slice(h * head, (h + 1) * head)
        a1, a2 = split(by_head(attended, targets)[h], 2)
        g1, g2 = split(gsum[:, cols], 2)
        grad_ref[kin:, cols] = dot(
            jnp.concatenate([a1, a1, a2], axis=0), jnp.concatenate([g1, g2, g1], axis=0), TN
        )
        left = [lefts[h]] + [ref[:, h * kin : (h + 1) * kin] for ref in others[0::2]]
        right = [rights[h]] + [ref[:, cols] for ref in others[1::2]]
        grad_ref[:kin, cols] = dot(
            jnp.concatenate(left, axis=0), jnp.concatenate(right, axis=0), TN
        )
    rows = 2 * kin // replicas
    trainer, store = lax.axis_index("trainer"), lax.axis_index("store")
    hi, lo, core = trainer // (2 * los), trainer // 2 % los, trainer % 2
    for lr in range(los):
        for sr in range(stores):
            for hr in range(his):
                to = ((lr * stores + sr) * his + hr) * rows
                base = ((hi ^ hr) * los + (lo ^ lr)) * 2
                for ref, c in ((keep_ref, core), (send_ref, 1 - core)):
                    src = ((base + c) * stores + (store ^ sr)) * rows
                    src = pl.multiple_of(src, rows)
                    ref[to : to + rows, :] = grad_ref[pl.ds(src, rows), :]


def gru_kernel(*refs, stores, targets):
    pack_ref, rows_ref, turns_ref, gi_ref, gh_ref = refs[:5]
    states, out_ref = refs[5 : 5 + stores], refs[5 + stores]
    width = gh_ref.shape[0]
    hb = HEADS * targets
    latest = sum(state[hb:, LANES:] for state in states)
    elapsed = pack_ref[:, width + LANES : width + LANES + 1]
    encoded = cosine(elapsed * turns_ref[0:1, :] + turns_ref[1:2, :])
    inputs = jnp.concatenate([latest.astype(bf16), encoded.astype(bf16)], axis=1)
    mem_rows = pack_ref[:, :width]
    gi = dot(inputs, gi_ref[...], NN)
    gh = dot(mem_rows.astype(bf16), gh_ref[...], NN)
    update = jax.nn.sigmoid(gi[:, :width] + gh[:, :width])
    reset = jax.nn.sigmoid(gi[:, width : 2 * width] + gh[:, width : 2 * width])
    candidate = jnp.tanh(gi[:, 2 * width :] + reset * gh[:, 2 * width :])
    out_ref[:targets, :] = (1.0 - update) * candidate + update * mem_rows
    out_ref[targets:, :] = jnp.zeros((8, width), f32)
    out_ref[targets : targets + 1, :targets] = rows_ref[...].astype(f32)


def place_kernel(memory_ref, new_ref, out_ref, ids_ref, sids_ref, sem):
    targets = new_ref.shape[0] - 8
    ids_ref[...] = new_ref[targets:, :LANES].astype(jnp.int32)
    copy = pltpu.make_async_copy(ids_ref, sids_ref, sem)
    copy.start()
    out_ref[...] = memory_ref[...]
    copy.wait()
    for b in range(targets):
        out_ref[pl.ds(sids_ref[0, b], 1), :] = new_ref[b : b + 1, :]


def sum_split_kernel(*refs, count, outs):
    total = refs[0][...]
    for ref in refs[1:count]:
        total = total + ref[...].astype(f32)
    size = total.shape[0] // outs
    for i, ref in enumerate(refs[count:]):
        ref[...] = total[i * size : (i + 1) * size].astype(ref.dtype)


def last_sum_kernel(*refs):
    total = refs[0][...]
    for ref in refs[1:-1]:
        total = total + ref[...].astype(f32)
    out_ref = refs[-1]
    rows, width = total.shape
    per = width // LANES
    for j in range(per):
        out_ref[pl.ds(j, rows, stride=per), :] = total[:, j * LANES : (j + 1) * LANES]


def call(kernel, ins, outs, scratch=(), specs=None, name=None):
    return pl.pallas_call(
        kernel,
        in_specs=specs or [VM] * len(ins),
        out_specs=[VM] * len(outs),
        out_shape=outs,
        scratch_shapes=list(scratch),
        compiler_params=PARAMS,
        name=name,
    )(*ins)


def near(x):
    return pltpu.with_memory_space_constraint(x, pltpu.VMEM)


def far(x):
    return pltpu.with_memory_space_constraint(x, pltpu.HBM)


def shape(*dims, dtype=f32):
    return pltpu.VMEM(dims, dtype)


def out_shape(*dims, dtype=f32):
    return jax.ShapeDtypeStruct(dims, dtype)


def on_device(
    memory,
    event_feats,
    batch_rows,
    target_time,
    neighbor_owner,
    neighbor_event,
    neighbor_time,
    time_freq,
    time_phase,
    w_query,
    w_key,
    w_value,
    ln_gain,
    gru_input,
    gru_hidden,
    emb_cotangent,
):
    trainers, stores = lax.axis_size("trainer"), lax.axis_size("store")
    replicas = trainers * stores
    targets, neighbors = neighbor_event.shape[1:]
    held, feat = event_feats.shape
    width = memory.shape[1]
    kin = w_key.shape[0]
    hb = HEADS * targets
    los = 2
    his = trainers // (2 * los)
    sources = [
        batch_rows,
        memory,
        neighbor_owner[0, :, :, 0],
        neighbor_event[0],
        neighbor_time[0],
        target_time,
        emb_cotangent[0],
        time_freq[None],
        time_phase[None],
        w_query,
        w_key,
    ]
    pack, turns, wq_near, wk_near = call(
        functools.partial(pack_kernel, held=held),
        [far(x) for x in sources],
        [
            shape(targets, 2 * width + 2 * LANES),
            shape(8, LANES),
            shape(*w_query.shape, dtype=bf16),
            shape(*w_key.shape, dtype=bf16),
        ],
        scratch=[pltpu.SMEM(batch_rows.shape, jnp.int32)]
        + [pltpu.VMEM(x.shape, x.dtype) for x in sources[1:9]]
        + [pltpu.SemaphoreType.DMA((len(sources),))],
        specs=[FAR] * len(sources),
        name="pack",
    )

    def from_store(value, d):
        return lax.ppermute(value, "store", [((i + d) % stores, i) for i in range(stores)])

    packs = [pack] + [from_store(pack, d) for d in range(1, stores)]
    table = far(event_feats)
    chunks = 4
    pair_scratch = [
        pltpu.VMEM((GROUP * targets // 2, LANES), f32),
        pltpu.VMEM((GROUP * targets // 2, LANES), f32),
        pltpu.VMEM((6 * hb, LANES), f32),
        pltpu.VMEM((hb, kin), f32),
    ]
    local, weights, queries, inputs = [], [], [], []
    for d in range(stores):
        state, p, q, x = call(
            functools.partial(attend_kernel, neighbors=neighbors),
            [
                near(packs[d]),
                table,
                near(turns),
                near(wq_near),
                near(wk_near),
            ],
            [
                shape(hb + targets, kin),
                shape(hb, LANES),
                shape(targets, width),
                shape(targets * LANES, kin, dtype=bf16),
            ],
            scratch=[
                pltpu.VMEM((held, feat), bf16),
                pltpu.VMEM((held, feat), f32),
                pltpu.VMEM((targets, LANES), jnp.int32),
                pltpu.SMEM((targets, LANES), jnp.int32),
                pltpu.VMEM((2 * LANES, feat), f32),
                pltpu.VMEM((GROUP * targets // 2, kin), bf16),
                pltpu.VMEM((hb, LANES), f32),
                pltpu.VMEM((targets, LANES), f32),
                pltpu.VMEM((targets, LANES), f32),
                pltpu.VMEM((targets * LANES, LANES), f32),
                *pair_scratch,
                pltpu.SemaphoreType.DMA((chunks,)),
                pltpu.SemaphoreType.DMA,
            ],
            specs=[VM, FAR] + [VM] * 3,
            name="attend",
        )
        local.append(state)
        weights.append(p)
        queries.append(q)
        inputs.append(x)
    gathered = [local] + [[from_store(state, e) for state in local] for e in range(1, stores)]
    states = [[gathered[e][(d - e) % stores] for e in range(stores)] for d in range(stores)]

    def set_of(d):
        return [near(x) for x in (packs[d], queries[d], weights[d], inputs[d], *states[d])]

    gain = ln_gain[None]
    others = []
    for d in range(1, stores):
        ins = [gain, w_value, *set_of(d)]
        others += call(
            functools.partial(other_grad_kernel, stores=stores, replicas=replicas),
            ins,
            [
                shape(3 * targets, HEADS * kin, dtype=bf16),
                shape(3 * targets, width, dtype=bf16),
            ],
            scratch=[*pair_scratch, pltpu.VMEM((hb, LANES), f32)],
            name="other_grads",
        )
    ins = [gain, w_value, *set_of(0), *map(near, others)]
    emb, keep, send = call(
        functools.partial(own_grad_kernel, stores=stores, replicas=replicas, grid=(his, los)),
        ins,
        [out_shape(targets, width, dtype=bf16), shape(kin, width), shape(kin, width)],
        scratch=[pltpu.VMEM((2 * kin, width), f32), *pair_scratch, pltpu.VMEM((hb, LANES), f32)],
        name="own_grads",
    )

    (news,) = call(
        functools.partial(gru_kernel, stores=stores, targets=targets),
        [near(pack), batch_rows, near(turns), gru_input, gru_hidden, *map(near, states[0])],
        [shape(targets + 8, width)],
        name="gru",
    )

    def exchange(value, hr, lr, cr, sr):
        def other(i):
            t, s = i // stores, i % stores
            t = ((t // (2 * los)) ^ hr) * 2 * los + (((t // 2) % los) ^ lr) * 2 + ((t % 2) ^ cr)
            return t * stores + (s ^ sr)

        return lax.ppermute(value, AXES, [(i, other(i)) for i in range(replicas)])

    swapped = exchange(send, 0, 0, 1, 0)
    members = los * stores
    out = call(
        functools.partial(sum_split_kernel, count=2, outs=members),
        [near(keep), near(swapped)],
        [shape(kin // members, width)]
        + [shape(kin // members, width, dtype=bf16)] * (members - 1),
        name="core_sum",
    )
    got = [exchange(out[j], 0, j // stores, 0, j % stores) for j in reversed(range(1, members))]
    out = call(
        functools.partial(sum_split_kernel, count=members, outs=his),
        [*map(near, [out[0], *got])],
        [shape(kin // members // his, width)] * his,
        name="plane_sum",
    )
    got = [exchange(out[j], j, 0, 0, 0) for j in reversed(range(1, his))]
    (share,) = call(
        last_sum_kernel,
        [*map(near, [out[0], *got])],
        [out_shape(2 * kin * width // replicas // LANES, LANES)],
        name="last_sum",
    )
    moved = lax.ppermute(news, "trainer", [(i, (i + 1) % trainers) for i in range(trainers)])
    (memory_next,) = call(
        place_kernel,
        [memory, near(moved)],
        [out_shape(*memory.shape)],
        scratch=[
            pltpu.VMEM((8, LANES), jnp.int32),
            pltpu.SMEM((8, LANES), jnp.int32),
            pltpu.SemaphoreType.DMA,
        ],
        name="place",
    )
    return (emb[None], memory_next[None], share.reshape(-1))


def solution(mesh):
    placed = (
        P("store", None),
        P("store", None),
        P("trainer", "store"),
        P("trainer", "store"),
        P("trainer", "store", None, None),
        P("trainer", "store", None),
        P("trainer", "store", None),
        P(),
        P(),
        P(),
        P(),
        P(),
        P(),
        P(),
        P(),
        P("trainer", "store", None),
    )
    return jax.shard_map(
        on_device,
        mesh=mesh,
        in_specs=placed,
        out_specs=(
            P("trainer", "store", None),
            P("trainer", "store", None),
            P(("trainer", "store")),
        ),
        check_vma=False,
    )
```

```python
import functools
import math

import jax
import jax.numpy as jnp
from jax import lax
from jax.experimental import pallas as pl
from jax.experimental.pallas import tpu as pltpu
from jax.sharding import PartitionSpec as P

HEADS = 2
LANES = 128
TOGETHER = 4
STRIP = 16
GROUP = 16
TURN = 0.5 / math.pi
AXES = ("trainer", "store")

f32 = jnp.float32
bf16 = jnp.bfloat16
NT = (((1,), (1,)), ((), ()))
NN = (((1,), (0,)), ((), ()))
TN = (((0,), (0,)), ((), ()))
VM = pl.BlockSpec(memory_space=pltpu.VMEM)
FAR = pl.BlockSpec(memory_space=pltpu.HBM)
PARAMS = pltpu.CompilerParams(vmem_limit_bytes=20 * 1024 * 1024)


def dot(a, b, dims):
    return lax.dot_general(a, b, dims, preferred_element_type=f32)


def split(x, parts):
    terms = []
    for _ in range(parts):
        term = x.astype(bf16)
        terms.append(term)
        x = x - term.astype(f32)
    return terms


SERIES = (-39.53670604797494, 76.5497822911237, -81.60100407314816, 41.341655031414376, -6.283185160089465)


def cosine(turns):
    part = turns - jnp.floor(turns)
    g = 0.25 - jnp.abs(part - 0.5)
    u = g * g
    c = f32(SERIES[0])
    for k in SERIES[1:]:
        c = c * u + f32(k)
    return c * g


def pack_kernel(*refs, held):
    sources, rest = refs[:11], refs[11:]
    out_ref, turns_ref, wq_out, wk_out = rest[:4]
    kept, sems = rest[4:13], rest[13]
    rows_ref, memory_ref, own_ref, event_ref, ntime_ref, ttime_ref, cot_ref, freq_ref, phase_ref = kept
    copies = [
        pltpu.make_async_copy(src, dst, sems.at[i])
        for i, (src, dst) in enumerate(zip(sources, (*kept, wq_out, wk_out)))
    ]
    for copy in copies:
        copy.start()
    for copy in copies[:-2]:
        copy.wait()
    turns_ref[0:1, :] = freq_ref[...] * TURN
    turns_ref[1:2, :] = phase_ref[...] * TURN
    turns_ref[2:, :] = jnp.zeros((turns_ref.shape[0] - 2, LANES), f32)
    targets, neighbors = event_ref.shape
    width = memory_ref.shape[1]
    ids = own_ref[...] * held + event_ref[...]
    out_ref[:, width : width + 2 * LANES] = jnp.full((targets, 2 * LANES), -1.0, f32)
    out_ref[:, width : width + neighbors] = ids.astype(f32)
    row = lax.broadcasted_iota(jnp.int32, (targets, targets), 0)
    lane = lax.broadcasted_iota(jnp.int32, (targets, targets), 1)
    times = jnp.sum(jnp.where(row == lane, ttime_ref[...].astype(f32), 0.0), axis=1, keepdims=True)
    elapsed = times - ntime_ref[...].astype(f32)
    out_ref[:, width + LANES : width + LANES + neighbors] = elapsed.astype(f32)
    out_ref[:, width + 2 * LANES :] = cot_ref[...].astype(f32)
    for b in range(targets):
        out_ref[pl.ds(b, 1), :width] = memory_ref[pl.ds(rows_ref[0, b], 1), :]
    for copy in copies[-2:]:
        copy.wait()


def attend_kernel(*refs, neighbors):
    pack_ref, table_ref, turns_ref, wq_ref, wk_ref = refs[:5]
    state_ref, p_ref, q_ref, x_ref = refs[5:9]
    tbf_ref, tab_ref, ids_ref, sids_ref, rows_ref, qk_ref, s_ref, when_ref, latest_ref = refs[9:18]
    column_ref, lo_ref, hi_ref, src_ref, acc_ref, tsem, isem = refs[18:]
    targets = pack_ref.shape[0]
    width = wq_ref.shape[0]
    kin = wk_ref.shape[0]
    feat = tab_ref.shape[1]
    head = width // HEADS
    hb = HEADS * targets
    held = tab_ref.shape[0]
    chunks = tsem.shape[0]
    step = held // chunks
    copies = [
        pltpu.make_async_copy(
            table_ref.at[pl.ds(c * step, step)], tbf_ref.at[pl.ds(c * step, step)], tsem.at[c]
        )
        for c in range(chunks)
    ]
    for copy in copies:
        copy.start()
    ids = pack_ref[:, width : width + LANES].astype(jnp.int32) - lax.axis_index("store") * held
    valid = (ids >= 0) & (ids < held)
    lane = lax.broadcasted_iota(jnp.int32, ids.shape, 1)
    valid = valid & (lane < neighbors)
    ids_ref[...] = jnp.where(valid, ids, 0)
    id_copy = pltpu.make_async_copy(ids_ref, sids_ref, isem)
    id_copy.start()
    mem_low = pack_ref[:, :width].astype(bf16)
    query = dot(mem_low, wq_ref[...], NN)
    q_ref[...] = query
    scale = 1.0 / math.sqrt(head)
    qk = []
    for h in range(HEADS):
        cols = slice(h * head, (h + 1) * head)
        qk.append(matmul3(query[:, cols], wk_ref[:, cols], NT) * scale)
    qk = split(jnp.concatenate(qk, axis=0), 3)
    qk_ref[...] = by_pair(qk, False, lo_ref, hi_ref, src_ref, targets)
    when_ref[...] = pack_ref[:, width + LANES : width + 2 * LANES]

    def stand_up(b, _):
        elapsed = when_ref[pl.ds(b, 1), :]
        at = pl.multiple_of(b * LANES, LANES)
        column_ref[pl.ds(at, LANES), :] = jnp.broadcast_to(elapsed, (LANES, LANES)).T
        return 0

    lax.fori_loop(0, targets, stand_up, 0, unroll=8)
    id_copy.wait()
    block = math.gcd(step, 320)
    for c in range(chunks):
        copies[c].wait()

        def widen(i, _, c=c):
            at = pl.multiple_of(c * step + i * block, block)
            tab_ref[pl.ds(at, block), :] = tbf_ref[pl.ds(at, block), :].astype(f32)
            return 0

        lax.fori_loop(0, step // block, widen, 0)

    freq, phase = turns_ref[0:1, :], turns_ref[1:2, :]
    pairs = targets // 2
    both = 2 * LANES

    def start_of(pair):
        return pl.multiple_of(pair * both, both)

    freq, phase = turns_ref[0:1, :], turns_ref[1:2, :]
    pairs = targets // 2
    both = 2 * LANES

    def one_group(group, _):
        first = group * TOGETHER
        at = pl.multiple_of(first * LANES, TOGETHER * LANES)
        row_ids = [sids_ref.at[first + t] for t in range(TOGETHER)]
        todo = [(n, t) for n in range(neighbors) for t in range(TOGETHER)]
        strips = TOGETHER * LANES // STRIP
        for i in range(strips):
            here = pl.ds(at + i * STRIP, STRIP)
            x_ref[here, feat:] = cosine(column_ref[here, :] * freq + phase).astype(bf16)
            for n, t in todo[i * len(todo) // strips : (i + 1) * len(todo) // strips]:
                rows_ref[t * LANES + n : t * LANES + n + 1, :] = tab_ref[pl.ds(row_ids[t][n], 1), :]
        x_ref[pl.ds(at, TOGETHER * LANES), :feat] = rows_ref[...].astype(bf16)
        for t in range(TOGETHER):
            latest_ref[pl.ds(first + t, 1), :] = rows_ref[t * LANES : t * LANES + 1, :]
        return 0

    rows_ref[...] = jnp.zeros(rows_ref.shape, f32)
    lax.fori_loop(0, targets // TOGETHER, one_group, 0)
    for pair in range(pairs):
        rows = qk_ref[pair * GROUP : (pair + 1) * GROUP, :]
        part = add_terms(dot(rows, x_ref[pair * both : (pair + 1) * both, :], NT), 3)
        for h in range(HEADS):
            for t in range(2):
                to = h * targets + 2 * pair + t
                row = part[2 * h + t : 2 * h + t + 1, t * LANES : (t + 1) * LANES]
                s_ref[to : to + 1, :] = row
    valid2 = jnp.concatenate([valid] * HEADS, axis=0)
    s = s_ref[...]
    top = jnp.max(jnp.where(valid2, s, -1e30), axis=1, keepdims=True)
    p = jnp.where(valid2, jnp.exp(s - top), 0.0)
    p_ref[...] = p
    total = jnp.sum(p, axis=1, keepdims=True)
    state_ref[:hb, :] = weighted(p, x_ref, lo_ref, hi_ref, src_ref, acc_ref)
    lane = lax.broadcasted_iota(jnp.int32, (targets, LANES), 1)
    stat = total[targets:]
    for value, end in ((top[targets:], 96), (total[:targets], 64), (top[:targets], 32)):
        stat = jnp.where(lane < end, value, stat)
    state_ref[hb:, :LANES] = stat
    first = jnp.where(valid, 1.0, 0.0)[:, :1]
    state_ref[hb:, LANES:] = latest_ref[...] * first


def by_pair(terms, lanes, lo_ref, hi_ref, src_ref, targets):
    hb = HEADS * targets
    pairs = targets // 2
    lo_ref[...] = jnp.zeros(lo_ref.shape, f32)
    hi_ref[...] = jnp.zeros(hi_ref.shape, f32)
    for i, term in enumerate(terms):
        for j in range(term.shape[1] // LANES):
            base = (2 * i + j) * hb
            src_ref[base : base + hb, :] = term[:, j * LANES : (j + 1) * LANES].astype(f32)
            for h in range(HEADS):
                for t in range(2):
                    ref = (lo_ref, hi_ref)[t if lanes else j]
                    rows = pl.ds(2 * HEADS * i + 2 * h + t, pairs, stride=GROUP)
                    ref[rows, :] = src_ref[pl.ds(base + h * targets + t, pairs, stride=2), :]
    return jnp.concatenate([lo_ref[...], hi_ref[...]], axis=1).astype(bf16)


def add_terms(full, count):
    step = 2 * HEADS
    return sum(full[i * step : (i + 1) * step] for i in range(1, count)) + full[:step]


def weighted(p, x_ref, lo_ref, hi_ref, src_ref, out_ref):
    hb = p.shape[0]
    targets = hb // HEADS
    rows = by_pair(split(p, 2), True, lo_ref, hi_ref, src_ref, targets)
    for pair in range(targets // 2):
        here = rows[pair * GROUP : (pair + 1) * GROUP]
        full = dot(here, x_ref[2 * pair * LANES : 2 * (pair + 1) * LANES, :], NN)
        part = add_terms(full, 2)
        for h in range(HEADS):
            to = h * targets + 2 * pair
            out_ref[to : to + 2, :] = part[2 * h : 2 * h + 2]
    return out_ref[...]


def matmul3(a, b, dims):
    n = a.shape[0]
    full = dot(jnp.concatenate(split(a, 3), axis=0), b, dims)
    return full[:n] + full[n : 2 * n] + full[2 * n :]


def by_head(rows, targets):
    return [rows[h * targets : (h + 1) * targets] for h in range(HEADS)]


def backward(gain_ref, wv_ref, pack_ref, q_ref, p_ref, x_ref, states, replicas, scratch):
    width = gain_ref.shape[1]
    head = width // HEADS
    targets = pack_ref.shape[0]
    hb = HEADS * targets
    gain = gain_ref[...]

    def stats(state):
        tops = jnp.concatenate([state[hb:, 0:1], state[hb:, 64:65]], axis=0)
        totals = jnp.concatenate([state[hb:, 32:33], state[hb:, 96:97]], axis=0)
        return tops, totals

    columns = [slice(h * head, (h + 1) * head) for h in range(HEADS)]
    parts = [stats(state) for state in states]
    top = functools.reduce(jnp.maximum, [m for m, _ in parts])
    fac = [jnp.exp(m - top) for m, _ in parts]
    inv = 1.0 / sum(f * l for f, (_, l) in zip(fac, parts))
    attended = sum(f * state[:hb, :] for f, state in zip(fac, states)) * inv
    share = fac[0] * inv
    agg = jnp.concatenate(
        [matmul3(a, wv_ref[:, c], NN) for a, c in zip(by_head(attended, targets), columns)], axis=1
    )
    summed = agg + pack_ref[:, :width]
    centered = summed - jnp.mean(summed, axis=1, keepdims=True)
    inv_std = lax.rsqrt(jnp.mean(centered * centered, axis=1, keepdims=True) + 1e-05)
    normed = centered * inv_std
    gn = pack_ref[:, width + 2 * LANES :] * (1.0 / math.sqrt(replicas)) * gain
    gsum = (
        gn
        - jnp.mean(gn, axis=1, keepdims=True)
        - normed * jnp.mean(gn * normed, axis=1, keepdims=True)
    ) * inv_std
    gv = jnp.concatenate([matmul3(gsum[:, c], wv_ref[:, c], NT) for c in columns], axis=0)
    rowdot = jnp.sum(gv * attended, axis=1, keepdims=True)
    *pair_refs, acc_ref, ga_ref = scratch
    rows = by_pair(split(gv, 3), False, *pair_refs, targets)
    for pair in range(targets // 2):
        here = rows[pair * GROUP : (pair + 1) * GROUP]
        part = add_terms(dot(here, x_ref[2 * pair * LANES : 2 * (pair + 1) * LANES, :], NT), 3)
        for h in range(HEADS):
            for t in range(2):
                to = h * targets + 2 * pair + t
                row = part[2 * h + t : 2 * h + t + 1, t * LANES : (t + 1) * LANES]
                ga_ref[to : to + 1, :] = row
    gs = p_ref[...] * share * (ga_ref[...] - rowdot)
    ks = weighted(gs, x_ref, *pair_refs, acc_ref) * (1.0 / math.sqrt(head))
    lefts, rights = [], []
    for k, c in zip(by_head(ks, targets), columns):
        k1, k2 = split(k, 2)
        q1, q2 = split(q_ref[:, c], 2)
        lefts.append(jnp.concatenate([k1, k1, k2], axis=0))
        rights.append(jnp.concatenate([q1, q2, q1], axis=0))
    return normed * gain, attended, gsum, lefts, rights


def other_grad_kernel(*refs, stores, replicas):
    gain_ref, wv_ref, pack_ref, q_ref, p_ref, x_ref = refs[:6]
    states, refs = refs[6 : 6 + stores], refs[6 + stores :]
    left_ref, right_ref, *scratch = refs
    *_, lefts, rights = backward(
        gain_ref, wv_ref, pack_ref, q_ref, p_ref, x_ref, states, replicas, scratch
    )
    left_ref[...] = jnp.concatenate(lefts, axis=1)
    right_ref[...] = jnp.concatenate(rights, axis=1)


def own_grad_kernel(*refs, stores, replicas, grid):
    gain_ref, wv_ref, pack_ref, q_ref, p_ref, x_ref = refs[:6]
    states, refs = refs[6 : 6 + stores], refs[6 + stores :]
    others, refs = refs[: 2 * (stores - 1)], refs[2 * (stores - 1) :]
    emb_ref, keep_ref, send_ref, grad_ref, *scratch = refs
    his, los = grid
    width = gain_ref.shape[1]
    head = width // HEADS
    kin = wv_ref.shape[0]
    targets = pack_ref.shape[0]
    embedded, attended, gsum, lefts, rights = backward(
        gain_ref, wv_ref, pack_ref, q_ref, p_ref, x_ref, states, replicas, scratch
    )
    emb_ref[...] = embedded.astype(bf16)
    for h in range(HEADS):
        cols = slice(h * head, (h + 1) * head)
        a1, a2 = split(by_head(attended, targets)[h], 2)
        g1, g2 = split(gsum[:, cols], 2)
        grad_ref[kin:, cols] = dot(
            jnp.concatenate([a1, a1, a2], axis=0), jnp.concatenate([g1, g2, g1], axis=0), TN
        )
        left = [lefts[h]] + [ref[:, h * kin : (h + 1) * kin] for ref in others[0::2]]
        right = [rights[h]] + [ref[:, cols] for ref in others[1::2]]
        grad_ref[:kin, cols] = dot(
            jnp.concatenate(left, axis=0), jnp.concatenate(right, axis=0), TN
        )
    rows = 2 * kin // replicas
    trainer, store = lax.axis_index("trainer"), lax.axis_index("store")
    hi, lo, core = trainer // (2 * los), trainer // 2 % los, trainer % 2
    for lr in range(los):
        for sr in range(stores):
            for hr in range(his):
                to = ((lr * stores + sr) * his + hr) * rows
                base = ((hi ^ hr) * los + (lo ^ lr)) * 2
                for ref, c in ((keep_ref, core), (send_ref, 1 - core)):
                    src = ((base + c) * stores + (store ^ sr)) * rows
                    src = pl.multiple_of(src, rows)
                    ref[to : to + rows, :] = grad_ref[pl.ds(src, rows), :]


def gru_kernel(*refs, stores, targets):
    pack_ref, rows_ref, turns_ref, gi_ref, gh_ref = refs[:5]
    states, out_ref = refs[5 : 5 + stores], refs[5 + stores]
    width = gh_ref.shape[0]
    hb = HEADS * targets
    latest = sum(state[hb:, LANES:] for state in states)
    elapsed = pack_ref[:, width + LANES : width + LANES + 1]
    encoded = cosine(elapsed * turns_ref[0:1, :] + turns_ref[1:2, :])
    inputs = jnp.concatenate([latest.astype(bf16), encoded.astype(bf16)], axis=1)
    mem_rows = pack_ref[:, :width]
    gi = dot(inputs, gi_ref[...], NN)
    gh = dot(mem_rows.astype(bf16), gh_ref[...], NN)
    update = jax.nn.sigmoid(gi[:, :width] + gh[:, :width])
    reset = jax.nn.sigmoid(gi[:, width : 2 * width] + gh[:, width : 2 * width])
    candidate = jnp.tanh(gi[:, 2 * width :] + reset * gh[:, 2 * width :])
    out_ref[:targets, :] = (1.0 - update) * candidate + update * mem_rows
    out_ref[targets:, :] = jnp.zeros((8, width), f32)
    out_ref[targets : targets + 1, :targets] = rows_ref[...].astype(f32)


def place_kernel(memory_ref, new_ref, out_ref, ids_ref, sids_ref, sem):
    targets = new_ref.shape[0] - 8
    ids_ref[...] = new_ref[targets:, :LANES].astype(jnp.int32)
    copy = pltpu.make_async_copy(ids_ref, sids_ref, sem)
    copy.start()
    out_ref[...] = memory_ref[...]
    copy.wait()
    for b in range(targets):
        out_ref[pl.ds(sids_ref[0, b], 1), :] = new_ref[b : b + 1, :]


def sum_split_kernel(*refs, count, outs):
    total = refs[0][...]
    for ref in refs[1:count]:
        total = total + ref[...].astype(f32)
    size = total.shape[0] // outs
    for i, ref in enumerate(refs[count:]):
        ref[...] = total[i * size : (i + 1) * size].astype(ref.dtype)


def last_sum_kernel(*refs):
    total = refs[0][...]
    for ref in refs[1:-1]:
        total = total + ref[...].astype(f32)
    out_ref = refs[-1]
    rows, width = total.shape
    per = width // LANES
    for j in range(per):
        out_ref[pl.ds(j, rows, stride=per), :] = total[:, j * LANES : (j + 1) * LANES]


def call(kernel, ins, outs, scratch=(), specs=None, name=None):
    return pl.pallas_call(
        kernel,
        in_specs=specs or [VM] * len(ins),
        out_specs=[VM] * len(outs),
        out_shape=outs,
        scratch_shapes=list(scratch),
        compiler_params=PARAMS,
        name=name,
    )(*ins)


def near(x):
    return pltpu.with_memory_space_constraint(x, pltpu.VMEM)


def far(x):
    return pltpu.with_memory_space_constraint(x, pltpu.HBM)


def shape(*dims, dtype=f32):
    return pltpu.VMEM(dims, dtype)


def out_shape(*dims, dtype=f32):
    return jax.ShapeDtypeStruct(dims, dtype)


def on_device(
    memory,
    event_feats,
    batch_rows,
    target_time,
    neighbor_owner,
    neighbor_event,
    neighbor_time,
    time_freq,
    time_phase,
    w_query,
    w_key,
    w_value,
    ln_gain,
    gru_input,
    gru_hidden,
    emb_cotangent,
):
    trainers, stores = lax.axis_size("trainer"), lax.axis_size("store")
    replicas = trainers * stores
    targets, neighbors = neighbor_event.shape[1:]
    held, feat = event_feats.shape
    width = memory.shape[1]
    kin = w_key.shape[0]
    hb = HEADS * targets
    los = 2
    his = trainers // (2 * los)
    sources = [
        batch_rows,
        memory,
        neighbor_owner[0, :, :, 0],
        neighbor_event[0],
        neighbor_time[0],
        target_time,
        emb_cotangent[0],
        time_freq[None],
        time_phase[None],
        w_query,
        w_key,
    ]
    pack, turns, wq_near, wk_near = call(
        functools.partial(pack_kernel, held=held),
        [far(x) for x in sources],
        [
            shape(targets, 2 * width + 2 * LANES),
            shape(8, LANES),
            shape(*w_query.shape, dtype=bf16),
            shape(*w_key.shape, dtype=bf16),
        ],
        scratch=[pltpu.SMEM(batch_rows.shape, jnp.int32)]
        + [pltpu.VMEM(x.shape, x.dtype) for x in sources[1:9]]
        + [pltpu.SemaphoreType.DMA((len(sources),))],
        specs=[FAR] * len(sources),
        name="pack",
    )

    def from_store(value, d):
        return lax.ppermute(value, "store", [((i + d) % stores, i) for i in range(stores)])

    packs = [pack] + [from_store(pack, d) for d in range(1, stores)]
    table = far(event_feats)
    chunks = 8
    pair_scratch = [
        pltpu.VMEM((GROUP * targets // 2, LANES), f32),
        pltpu.VMEM((GROUP * targets // 2, LANES), f32),
        pltpu.VMEM((6 * hb, LANES), f32),
        pltpu.VMEM((hb, kin), f32),
    ]
    local, weights, queries, inputs = [], [], [], []
    for d in range(stores):
        state, p, q, x = call(
            functools.partial(attend_kernel, neighbors=neighbors),
            [
                near(packs[d]),
                table,
                near(turns),
                near(wq_near),
                near(wk_near),
            ],
            [
                shape(hb + targets, kin),
                shape(hb, LANES),
                shape(targets, width),
                shape(targets * LANES, kin, dtype=bf16),
            ],
            scratch=[
                pltpu.VMEM((held, feat), bf16),
                pltpu.VMEM((held, feat), f32),
                pltpu.VMEM((targets, LANES), jnp.int32),
                pltpu.SMEM((targets, LANES), jnp.int32),
                pltpu.VMEM((TOGETHER * LANES, feat), f32),
                pltpu.VMEM((GROUP * targets // 2, kin), bf16),
                pltpu.VMEM((hb, LANES), f32),
                pltpu.VMEM((targets, LANES), f32),
                pltpu.VMEM((targets, LANES), f32),
                pltpu.VMEM((targets * LANES, LANES), f32),
                *pair_scratch,
                pltpu.SemaphoreType.DMA((chunks,)),
                pltpu.SemaphoreType.DMA,
            ],
            specs=[VM, FAR] + [VM] * 3,
            name="attend",
        )
        local.append(state)
        weights.append(p)
        queries.append(q)
        inputs.append(x)
    gathered = [local] + [[from_store(state, e) for state in local] for e in range(1, stores)]
    states = [[gathered[e][(d - e) % stores] for e in range(stores)] for d in range(stores)]

    def set_of(d):
        return [near(x) for x in (packs[d], queries[d], weights[d], inputs[d], *states[d])]

    gain = ln_gain[None]
    others = []
    for d in range(1, stores):
        ins = [gain, w_value, *set_of(d)]
        others += call(
            functools.partial(other_grad_kernel, stores=stores, replicas=replicas),
            ins,
            [
                shape(3 * targets, HEADS * kin, dtype=bf16),
                shape(3 * targets, width, dtype=bf16),
            ],
            scratch=[*pair_scratch, pltpu.VMEM((hb, LANES), f32)],
            name="other_grads",
        )
    ins = [gain, w_value, *set_of(0), *map(near, others)]
    emb, keep, send = call(
        functools.partial(own_grad_kernel, stores=stores, replicas=replicas, grid=(his, los)),
        ins,
        [out_shape(targets, width, dtype=bf16), shape(kin, width), shape(kin, width)],
        scratch=[pltpu.VMEM((2 * kin, width), f32), *pair_scratch, pltpu.VMEM((hb, LANES), f32)],
        name="own_grads",
    )

    (news,) = call(
        functools.partial(gru_kernel, stores=stores, targets=targets),
        [near(pack), batch_rows, near(turns), gru_input, gru_hidden, *map(near, states[0])],
        [shape(targets + 8, width)],
        name="gru",
    )

    def exchange(value, hr, lr, cr, sr):
        def other(i):
            t, s = i // stores, i % stores
            t = ((t // (2 * los)) ^ hr) * 2 * los + (((t // 2) % los) ^ lr) * 2 + ((t % 2) ^ cr)
            return t * stores + (s ^ sr)

        return lax.ppermute(value, AXES, [(i, other(i)) for i in range(replicas)])

    swapped = exchange(send, 0, 0, 1, 0)
    members = los * stores
    out = call(
        functools.partial(sum_split_kernel, count=2, outs=members),
        [near(keep), near(swapped)],
        [shape(kin // members, width)]
        + [shape(kin // members, width, dtype=bf16)] * (members - 1),
        name="core_sum",
    )
    got = [exchange(out[j], 0, j // stores, 0, j % stores) for j in reversed(range(1, members))]
    out = call(
        functools.partial(sum_split_kernel, count=members, outs=his),
        [*map(near, [out[0], *got])],
        [shape(kin // members // his, width)] * his,
        name="plane_sum",
    )
    got = [exchange(out[j], j, 0, 0, 0) for j in reversed(range(1, his))]
    (share,) = call(
        last_sum_kernel,
        [*map(near, [out[0], *got])],
        [out_shape(2 * kin * width // replicas // LANES, LANES)],
        name="last_sum",
    )
    moved = lax.ppermute(news, "trainer", [(i, (i + 1) % trainers) for i in range(trainers)])
    (memory_next,) = call(
        place_kernel,
        [memory, near(moved)],
        [out_shape(*memory.shape)],
        scratch=[
            pltpu.VMEM((8, LANES), jnp.int32),
            pltpu.SMEM((8, LANES), jnp.int32),
            pltpu.SemaphoreType.DMA,
        ],
        name="place",
    )
    return (emb[None], memory_next[None], share.reshape(-1))


def solution(mesh):
    placed = (
        P("store", None),
        P("store", None),
        P("trainer", "store"),
        P("trainer", "store"),
        P("trainer", "store", None, None),
        P("trainer", "store", None),
        P("trainer", "store", None),
        P(),
        P(),
        P(),
        P(),
        P(),
        P(),
        P(),
        P(),
        P("trainer", "store", None),
    )
    return jax.shard_map(
        on_device,
        mesh=mesh,
        in_specs=placed,
        out_specs=(
            P("trainer", "store", None),
            P("trainer", "store", None),
            P(("trainer", "store")),
        ),
        check_vma=False,
    )
```

```python
import functools
import math

import jax
import jax.numpy as jnp
from jax import lax
from jax.experimental import pallas as pl
from jax.experimental.pallas import tpu as pltpu
from jax.sharding import PartitionSpec as P

HEADS = 2
LANES = 128
TOGETHER = 4
STRIP = 16
GROUP = 16
TURN = 0.5 / math.pi
AXES = ("trainer", "store")

f32 = jnp.float32
bf16 = jnp.bfloat16
NT = (((1,), (1,)), ((), ()))
NN = (((1,), (0,)), ((), ()))
TN = (((0,), (0,)), ((), ()))
VM = pl.BlockSpec(memory_space=pltpu.VMEM)
FAR = pl.BlockSpec(memory_space=pltpu.HBM)
PARAMS = pltpu.CompilerParams(vmem_limit_bytes=20 * 1024 * 1024)


def dot(a, b, dims):
    return lax.dot_general(a, b, dims, preferred_element_type=f32)


def split(x, parts):
    terms = []
    for _ in range(parts):
        term = x.astype(bf16)
        terms.append(term)
        x = x - term.astype(f32)
    return terms


SERIES = (-39.53670604797494, 76.5497822911237, -81.60100407314816, 41.341655031414376, -6.283185160089465)


def cosine(turns):
    part = turns - jnp.floor(turns)
    g = 0.25 - jnp.abs(part - 0.5)
    u = g * g
    c = f32(SERIES[0])
    for k in SERIES[1:]:
        c = c * u + f32(k)
    return c * g


def pack_kernel(*refs, held):
    sources, rest = refs[:11], refs[11:]
    out_ref, turns_ref, wq_out, wk_out = rest[:4]
    kept, sems = rest[4:13], rest[13]
    rows_ref, memory_ref, own_ref, event_ref, ntime_ref, ttime_ref, cot_ref, freq_ref, phase_ref = kept
    copies = [
        pltpu.make_async_copy(src, dst, sems.at[i])
        for i, (src, dst) in enumerate(zip(sources, (*kept, wq_out, wk_out)))
    ]
    for copy in copies:
        copy.start()
    for copy in copies[:-2]:
        copy.wait()
    turns_ref[0:1, :] = freq_ref[...] * TURN
    turns_ref[1:2, :] = phase_ref[...] * TURN
    turns_ref[2:, :] = jnp.zeros((turns_ref.shape[0] - 2, LANES), f32)
    targets, neighbors = event_ref.shape
    width = memory_ref.shape[1]
    ids = own_ref[...] * held + event_ref[...]
    out_ref[:, width : width + 2 * LANES] = jnp.full((targets, 2 * LANES), -1.0, f32)
    out_ref[:, width : width + neighbors] = ids.astype(f32)
    row = lax.broadcasted_iota(jnp.int32, (targets, targets), 0)
    lane = lax.broadcasted_iota(jnp.int32, (targets, targets), 1)
    times = jnp.sum(jnp.where(row == lane, ttime_ref[...].astype(f32), 0.0), axis=1, keepdims=True)
    elapsed = times - ntime_ref[...].astype(f32)
    out_ref[:, width + LANES : width + LANES + neighbors] = elapsed.astype(f32)
    out_ref[:, width + 2 * LANES :] = cot_ref[...].astype(f32)
    for b in range(targets):
        out_ref[pl.ds(b, 1), :width] = memory_ref[pl.ds(rows_ref[0, b], 1), :]
    for copy in copies[-2:]:
        copy.wait()


def attend_kernel(*refs, neighbors):
    pack_ref, table_ref, turns_ref, wq_ref, wk_ref = refs[:5]
    state_ref, p_ref, q_ref, x_ref = refs[5:9]
    tbf_ref, tab_ref, ids_ref, sids_ref, rows_ref, qk_ref, s_ref, when_ref, latest_ref = refs[9:18]
    column_ref, lo_ref, hi_ref, src_ref, acc_ref, tsem, isem = refs[18:]
    targets = pack_ref.shape[0]
    width = wq_ref.shape[0]
    kin = wk_ref.shape[0]
    feat = tab_ref.shape[1]
    head = width // HEADS
    hb = HEADS * targets
    held = tab_ref.shape[0]
    chunks = tsem.shape[0]
    step = held // chunks
    copies = [
        pltpu.make_async_copy(
            table_ref.at[pl.ds(c * step, step)], tbf_ref.at[pl.ds(c * step, step)], tsem.at[c]
        )
        for c in range(chunks)
    ]
    for copy in copies:
        copy.start()
    ids = pack_ref[:, width : width + LANES].astype(jnp.int32) - lax.axis_index("store") * held
    valid = (ids >= 0) & (ids < held)
    lane = lax.broadcasted_iota(jnp.int32, ids.shape, 1)
    valid = valid & (lane < neighbors)
    ids_ref[...] = jnp.where(valid, ids, 0)
    id_copy = pltpu.make_async_copy(ids_ref, sids_ref, isem)
    id_copy.start()
    when_ref[...] = pack_ref[:, width + LANES : width + 2 * LANES]
    def stand_up(b, _):
        elapsed = when_ref[pl.ds(b, 1), :]
        at = pl.multiple_of(b * LANES, LANES)
        column_ref[pl.ds(at, LANES), :] = jnp.broadcast_to(elapsed, (LANES, LANES)).T
        return 0

    lax.fori_loop(0, targets, stand_up, 0, unroll=8)
    mem_low = pack_ref[:, :width].astype(bf16)
    query = dot(mem_low, wq_ref[...], NN)
    q_ref[...] = query
    scale = 1.0 / math.sqrt(head)
    qk = []
    for h in range(HEADS):
        cols = slice(h * head, (h + 1) * head)
        qk.append(matmul3(query[:, cols], wk_ref[:, cols], NT) * scale)
    qk = split(jnp.concatenate(qk, axis=0), 3)
    qk_ref[...] = by_pair(qk, False, lo_ref, hi_ref, src_ref, targets)

    id_copy.wait()
    block = math.gcd(step, 320)
    for c in range(chunks):
        copies[c].wait()

        def widen(i, _, c=c):
            at = pl.multiple_of(c * step + i * block, block)
            tab_ref[pl.ds(at, block), :] = tbf_ref[pl.ds(at, block), :].astype(f32)
            return 0

        lax.fori_loop(0, step // block, widen, 0)

    freq, phase = turns_ref[0:1, :], turns_ref[1:2, :]
    pairs = targets // 2
    both = 2 * LANES

    def start_of(pair):
        return pl.multiple_of(pair * both, both)

    freq, phase = turns_ref[0:1, :], turns_ref[1:2, :]
    pairs = targets // 2
    both = 2 * LANES

    def one_group(group, _):
        first = group * TOGETHER
        at = pl.multiple_of(first * LANES, TOGETHER * LANES)
        row_ids = [sids_ref.at[first + t] for t in range(TOGETHER)]
        todo = [(n, t) for n in range(neighbors) for t in range(TOGETHER)]
        strips = TOGETHER * LANES // STRIP
        for i in range(strips):
            here = pl.ds(at + i * STRIP, STRIP)
            x_ref[here, feat:] = cosine(column_ref[here, :] * freq + phase).astype(bf16)
            for n, t in todo[i * len(todo) // strips : (i + 1) * len(todo) // strips]:
                rows_ref[t * LANES + n : t * LANES + n + 1, :] = tab_ref[pl.ds(row_ids[t][n], 1), :]
        x_ref[pl.ds(at, TOGETHER * LANES), :feat] = rows_ref[...].astype(bf16)
        for t in range(TOGETHER):
            latest_ref[pl.ds(first + t, 1), :] = rows_ref[t * LANES : t * LANES + 1, :]
        return 0

    rows_ref[...] = jnp.zeros(rows_ref.shape, f32)
    lax.fori_loop(0, targets // TOGETHER, one_group, 0)
    for pair in range(pairs):
        rows = qk_ref[pair * GROUP : (pair + 1) * GROUP, :]
        part = add_terms(dot(rows, x_ref[pair * both : (pair + 1) * both, :], NT), 3)
        for h in range(HEADS):
            for t in range(2):
                to = h * targets + 2 * pair + t
                row = part[2 * h + t : 2 * h + t + 1, t * LANES : (t + 1) * LANES]
                s_ref[to : to + 1, :] = row
    valid2 = jnp.concatenate([valid] * HEADS, axis=0)
    s = s_ref[...]
    top = jnp.max(jnp.where(valid2, s, -1e30), axis=1, keepdims=True)
    p = jnp.where(valid2, jnp.exp(s - top), 0.0)
    p_ref[...] = p
    total = jnp.sum(p, axis=1, keepdims=True)
    state_ref[:hb, :] = weighted(p, x_ref, lo_ref, hi_ref, src_ref, acc_ref)
    lane = lax.broadcasted_iota(jnp.int32, (targets, LANES), 1)
    stat = total[targets:]
    for value, end in ((top[targets:], 96), (total[:targets], 64), (top[:targets], 32)):
        stat = jnp.where(lane < end, value, stat)
    state_ref[hb:, :LANES] = stat
    first = jnp.where(valid, 1.0, 0.0)[:, :1]
    state_ref[hb:, LANES:] = latest_ref[...] * first


def by_pair(terms, lanes, lo_ref, hi_ref, src_ref, targets):
    hb = HEADS * targets
    pairs = targets // 2
    lo_ref[...] = jnp.zeros(lo_ref.shape, f32)
    hi_ref[...] = jnp.zeros(hi_ref.shape, f32)
    for i, term in enumerate(terms):
        for j in range(term.shape[1] // LANES):
            base = (2 * i + j) * hb
            src_ref[base : base + hb, :] = term[:, j * LANES : (j + 1) * LANES].astype(f32)
            for h in range(HEADS):
                for t in range(2):
                    ref = (lo_ref, hi_ref)[t if lanes else j]
                    rows = pl.ds(2 * HEADS * i + 2 * h + t, pairs, stride=GROUP)
                    ref[rows, :] = src_ref[pl.ds(base + h * targets + t, pairs, stride=2), :]
    return jnp.concatenate([lo_ref[...], hi_ref[...]], axis=1).astype(bf16)


def add_terms(full, count):
    step = 2 * HEADS
    return sum(full[i * step : (i + 1) * step] for i in range(1, count)) + full[:step]


def weighted(p, x_ref, lo_ref, hi_ref, src_ref, out_ref):
    hb = p.shape[0]
    targets = hb // HEADS
    rows = by_pair(split(p, 2), True, lo_ref, hi_ref, src_ref, targets)
    for pair in range(targets // 2):
        here = rows[pair * GROUP : (pair + 1) * GROUP]
        full = dot(here, x_ref[2 * pair * LANES : 2 * (pair + 1) * LANES, :], NN)
        part = add_terms(full, 2)
        for h in range(HEADS):
            to = h * targets + 2 * pair
            out_ref[to : to + 2, :] = part[2 * h : 2 * h + 2]
    return out_ref[...]


def matmul3(a, b, dims):
    n = a.shape[0]
    full = dot(jnp.concatenate(split(a, 3), axis=0), b, dims)
    return full[:n] + full[n : 2 * n] + full[2 * n :]


def by_head(rows, targets):
    return [rows[h * targets : (h + 1) * targets] for h in range(HEADS)]


def backward(gain_ref, wv_ref, pack_ref, q_ref, p_ref, x_ref, states, replicas, scratch):
    width = gain_ref.shape[1]
    head = width // HEADS
    targets = pack_ref.shape[0]
    hb = HEADS * targets
    gain = gain_ref[...]

    def stats(state):
        tops = jnp.concatenate([state[hb:, 0:1], state[hb:, 64:65]], axis=0)
        totals = jnp.concatenate([state[hb:, 32:33], state[hb:, 96:97]], axis=0)
        return tops, totals

    columns = [slice(h * head, (h + 1) * head) for h in range(HEADS)]
    parts = [stats(state) for state in states]
    top = functools.reduce(jnp.maximum, [m for m, _ in parts])
    fac = [jnp.exp(m - top) for m, _ in parts]
    inv = 1.0 / sum(f * l for f, (_, l) in zip(fac, parts))
    attended = sum(f * state[:hb, :] for f, state in zip(fac, states)) * inv
    share = fac[0] * inv
    agg = jnp.concatenate(
        [matmul3(a, wv_ref[:, c], NN) for a, c in zip(by_head(attended, targets), columns)], axis=1
    )
    summed = agg + pack_ref[:, :width]
    centered = summed - jnp.mean(summed, axis=1, keepdims=True)
    inv_std = lax.rsqrt(jnp.mean(centered * centered, axis=1, keepdims=True) + 1e-05)
    normed = centered * inv_std
    gn = pack_ref[:, width + 2 * LANES :] * (1.0 / math.sqrt(replicas)) * gain
    gsum = (
        gn
        - jnp.mean(gn, axis=1, keepdims=True)
        - normed * jnp.mean(gn * normed, axis=1, keepdims=True)
    ) * inv_std
    gv = jnp.concatenate([matmul3(gsum[:, c], wv_ref[:, c], NT) for c in columns], axis=0)
    rowdot = jnp.sum(gv * attended, axis=1, keepdims=True)
    *pair_refs, acc_ref, ga_ref = scratch
    rows = by_pair(split(gv, 3), False, *pair_refs, targets)
    for pair in range(targets // 2):
        here = rows[pair * GROUP : (pair + 1) * GROUP]
        part = add_terms(dot(here, x_ref[2 * pair * LANES : 2 * (pair + 1) * LANES, :], NT), 3)
        for h in range(HEADS):
            for t in range(2):
                to = h * targets + 2 * pair + t
                row = part[2 * h + t : 2 * h + t + 1, t * LANES : (t + 1) * LANES]
                ga_ref[to : to + 1, :] = row
    gs = p_ref[...] * share * (ga_ref[...] - rowdot)
    ks = weighted(gs, x_ref, *pair_refs, acc_ref) * (1.0 / math.sqrt(head))
    lefts, rights = [], []
    for k, c in zip(by_head(ks, targets), columns):
        k1, k2 = split(k, 2)
        q1, q2 = split(q_ref[:, c], 2)
        lefts.append(jnp.concatenate([k1, k1, k2], axis=0))
        rights.append(jnp.concatenate([q1, q2, q1], axis=0))
    return normed * gain, attended, gsum, lefts, rights


def other_grad_kernel(*refs, stores, replicas):
    gain_ref, wv_ref, pack_ref, q_ref, p_ref, x_ref = refs[:6]
    states, refs = refs[6 : 6 + stores], refs[6 + stores :]
    left_ref, right_ref, *scratch = refs
    *_, lefts, rights = backward(
        gain_ref, wv_ref, pack_ref, q_ref, p_ref, x_ref, states, replicas, scratch
    )
    left_ref[...] = jnp.concatenate(lefts, axis=1)
    right_ref[...] = jnp.concatenate(rights, axis=1)


def own_grad_kernel(*refs, stores, replicas, grid):
    gain_ref, wv_ref, pack_ref, q_ref, p_ref, x_ref = refs[:6]
    states, refs = refs[6 : 6 + stores], refs[6 + stores :]
    others, refs = refs[: 2 * (stores - 1)], refs[2 * (stores - 1) :]
    emb_ref, keep_ref, send_ref, grad_ref, *scratch = refs
    his, los = grid
    width = gain_ref.shape[1]
    head = width // HEADS
    kin = wv_ref.shape[0]
    targets = pack_ref.shape[0]
    embedded, attended, gsum, lefts, rights = backward(
        gain_ref, wv_ref, pack_ref, q_ref, p_ref, x_ref, states, replicas, scratch
    )
    emb_ref[...] = embedded.astype(bf16)
    for h in range(HEADS):
        cols = slice(h * head, (h + 1) * head)
        a1, a2 = split(by_head(attended, targets)[h], 2)
        g1, g2 = split(gsum[:, cols], 2)
        grad_ref[kin:, cols] = dot(
            jnp.concatenate([a1, a1, a2], axis=0), jnp.concatenate([g1, g2, g1], axis=0), TN
        )
        left = [lefts[h]] + [ref[:, h * kin : (h + 1) * kin] for ref in others[0::2]]
        right = [rights[h]] + [ref[:, cols] for ref in others[1::2]]
        grad_ref[:kin, cols] = dot(
            jnp.concatenate(left, axis=0), jnp.concatenate(right, axis=0), TN
        )
    rows = 2 * kin // replicas
    trainer, store = lax.axis_index("trainer"), lax.axis_index("store")
    hi, lo, core = trainer // (2 * los), trainer // 2 % los, trainer % 2
    for lr in range(los):
        for sr in range(stores):
            for hr in range(his):
                to = ((lr * stores + sr) * his + hr) * rows
                base = ((hi ^ hr) * los + (lo ^ lr)) * 2
                for ref, c in ((keep_ref, core), (send_ref, 1 - core)):
                    src = ((base + c) * stores + (store ^ sr)) * rows
                    src = pl.multiple_of(src, rows)
                    ref[to : to + rows, :] = grad_ref[pl.ds(src, rows), :]


def gru_kernel(*refs, stores, targets):
    pack_ref, rows_ref, turns_ref, gi_ref, gh_ref = refs[:5]
    states, out_ref = refs[5 : 5 + stores], refs[5 + stores]
    width = gh_ref.shape[0]
    hb = HEADS * targets
    latest = sum(state[hb:, LANES:] for state in states)
    elapsed = pack_ref[:, width + LANES : width + LANES + 1]
    encoded = cosine(elapsed * turns_ref[0:1, :] + turns_ref[1:2, :])
    inputs = jnp.concatenate([latest.astype(bf16), encoded.astype(bf16)], axis=1)
    mem_rows = pack_ref[:, :width]
    gi = dot(inputs, gi_ref[...], NN)
    gh = dot(mem_rows.astype(bf16), gh_ref[...], NN)
    update = jax.nn.sigmoid(gi[:, :width] + gh[:, :width])
    reset = jax.nn.sigmoid(gi[:, width : 2 * width] + gh[:, width : 2 * width])
    candidate = jnp.tanh(gi[:, 2 * width :] + reset * gh[:, 2 * width :])
    out_ref[:targets, :] = (1.0 - update) * candidate + update * mem_rows
    out_ref[targets:, :] = jnp.zeros((8, width), f32)
    out_ref[targets : targets + 1, :targets] = rows_ref[...].astype(f32)


def place_kernel(memory_ref, new_ref, out_ref, ids_ref, sids_ref, sem):
    targets = new_ref.shape[0] - 8
    ids_ref[...] = new_ref[targets:, :LANES].astype(jnp.int32)
    copy = pltpu.make_async_copy(ids_ref, sids_ref, sem)
    copy.start()
    out_ref[...] = memory_ref[...]
    copy.wait()
    for b in range(targets):
        out_ref[pl.ds(sids_ref[0, b], 1), :] = new_ref[b : b + 1, :]


def sum_split_kernel(*refs, count, outs):
    total = refs[0][...]
    for ref in refs[1:count]:
        total = total + ref[...].astype(f32)
    size = total.shape[0] // outs
    for i, ref in enumerate(refs[count:]):
        ref[...] = total[i * size : (i + 1) * size].astype(ref.dtype)


def last_sum_kernel(*refs):
    total = refs[0][...]
    for ref in refs[1:-1]:
        total = total + ref[...].astype(f32)
    out_ref = refs[-1]
    rows, width = total.shape
    per = width // LANES
    for j in range(per):
        out_ref[pl.ds(j, rows, stride=per), :] = total[:, j * LANES : (j + 1) * LANES]


def call(kernel, ins, outs, scratch=(), specs=None, name=None):
    return pl.pallas_call(
        kernel,
        in_specs=specs or [VM] * len(ins),
        out_specs=[VM] * len(outs),
        out_shape=outs,
        scratch_shapes=list(scratch),
        compiler_params=PARAMS,
        name=name,
    )(*ins)


def near(x):
    return pltpu.with_memory_space_constraint(x, pltpu.VMEM)


def far(x):
    return pltpu.with_memory_space_constraint(x, pltpu.HBM)


def shape(*dims, dtype=f32):
    return pltpu.VMEM(dims, dtype)


def out_shape(*dims, dtype=f32):
    return jax.ShapeDtypeStruct(dims, dtype)


def on_device(
    memory,
    event_feats,
    batch_rows,
    target_time,
    neighbor_owner,
    neighbor_event,
    neighbor_time,
    time_freq,
    time_phase,
    w_query,
    w_key,
    w_value,
    ln_gain,
    gru_input,
    gru_hidden,
    emb_cotangent,
):
    trainers, stores = lax.axis_size("trainer"), lax.axis_size("store")
    replicas = trainers * stores
    targets, neighbors = neighbor_event.shape[1:]
    held, feat = event_feats.shape
    width = memory.shape[1]
    kin = w_key.shape[0]
    hb = HEADS * targets
    los = 2
    his = trainers // (2 * los)
    sources = [
        batch_rows,
        memory,
        neighbor_owner[0, :, :, 0],
        neighbor_event[0],
        neighbor_time[0],
        target_time,
        emb_cotangent[0],
        time_freq[None],
        time_phase[None],
        w_query,
        w_key,
    ]
    pack, turns, wq_near, wk_near = call(
        functools.partial(pack_kernel, held=held),
        [far(x) for x in sources],
        [
            shape(targets, 2 * width + 2 * LANES),
            shape(8, LANES),
            shape(*w_query.shape, dtype=bf16),
            shape(*w_key.shape, dtype=bf16),
        ],
        scratch=[pltpu.SMEM(batch_rows.shape, jnp.int32)]
        + [pltpu.VMEM(x.shape, x.dtype) for x in sources[1:9]]
        + [pltpu.SemaphoreType.DMA((len(sources),))],
        specs=[FAR] * len(sources),
        name="pack",
    )

    def from_store(value, d):
        return lax.ppermute(value, "store", [((i + d) % stores, i) for i in range(stores)])

    packs = [pack] + [from_store(pack, d) for d in range(1, stores)]
    table = far(event_feats)
    chunks = 8
    pair_scratch = [
        pltpu.VMEM((GROUP * targets // 2, LANES), f32),
        pltpu.VMEM((GROUP * targets // 2, LANES), f32),
        pltpu.VMEM((6 * hb, LANES), f32),
        pltpu.VMEM((hb, kin), f32),
    ]
    local, weights, queries, inputs = [], [], [], []
    for d in range(stores):
        state, p, q, x = call(
            functools.partial(attend_kernel, neighbors=neighbors),
            [
                near(packs[d]),
                table,
                near(turns),
                near(wq_near),
                near(wk_near),
            ],
            [
                shape(hb + targets, kin),
                shape(hb, LANES),
                shape(targets, width),
                shape(targets * LANES, kin, dtype=bf16),
            ],
            scratch=[
                pltpu.VMEM((held, feat), bf16),
                pltpu.VMEM((held, feat), f32),
                pltpu.VMEM((targets, LANES), jnp.int32),
                pltpu.SMEM((targets, LANES), jnp.int32),
                pltpu.VMEM((TOGETHER * LANES, feat), f32),
                pltpu.VMEM((GROUP * targets // 2, kin), bf16),
                pltpu.VMEM((hb, LANES), f32),
                pltpu.VMEM((targets, LANES), f32),
                pltpu.VMEM((targets, LANES), f32),
                pltpu.VMEM((targets * LANES, LANES), f32),
                *pair_scratch,
                pltpu.SemaphoreType.DMA((chunks,)),
                pltpu.SemaphoreType.DMA,
            ],
            specs=[VM, FAR] + [VM] * 3,
            name="attend",
        )
        local.append(state)
        weights.append(p)
        queries.append(q)
        inputs.append(x)
    gathered = [local] + [[from_store(state, e) for state in local] for e in range(1, stores)]
    states = [[gathered[e][(d - e) % stores] for e in range(stores)] for d in range(stores)]

    def set_of(d):
        return [near(x) for x in (packs[d], queries[d], weights[d], inputs[d], *states[d])]

    gain = ln_gain[None]
    others = []
    for d in range(1, stores):
        ins = [gain, w_value, *set_of(d)]
        others += call(
            functools.partial(other_grad_kernel, stores=stores, replicas=replicas),
            ins,
            [
                shape(3 * targets, HEADS * kin, dtype=bf16),
                shape(3 * targets, width, dtype=bf16),
            ],
            scratch=[*pair_scratch, pltpu.VMEM((hb, LANES), f32)],
            name="other_grads",
        )
    ins = [gain, w_value, *set_of(0), *map(near, others)]
    emb, keep, send = call(
        functools.partial(own_grad_kernel, stores=stores, replicas=replicas, grid=(his, los)),
        ins,
        [out_shape(targets, width, dtype=bf16), shape(kin, width), shape(kin, width)],
        scratch=[pltpu.VMEM((2 * kin, width), f32), *pair_scratch, pltpu.VMEM((hb, LANES), f32)],
        name="own_grads",
    )

    (news,) = call(
        functools.partial(gru_kernel, stores=stores, targets=targets),
        [near(pack), batch_rows, near(turns), gru_input, gru_hidden, *map(near, states[0])],
        [shape(targets + 8, width)],
        name="gru",
    )

    def exchange(value, hr, lr, cr, sr):
        def other(i):
            t, s = i // stores, i % stores
            t = ((t // (2 * los)) ^ hr) * 2 * los + (((t // 2) % los) ^ lr) * 2 + ((t % 2) ^ cr)
            return t * stores + (s ^ sr)

        return lax.ppermute(value, AXES, [(i, other(i)) for i in range(replicas)])

    swapped = exchange(send, 0, 0, 1, 0)
    members = los * stores
    out = call(
        functools.partial(sum_split_kernel, count=2, outs=members),
        [near(keep), near(swapped)],
        [shape(kin // members, width)]
        + [shape(kin // members, width, dtype=bf16)] * (members - 1),
        name="core_sum",
    )
    got = [exchange(out[j], 0, j // stores, 0, j % stores) for j in reversed(range(1, members))]
    out = call(
        functools.partial(sum_split_kernel, count=members, outs=his),
        [*map(near, [out[0], *got])],
        [shape(kin // members // his, width)] * his,
        name="plane_sum",
    )
    got = [exchange(out[j], j, 0, 0, 0) for j in reversed(range(1, his))]
    (share,) = call(
        last_sum_kernel,
        [*map(near, [out[0], *got])],
        [out_shape(2 * kin * width // replicas // LANES, LANES)],
        name="last_sum",
    )
    moved = lax.ppermute(news, "trainer", [(i, (i + 1) % trainers) for i in range(trainers)])
    (memory_next,) = call(
        place_kernel,
        [memory, near(moved)],
        [out_shape(*memory.shape)],
        scratch=[
            pltpu.VMEM((8, LANES), jnp.int32),
            pltpu.SMEM((8, LANES), jnp.int32),
            pltpu.SemaphoreType.DMA,
        ],
        name="place",
    )
    return (emb[None], memory_next[None], share.reshape(-1))


def solution(mesh):
    placed = (
        P("store", None),
        P("store", None),
        P("trainer", "store"),
        P("trainer", "store"),
        P("trainer", "store", None, None),
        P("trainer", "store", None),
        P("trainer", "store", None),
        P(),
        P(),
        P(),
        P(),
        P(),
        P(),
        P(),
        P(),
        P("trainer", "store", None),
    )
    return jax.shard_map(
        on_device,
        mesh=mesh,
        in_specs=placed,
        out_specs=(
            P("trainer", "store", None),
            P("trainer", "store", None),
            P(("trainer", "store")),
        ),
        check_vma=False,
    )
```
